32 devices in a mesh: dp: 16 (over z, y, x), mp: 2 (over core).
Axes of the slice: x: 2, y: 2, z: 4, core: 2. Of those that a mesh axis runs over, the one named last changes fastest.
Arguments:
- tokens: bfloat16 [8192, 2048], P('dp'), may hold values from -6 to 6
- cotangent: bfloat16 [8192, 2048], P('dp'), may hold values from -6 to 6
- lengths: int32 [64], replicated, may hold values from 0 to 512, as said below
- seq_deal: int32 [64], replicated, may hold values from 0 to 63, as said below
- token_order: int32 [8192], replicated, may hold values from 0 to 8191, as said below
- gain_attn: float32 [2048], P('dp'), may hold values from 0.5 to 1.5
- w_query: float32 [2048, 2048], P('dp', 'mp'), may hold values from -0.125 to 0.125
- key_weight: float32 [2048, 1024], P('dp', 'mp'), may hold values from -0.125 to 0.125
- value_weight: float32 [2048, 1024], P('dp', 'mp'), may hold values from -0.125 to 0.125
- w_out: float32 [2048, 2048], P('mp', 'dp'), may hold values from -1 to 1
- gain_ffn: float32 [2048], P('dp'), may hold values from 0.5 to 1.5
- w_gate: float32 [2048, 8192], P('dp', 'mp'), may hold values from -0.125 to 0.125
- w_up: float32 [2048, 8192], P('dp', 'mp'), may hold values from -0.125 to 0.125
- w_down: float32 [8192, 2048], P('mp', 'dp'), may hold values from -0.0625 to 0.0625
- moment_gain_attn: float32 [2048], P('dp'), may hold values from -6 to 6
- moment_w_query: float32 [2048, 2048], P('dp', 'mp'), may hold values from -6 to 6
- key_weight_momentum: float32 [2048, 1024], P('dp', 'mp'), may hold values from -6 to 6
- value_weight_momentum: float32 [2048, 1024], P('dp', 'mp'), may hold values from -6 to 6
- moment_w_out: float32 [2048, 2048], P('mp', 'dp'), may hold values from -6 to 6
- moment_gain_ffn: float32 [2048], P('dp'), may hold values from -6 to 6
- moment_w_gate: float32 [2048, 8192], P('dp', 'mp'), may hold values from -6 to 6
- moment_w_up: float32 [2048, 8192], P('dp', 'mp'), may hold values from -6 to 6
- moment_w_down: float32 [8192, 2048], P('mp', 'dp'), may hold values from -6 to 6
Outputs:
- activations: bfloat16 [8192, 2048], P('dp')
- input_grad: bfloat16 [8192, 2048], P('dp')
- grad_norm: float32 [], replicated
- next_moment_gain_attn: float32 [2048], P('dp')
- next_moment_w_query: float32 [2048, 2048], P('dp', 'mp')
- next_moment_w_key: float32 [2048, 1024], P('dp', 'mp')
- next_moment_w_value: float32 [2048, 1024], P('dp', 'mp')
- next_moment_w_out: float32 [2048, 2048], P('mp', 'dp')
- next_moment_gain_ffn: float32 [2048], P('dp')
- next_moment_w_gate: float32 [2048, 8192], P('dp', 'mp')
- next_moment_w_up: float32 [2048, 8192], P('dp', 'mp')
- next_moment_w_down: float32 [8192, 2048], P('mp', 'dp')
- next_gain_attn: float32 [2048], P('dp')
- next_w_query: float32 [2048, 2048], P('dp', 'mp')
- next_w_key: float32 [2048, 1024], P('dp', 'mp')
- next_w_value: float32 [2048, 1024], P('dp', 'mp')
- next_w_out: float32 [2048, 2048], P('mp', 'dp')
- next_gain_ffn: float32 [2048], P('dp')
- next_w_gate: float32 [2048, 8192], P('dp', 'mp')
- next_w_up: float32 [2048, 8192], P('dp', 'mp')
- next_w_down: float32 [8192, 2048], P('mp', 'dp')
The draws below stay inside these ranges and needn't reach their ends.
Inputs may be any that keep to these rules, and one draw needn't show every extreme that they name: The 4 sequences of each aligned group of 4 dealt slots have lengths that sum to 512; some sequence has exactly 512 tokens; lengths of 0 occur. `seq_deal`: A permutation of the 64 sequence numbers. `token_order`: A permutation of the 8192 rows; the 512 dealt positions of each aligned block take exactly 32 rows from each aligned block of 512 rows of tokens.
All inputs are finite; a program needn't handle non-finite values.
Results may differ from the reference program's by a relative error of at most 0.014.
Values may be sent and summed in bfloat16 or wider, within the bound.
A program may use at most 320 MiB of HBM per device.

```python
import math
import jax
import jax.numpy as jnp
from jax import lax

MODEL_WIDTH = 2048
QUERY_HEADS = 8
KEY_VALUE_HEADS = 4
HEAD_SIZE = 256
FF = 8192
TOK_DEV = 512
SEQ_DEV = 4
NSEQ = 64
TOKENS = 8192
PARAMS = 62918656


def deal_tables(key):
    base = jax.random.fold_in(key, 1234)
    key_cuts, key_full, key_deal, key_rows, key_mix = jax.random.split(base, 5)
    groups = NSEQ // SEQ_DEV
    cuts = jnp.sort(jax.random.randint(key_cuts, (groups, SEQ_DEV - 1), 0, TOK_DEV + 1), axis=1)
    full_group = jax.random.randint(key_full, (), 0, groups)
    cuts = jnp.where(jnp.arange(groups)[:, None] == full_group, TOK_DEV, cuts).astype(jnp.int32)
    bounds = jnp.concatenate([jnp.zeros((groups, 1), jnp.int32), cuts, jnp.full((groups, 1), TOK_DEV, jnp.int32)], axis=1)
    group_len = bounds[:, 1:] - bounds[:, :-1]
    seq_deal = jax.random.permutation(key_deal, NSEQ).astype(jnp.int32)
    lengths = jnp.zeros((NSEQ,), jnp.int32).at[seq_deal].set(group_len.reshape(-1))
    blocks = TOKENS // TOK_DEV
    per_peer = TOK_DEV // blocks
    shuffled = jax.vmap(lambda part_key: jax.random.permutation(part_key, TOK_DEV))(jax.random.split(key_rows, blocks)).astype(jnp.int32)
    sources = shuffled + (jnp.arange(blocks, dtype=jnp.int32) * TOK_DEV)[:, None]
    taken = sources.reshape(blocks, blocks, per_peer).transpose(1, 0, 2).reshape(blocks, TOK_DEV)
    mixed = jax.vmap(jax.random.permutation)(jax.random.split(key_mix, blocks), taken)
    return (lengths, seq_deal, mixed.reshape(-1).astype(jnp.int32))


def draw_lengths(key, part):
    return deal_tables(key)[0]


def draw_seq_deal(key, part):
    return deal_tables(key)[1]


def draw_token_order(key, part):
    return deal_tables(key)[2]


def block_levels(rng, shape, shards, least, largest):
    def one(axis_at, shards_of):
        steps = jax.random.uniform(jax.random.fold_in(jax.random.fold_in(rng, 6), axis_at), (shards_of,), jnp.float32, least / len(shards), largest / len(shards))
        return jnp.repeat(jnp.exp(steps), shape[axis_at] // shards_of).reshape((-1,) + (1,) * (len(shape) - axis_at - 1))

    level = one(*shards[0])
    for cut in shards[1:]:
        level = level * one(*cut)
    return level


def centred(key, shape, spread, most, cuts=(), held_as=jnp.bfloat16):
    level = block_levels(key, shape, cuts, -0.22, 0.18) if cuts else 1.0
    drawn = jax.random.normal(key, shape, jnp.float32) * spread * level
    return jnp.minimum(jnp.maximum(drawn, -most), most).astype(held_as)


def setup_inputs(seed: int = 0) -> dict:
    seeds = jax.random.split(jax.random.key(seed), 24)
    tokens = centred(seeds[0], (TOKENS, MODEL_WIDTH), 1.0, 6.0, ((0, 16),))
    cotangent = centred(seeds[1], (TOKENS, MODEL_WIDTH), 1.0, 6.0, ((0, 16),))
    lengths = draw_lengths(jax.random.fold_in(seeds[23], 71), 0)
    seq_deal = draw_seq_deal(jax.random.fold_in(seeds[23], 71), 0)
    token_order = draw_token_order(jax.random.fold_in(seeds[23], 71), 0)
    gain_attn = jnp.clip(1.0 + 0.1 * jax.random.normal(seeds[5], (MODEL_WIDTH,), jnp.float32), 0.5, 1.5)
    w_query = centred(seeds[6], (MODEL_WIDTH, QUERY_HEADS * HEAD_SIZE), MODEL_WIDTH ** -0.5, 0.125, ((0, 16), (1, 2)), jnp.float32)
    key_weight = centred(seeds[7], (MODEL_WIDTH, KEY_VALUE_HEADS * HEAD_SIZE), MODEL_WIDTH ** -0.5, 0.125, ((0, 16), (1, 2)), jnp.float32)
    value_weight = centred(seeds[8], (MODEL_WIDTH, KEY_VALUE_HEADS * HEAD_SIZE), MODEL_WIDTH ** -0.5, 0.125, ((0, 16), (1, 2)), jnp.float32)
    w_out = centred(seeds[9], (QUERY_HEADS * HEAD_SIZE, MODEL_WIDTH), (QUERY_HEADS * HEAD_SIZE // 64) ** -0.5, 1.0, ((0, 2), (1, 16)), jnp.float32)
    gain_ffn = jnp.clip(1.0 + 0.1 * jax.random.normal(seeds[10], (MODEL_WIDTH,), jnp.float32), 0.5, 1.5)
    w_gate = centred(seeds[11], (MODEL_WIDTH, FF), MODEL_WIDTH ** -0.5, 0.125, ((0, 16), (1, 2)), jnp.float32)
    w_up = centred(seeds[12], (MODEL_WIDTH, FF), MODEL_WIDTH ** -0.5, 0.125, ((0, 16), (1, 2)), jnp.float32)
    w_down = centred(seeds[13], (FF, MODEL_WIDTH), FF ** -0.5, 0.0625, ((0, 2), (1, 16)), jnp.float32)
    moment_gain_attn = centred(seeds[14], (MODEL_WIDTH,), 1.0, 6.0, ((0, 16),), jnp.float32)
    moment_w_query = centred(seeds[15], (MODEL_WIDTH, QUERY_HEADS * HEAD_SIZE), 1.0, 6.0, ((0, 16), (1, 2)), jnp.float32)
    key_weight_momentum = centred(seeds[16], (MODEL_WIDTH, KEY_VALUE_HEADS * HEAD_SIZE), 1.0, 6.0, ((0, 16), (1, 2)), jnp.float32)
    value_weight_momentum = centred(seeds[17], (MODEL_WIDTH, KEY_VALUE_HEADS * HEAD_SIZE), 1.0, 6.0, ((0, 16), (1, 2)), jnp.float32)
    moment_w_out = centred(seeds[18], (QUERY_HEADS * HEAD_SIZE, MODEL_WIDTH), 1.0, 6.0, ((0, 2), (1, 16)), jnp.float32)
    moment_gain_ffn = centred(seeds[19], (MODEL_WIDTH,), 1.0, 6.0, ((0, 16),), jnp.float32)
    moment_w_gate = centred(seeds[20], (MODEL_WIDTH, FF), 1.0, 6.0, ((0, 16), (1, 2)), jnp.float32)
    moment_w_up = centred(seeds[21], (MODEL_WIDTH, FF), 1.0, 6.0, ((0, 16), (1, 2)), jnp.float32)
    moment_w_down = centred(seeds[22], (FF, MODEL_WIDTH), 1.0, 6.0, ((0, 2), (1, 16)), jnp.float32)
    return dict(tokens=tokens, cotangent=cotangent, lengths=lengths, seq_deal=seq_deal, token_order=token_order, gain_attn=gain_attn, w_query=w_query, key_weight=key_weight, value_weight=value_weight, w_out=w_out, gain_ffn=gain_ffn, w_gate=w_gate, w_up=w_up, w_down=w_down, moment_gain_attn=moment_gain_attn, moment_w_query=moment_w_query, key_weight_momentum=key_weight_momentum, value_weight_momentum=value_weight_momentum, moment_w_out=moment_w_out, moment_gain_ffn=moment_gain_ffn, moment_w_gate=moment_w_gate, moment_w_up=moment_w_up, moment_w_down=moment_w_down)


EPS = 1e-06
THETA = 1000042.0
LEARN = 0.5
DECAY = 0.1
HIGH_ACCURACY = lax.Precision.HIGHEST

@jax.custom_vjp
def reduced_precision(v):
    return lax.optimization_barrier(v.astype(jnp.bfloat16)).astype(jnp.float32)

@jax.custom_vjp
def reduced_precision_backward(v):
    return v

def low_keep(v):
    return (reduced_precision(v), None)

def low_pass(kept, grad):
    return (grad,)

def back_keep(v):
    return (v, None)

def back_low(kept, grad):
    return (reduced_precision(grad),)
reduced_precision.defvjp(low_keep, low_pass)
reduced_precision_backward.defvjp(back_keep, back_low)

def angles(position, head):
    half = head // 2
    freq = THETA ** (-(2.0 * jnp.arange(half, dtype=jnp.float32)) / head)
    turned = position[:, None] * freq[None, :]
    return (jnp.cos(turned)[:, None, :], jnp.sin(turned)[:, None, :])

def apply_rotary(value_matrix, cosine_table, sine_table):
    half = value_matrix.shape[-1] // 2
    first = value_matrix[..., :half]
    second = value_matrix[..., half:]
    return jnp.concatenate([first * cosine_table - second * sine_table, second * cosine_table + first * sine_table], axis=-1)

def layout(block_len, row_count_local):
    ends = jnp.cumsum(block_len)
    starts = ends - block_len
    index = jnp.arange(row_count_local, dtype=jnp.int32)
    inside = (index[:, None] >= starts[None, :]) & (index[:, None] < ends[None, :])
    slots = jnp.arange(block_len.shape[0], dtype=jnp.int32)
    segment = lax.optimization_barrier(jnp.sum(jnp.where(inside, slots[None, :], 0), axis=1))
    position = lax.optimization_barrier(jnp.sum(jnp.where(inside, index[:, None] - starts[None, :], 0), axis=1))
    mask = (segment[:, None] == segment[None, :]) & (index[None, :] <= index[:, None])
    return (position.astype(jnp.float32), mask)

def layer(inputs, gain_attn, w_query, key_weight, value_weight, w_out, gain_ffn, w_gate, w_up, w_down, cosine_table, sine_table, mask):
    row_count_local = inputs.shape[0]
    head_group = QUERY_HEADS // KEY_VALUE_HEADS
    hidden_after_attention = reduced_precision(inputs * lax.rsqrt(lax.optimization_barrier(jnp.mean(inputs * inputs, axis=-1, keepdims=True)) + EPS) * gain_attn)
    query_matrix = reduced_precision_backward(jnp.dot(hidden_after_attention, w_query, precision=HIGH_ACCURACY)).reshape(row_count_local, QUERY_HEADS, HEAD_SIZE)
    key_matrix = reduced_precision_backward(jnp.dot(hidden_after_attention, key_weight, precision=HIGH_ACCURACY)).reshape(row_count_local, KEY_VALUE_HEADS, HEAD_SIZE)
    value_matrix = reduced_precision(reduced_precision_backward(jnp.dot(hidden_after_attention, value_weight, precision=HIGH_ACCURACY))).reshape(row_count_local, KEY_VALUE_HEADS, HEAD_SIZE)
    query_rotated = reduced_precision(apply_rotary(query_matrix, cosine_table, sine_table)).reshape(row_count_local, KEY_VALUE_HEADS, head_group, HEAD_SIZE)
    key_rot = reduced_precision(apply_rotary(key_matrix, cosine_table, sine_table))
    scores = reduced_precision_backward(jnp.einsum('rhgd,chd->hgrc', query_rotated, key_rot, precision=HIGH_ACCURACY) * HEAD_SIZE ** (-0.5))
    scores = jnp.where(mask[None, None], scores, -1e+30)
    top = lax.optimization_barrier(jnp.max(scores, axis=-1, keepdims=True))
    expo = jnp.exp(scores - top)
    prob = reduced_precision(expo / lax.optimization_barrier(jnp.sum(expo, axis=-1, keepdims=True)))
    mixed = reduced_precision(reduced_precision_backward(jnp.einsum('hgrc,chd->rhgd', prob, value_matrix, precision=HIGH_ACCURACY))).reshape(row_count_local, QUERY_HEADS * HEAD_SIZE)
    middle = inputs + reduced_precision_backward(jnp.dot(mixed, w_out, precision=HIGH_ACCURACY))
    hidden2 = reduced_precision(middle * lax.rsqrt(lax.optimization_barrier(jnp.mean(middle * middle, axis=-1, keepdims=True)) + EPS) * gain_ffn)
    gate = reduced_precision_backward(jnp.dot(hidden2, w_gate, precision=HIGH_ACCURACY))
    upper = reduced_precision_backward(jnp.dot(hidden2, w_up, precision=HIGH_ACCURACY))
    inner = reduced_precision(jax.nn.silu(gate) * upper)
    return middle + reduced_precision_backward(jnp.dot(inner, w_down, precision=HIGH_ACCURACY))

def reference(tokens, cotangent, lengths, seq_deal, token_order, gain_attn, w_query, key_weight, value_weight, w_out, gain_ffn, w_gate, w_up, w_down, moment_gain_attn, moment_w_query, key_weight_momentum, value_weight_momentum, moment_w_out, moment_gain_ffn, moment_w_gate, moment_w_up, moment_w_down):
    weights = (gain_attn, w_query, key_weight, value_weight, w_out, gain_ffn, w_gate, w_up, w_down)
    moments = (moment_gain_attn, moment_w_query, key_weight_momentum, value_weight_momentum, moment_w_out, moment_gain_ffn, moment_w_gate, moment_w_up, moment_w_down)
    rounded = tuple((w.astype(jnp.bfloat16).astype(jnp.float32) for w in weights))
    blocks = TOKENS // TOK_DEV
    dealt = tokens[token_order].astype(jnp.float32).reshape(blocks, TOK_DEV, MODEL_WIDTH)
    dealt_cot = cotangent[token_order].astype(jnp.float32).reshape(blocks, TOK_DEV, MODEL_WIDTH)
    block_lens = lengths[seq_deal].reshape(blocks, SEQ_DEV)

    def one_block(totals, items):
        inputs, grad_out, block_len = items
        position, mask = layout(block_len, TOK_DEV)
        cosine_table, sine_table = angles(position, HEAD_SIZE)

        def run(inputs, *ws):
            return layer(inputs, *ws, cosine_table, sine_table, mask)
        output, pull = jax.vjp(run, inputs, *rounded)
        grads = pull(grad_out)
        totals = tuple((t + g for t, g in zip(totals, grads[1:])))
        return (totals, (output, grads[0]))
    zeros = tuple((jnp.zeros_like(w) for w in rounded))
    totals, (outputs, in_grads) = lax.scan(one_block, zeros, (dealt, dealt_cot, block_lens))
    inverse = jnp.argsort(token_order)
    activations = outputs.reshape(TOKENS, MODEL_WIDTH)[inverse].astype(jnp.bfloat16)
    input_grad = in_grads.reshape(TOKENS, MODEL_WIDTH)[inverse].astype(jnp.bfloat16)
    squares = jnp.float32(0.0)
    for grad in totals:
        squares = squares + jnp.sum(grad * grad)
    grad_norm = jnp.sqrt(squares)
    factor = jnp.minimum(1.0, math.sqrt(PARAMS) / grad_norm)
    new_moments = tuple((0.5 * m + 0.5 * factor * g for m, g in zip(moments, totals)))
    new_weights = tuple((w - LEARN * (m + DECAY * w) for w, m in zip(weights, new_moments)))
    return (activations, input_grad, grad_norm, new_moments[0], new_moments[1], new_moments[2], new_moments[3], new_moments[4], new_moments[5], new_moments[6], new_moments[7], new_moments[8], new_weights[0], new_weights[1], new_weights[2], new_weights[3], new_weights[4], new_weights[5], new_weights[6], new_weights[7], new_weights[8])
```

```python
import math

import jax
import jax.numpy as jnp
from jax import lax
from jax.sharding import PartitionSpec as P

HEAD_SIZE = 256
PARAMS = 62918656


EPS = 1e-06
THETA = 1000042.0
LEARN = 0.5
DECAY = 0.1


def angles(position, head):
    half = head // 2
    freq = THETA ** (-(2.0 * jnp.arange(half, dtype=jnp.float32)) / head)
    turned = position[:, None] * freq[None, :]
    return (jnp.cos(turned)[:, None, :], jnp.sin(turned)[:, None, :])


def apply_rotary(value_matrix, cosine_table, sine_table):
    half = value_matrix.shape[-1] // 2
    first = value_matrix[..., :half]
    second = value_matrix[..., half:]
    return jnp.concatenate(
        [first * cosine_table - second * sine_table, second * cosine_table + first * sine_table],
        axis=-1,
    )


def unrotate(grads, cosine_table, sine_table):
    half = grads.shape[-1] // 2
    first = grads[..., :half]
    second = grads[..., half:]
    return jnp.concatenate(
        [first * cosine_table + second * sine_table, second * cosine_table - first * sine_table],
        axis=-1,
    )


def layout(block_len, row_count_local):
    rank = jnp.arange(block_len.shape[0], dtype=jnp.int32)
    ends = jnp.sum(jnp.where(rank[None, :] <= rank[:, None], block_len[None, :], 0), axis=1)
    starts = ends - block_len
    index = jnp.arange(row_count_local, dtype=jnp.int32)
    inside = (index[:, None] >= starts[None, :]) & (index[:, None] < ends[None, :])
    slots = jnp.arange(block_len.shape[0], dtype=jnp.int32)
    segment = jnp.sum(jnp.where(inside, slots[None, :], 0), axis=1)
    position = jnp.sum(jnp.where(inside, index[:, None] - starts[None, :], 0), axis=1)
    mask = (segment[:, None] == segment[None, :]) & (index[None, :] <= index[:, None])
    return (position.astype(jnp.float32), mask)


def normalize(value_matrix):
    scale_inv = lax.rsqrt(jnp.mean(value_matrix * value_matrix, axis=-1, keepdims=True) + EPS)
    return (value_matrix * scale_inv, scale_inv)


def norm_back(grad_normed, normed, scale_inv, gain):
    scaled = grad_normed * gain
    return scale_inv * (scaled - normed * jnp.mean(scaled * normed, axis=-1, keepdims=True))


def mat_nt(left, right):
    return lax.dot_general(
        left, right, (((1,), (1,)), ((), ())), preferred_element_type=jnp.float32
    )


def mat_tn(left, right):
    return lax.dot_general(
        left, right, (((0,), (0,)), ((), ())), preferred_element_type=jnp.float32
    )


def head_sum(partial_value):
    return lax.psum(partial_value, "mp")


def fetch_attn(gain_attn, w_query, key_weight, value_weight, w_out):
    return (
        lax.all_gather(gain_attn.astype(jnp.bfloat16), "dp", axis=0, tiled=True),
        lax.all_gather(w_query.astype(jnp.bfloat16), "dp", axis=0, tiled=True),
        lax.all_gather(key_weight.astype(jnp.bfloat16), "dp", axis=0, tiled=True),
        lax.all_gather(value_weight.astype(jnp.bfloat16), "dp", axis=0, tiled=True),
        lax.all_gather(w_out.astype(jnp.bfloat16), "dp", axis=1, tiled=True),
    )


def fetch_ffn(gain_ffn, w_gate, w_up, w_down):
    return (
        lax.all_gather(gain_ffn.astype(jnp.bfloat16), "dp", axis=0, tiled=True),
        lax.all_gather(w_gate.astype(jnp.bfloat16), "dp", axis=0, tiled=True),
        lax.all_gather(w_up.astype(jnp.bfloat16), "dp", axis=0, tiled=True),
        lax.all_gather(w_down.astype(jnp.bfloat16), "dp", axis=1, tiled=True),
    )


def attn_scores(query_rotated, key_rot, mask):
    scores = jnp.einsum(
        "rhgd,chd->hgrc", query_rotated, key_rot, preferred_element_type=jnp.float32
    ) * HEAD_SIZE ** (-0.5)
    return jnp.where(mask[None, None], scores, -1e30)


def on_device(
    tokens,
    cotangent,
    lengths,
    seq_deal,
    token_order,
    gain_attn,
    w_query,
    key_weight,
    value_weight,
    w_out,
    gain_ffn,
    w_gate,
    w_up,
    w_down,
    moment_gain_attn,
    moment_w_query,
    key_weight_momentum,
    value_weight_momentum,
    moment_w_out,
    moment_gain_ffn,
    moment_w_gate,
    moment_w_up,
    moment_w_down,
):
    row_count_local = tokens.shape[0]
    total_rows = token_order.shape[0]
    device = lax.axis_index("dp")
    place = (
        jnp.zeros((total_rows,), jnp.int32)
        .at[token_order]
        .set(jnp.arange(total_rows, dtype=jnp.int32))
    )
    own_place = lax.dynamic_slice_in_dim(place, device * row_count_local, row_count_local)
    send_order = jnp.argsort(own_place)
    wanted = lax.dynamic_slice_in_dim(token_order, device * row_count_local, row_count_local)
    arrival = jnp.argsort(
        wanted // row_count_local * row_count_local + jnp.arange(row_count_local, dtype=jnp.int32)
    )
    arrival_rank = jnp.argsort(arrival)
    got_tokens, got_cot = (
        lax.all_to_all(tokens[send_order], "dp", split_axis=0, concat_axis=0, tiled=True),
        lax.all_to_all(cotangent[send_order], "dp", split_axis=0, concat_axis=0, tiled=True),
    )
    dealt = got_tokens[arrival_rank]
    dealt_cot = got_cot[arrival_rank]
    seq_dev = seq_deal.shape[0] // lax.axis_size("dp")
    mine = lax.dynamic_slice_in_dim(seq_deal, device * seq_dev, seq_dev)
    block_len = lengths[mine]
    position, mask = layout(block_len, row_count_local)
    cosine_table, sine_table = angles(position, HEAD_SIZE)
    gain_a, query_w, key_w, value_w, out_w = fetch_attn(
        gain_attn, w_query, key_weight, value_weight, w_out
    )
    gain_f, gate_w, up_w, down_w = fetch_ffn(gain_ffn, w_gate, w_up, w_down)
    heads_q = query_w.shape[1] // HEAD_SIZE
    heads_kv = key_w.shape[1] // HEAD_SIZE
    head_group = heads_q // heads_kv
    inputs = dealt.astype(jnp.float32)
    normed1, scale1 = normalize(inputs)
    hidden_after_attention = (normed1 * gain_a).astype(jnp.bfloat16)
    query_matrix = jnp.dot(
        hidden_after_attention, query_w, preferred_element_type=jnp.float32
    ).reshape(row_count_local, heads_q, HEAD_SIZE)
    key_matrix = jnp.dot(hidden_after_attention, key_w, preferred_element_type=jnp.float32).reshape(
        row_count_local, heads_kv, HEAD_SIZE
    )
    value_matrix = (
        jnp.dot(hidden_after_attention, value_w, preferred_element_type=jnp.float32)
        .astype(jnp.bfloat16)
        .reshape(row_count_local, heads_kv, HEAD_SIZE)
    )
    query_rotated = (
        apply_rotary(query_matrix, cosine_table, sine_table)
        .astype(jnp.bfloat16)
        .reshape(row_count_local, heads_kv, head_group, HEAD_SIZE)
    )
    key_rot = apply_rotary(key_matrix, cosine_table, sine_table).astype(jnp.bfloat16)
    scores = attn_scores(query_rotated, key_rot, mask)
    top = jnp.max(scores, axis=-1, keepdims=True)
    expo = jnp.exp(scores - top)
    total = jnp.sum(expo, axis=-1, keepdims=True)
    lse = top + jnp.log(total)
    prob_low = (expo / total).astype(jnp.bfloat16)
    mixed_low = (
        jnp.einsum("hgrc,chd->rhgd", prob_low, value_matrix, preferred_element_type=jnp.float32)
        .reshape(row_count_local, heads_q * HEAD_SIZE)
        .astype(jnp.bfloat16)
    )
    middle = inputs + head_sum(jnp.dot(mixed_low, out_w, preferred_element_type=jnp.float32))
    normed2, scale2 = normalize(middle)
    hidden2 = (normed2 * gain_f).astype(jnp.bfloat16)
    gate = jnp.dot(hidden2, gate_w, preferred_element_type=jnp.float32)
    upper = jnp.dot(hidden2, up_w, preferred_element_type=jnp.float32)
    activ = jax.nn.silu(gate)
    inner = (activ * upper).astype(jnp.bfloat16)
    result = middle + head_sum(jnp.dot(inner, down_w, preferred_element_type=jnp.float32))
    grad_out = dealt_cot.astype(jnp.float32)
    grad_inner = mat_nt(dealt_cot, down_w)
    grad_wd = mat_tn(inner, dealt_cot)
    sigma = jax.nn.sigmoid(gate)
    grad_gate = (grad_inner * upper * (sigma * (1.0 + gate * (1.0 - sigma)))).astype(jnp.bfloat16)
    grad_up = (grad_inner * activ).astype(jnp.bfloat16)
    grad_wg = mat_tn(hidden2, grad_gate)
    grad_wu = mat_tn(hidden2, grad_up)
    grad_h2 = head_sum(mat_nt(grad_gate, gate_w) + mat_nt(grad_up, up_w))
    grad_gf = jnp.sum(grad_h2 * normed2, axis=0)
    grad_mid = grad_out + norm_back(grad_h2, normed2, scale2, gain_f)
    owned_ffn = (grad_gf, grad_wg, grad_wu, grad_wd)
    mid_low = grad_mid.astype(jnp.bfloat16)
    grad_wo = mat_tn(mixed_low, mid_low)
    grad_mixed = (
        mat_nt(mid_low, out_w)
        .astype(jnp.bfloat16)
        .reshape(row_count_local, heads_kv, head_group, HEAD_SIZE)
    )
    prob = jnp.exp(attn_scores(query_rotated, key_rot, mask) - lse)
    prob_back = prob.astype(jnp.bfloat16)
    grad_prob = jnp.einsum(
        "rhgd,chd->hgrc", grad_mixed, value_matrix, preferred_element_type=jnp.float32
    )
    delta = jnp.sum(prob * grad_prob, axis=-1, keepdims=True)
    grad_scores = (prob * (grad_prob - delta)).astype(jnp.bfloat16)
    grad_qrot = jnp.einsum(
        "hgrc,chd->rhgd", grad_scores, key_rot, preferred_element_type=jnp.float32
    ) * HEAD_SIZE ** (-0.5)
    grad_krot = jnp.einsum(
        "hgrc,rhgd->chd", grad_scores, query_rotated, preferred_element_type=jnp.float32
    ) * HEAD_SIZE ** (-0.5)
    grad_values = jnp.einsum(
        "hgrc,rhgd->chd", prob_back, grad_mixed, preferred_element_type=jnp.float32
    )
    grad_query = (
        unrotate(grad_qrot.reshape(row_count_local, heads_q, HEAD_SIZE), cosine_table, sine_table)
        .reshape(row_count_local, heads_q * HEAD_SIZE)
        .astype(jnp.bfloat16)
    )
    grad_keys = (
        unrotate(grad_krot, cosine_table, sine_table)
        .reshape(row_count_local, heads_kv * HEAD_SIZE)
        .astype(jnp.bfloat16)
    )
    grad_vlow = grad_values.reshape(row_count_local, heads_kv * HEAD_SIZE).astype(jnp.bfloat16)
    grad_h1 = head_sum(
        mat_nt(grad_query, query_w) + mat_nt(grad_keys, key_w) + mat_nt(grad_vlow, value_w)
    )
    grad_wq = mat_tn(hidden_after_attention, grad_query)
    grad_wk = mat_tn(hidden_after_attention, grad_keys)
    grad_wv = mat_tn(hidden_after_attention, grad_vlow)
    grad_ga = jnp.sum(grad_h1 * normed1, axis=0)
    grad_in = grad_mid + norm_back(grad_h1, normed1, scale1, gain_a)
    owned = (
        lax.psum_scatter(grad_ga, "dp", scatter_dimension=0, tiled=True),
        lax.psum_scatter(grad_wq, "dp", scatter_dimension=0, tiled=True),
        lax.psum_scatter(grad_wk, "dp", scatter_dimension=0, tiled=True),
        lax.psum_scatter(grad_wv, "dp", scatter_dimension=0, tiled=True),
        lax.psum_scatter(grad_wo, "dp", scatter_dimension=1, tiled=True),
        lax.psum_scatter(owned_ffn[0], "dp", scatter_dimension=0, tiled=True),
        lax.psum_scatter(owned_ffn[1], "dp", scatter_dimension=0, tiled=True),
        lax.psum_scatter(owned_ffn[2], "dp", scatter_dimension=0, tiled=True),
        lax.psum_scatter(owned_ffn[3], "dp", scatter_dimension=1, tiled=True),
    )
    back_out, back_grad = (
        lax.all_to_all(
            result.astype(jnp.bfloat16)[arrival], "dp", split_axis=0, concat_axis=0, tiled=True
        ),
        lax.all_to_all(
            grad_in.astype(jnp.bfloat16)[arrival], "dp", split_axis=0, concat_axis=0, tiled=True
        ),
    )
    send_rank = jnp.argsort(send_order)
    activations = back_out[send_rank]
    input_grad = back_grad[send_rank]
    share = 0.5 * (jnp.sum(owned[0] * owned[0]) + jnp.sum(owned[5] * owned[5]))
    for position_index in (1, 2, 3, 4, 6, 7, 8):
        share = share + jnp.sum(owned[position_index] * owned[position_index])
    grad_norm = jnp.sqrt(lax.psum(share, ("dp", "mp")))
    factor = jnp.minimum(1.0, math.sqrt(PARAMS) / grad_norm)
    weights = (gain_attn, w_query, key_weight, value_weight, w_out, gain_ffn, w_gate, w_up, w_down)
    moments = (
        moment_gain_attn,
        moment_w_query,
        key_weight_momentum,
        value_weight_momentum,
        moment_w_out,
        moment_gain_ffn,
        moment_w_gate,
        moment_w_up,
        moment_w_down,
    )
    new_moments = tuple(
        (0.5 * m_old + 0.5 * factor * g_new for m_old, g_new in zip(moments, owned))
    )
    new_weights = tuple(
        (w_old - LEARN * (m_new + DECAY * w_old) for w_old, m_new in zip(weights, new_moments))
    )
    return (
        activations,
        input_grad,
        grad_norm,
        new_moments[0],
        new_moments[1],
        new_moments[2],
        new_moments[3],
        new_moments[4],
        new_moments[5],
        new_moments[6],
        new_moments[7],
        new_moments[8],
        new_weights[0],
        new_weights[1],
        new_weights[2],
        new_weights[3],
        new_weights[4],
        new_weights[5],
        new_weights[6],
        new_weights[7],
        new_weights[8],
    )


def solution(mesh):
    in_specs = (
        P("dp", None),
        P("dp", None),
        P(),
        P(),
        P(),
        P("dp"),
        P("dp", "mp"),
        P("dp", "mp"),
        P("dp", "mp"),
        P("mp", "dp"),
        P("dp"),
        P("dp", "mp"),
        P("dp", "mp"),
        P("mp", "dp"),
        P("dp"),
        P("dp", "mp"),
        P("dp", "mp"),
        P("dp", "mp"),
        P("mp", "dp"),
        P("dp"),
        P("dp", "mp"),
        P("dp", "mp"),
        P("mp", "dp"),
    )
    out_specs = (
        P("dp", None),
        P("dp", None),
        P(),
        P("dp"),
        P("dp", "mp"),
        P("dp", "mp"),
        P("dp", "mp"),
        P("mp", "dp"),
        P("dp"),
        P("dp", "mp"),
        P("dp", "mp"),
        P("mp", "dp"),
        P("dp"),
        P("dp", "mp"),
        P("dp", "mp"),
        P("dp", "mp"),
        P("mp", "dp"),
        P("dp"),
        P("dp", "mp"),
        P("dp", "mp"),
        P("mp", "dp"),
    )
    return jax.shard_map(
        on_device, mesh=mesh, in_specs=in_specs, out_specs=out_specs, check_vma=False
    )
```

```python
import math

import jax
import jax.numpy as jnp
from jax import lax
from jax.sharding import Mesh
from jax.sharding import PartitionSpec as P

HEAD_SIZE = 256
PARAMS = 62918656
EPS = 1e-06
THETA = 1000042.0
LEARN = 0.5
DECAY = 0.1
GROUP = 4
BF = jnp.bfloat16
F32 = jnp.float32


def angles(position, head):
    half = head // 2
    freq = THETA ** (-(2.0 * jnp.arange(half, dtype=F32)) / head)
    turned = position[:, None] * freq[None, :]
    return (jnp.cos(turned)[:, None, :], jnp.sin(turned)[:, None, :])


def apply_rotary(value, cosine, sine):
    half = value.shape[-1] // 2
    first, second = value[..., :half], value[..., half:]
    return jnp.concatenate(
        [first * cosine - second * sine, second * cosine + first * sine], axis=-1
    )


def unrotate(grads, cosine, sine):
    half = grads.shape[-1] // 2
    first, second = grads[..., :half], grads[..., half:]
    return jnp.concatenate(
        [first * cosine + second * sine, second * cosine - first * sine], axis=-1
    )


def layout(block_len, rows):
    rank = jnp.arange(block_len.shape[0], dtype=jnp.int32)
    ends = jnp.sum(jnp.where(rank[None, :] <= rank[:, None], block_len[None, :], 0), axis=1)
    starts = ends - block_len
    index = jnp.arange(rows, dtype=jnp.int32)
    inside = (index[:, None] >= starts[None, :]) & (index[:, None] < ends[None, :])
    segment = jnp.sum(jnp.where(inside, rank[None, :], 0), axis=1)
    position = jnp.sum(jnp.where(inside, index[:, None] - starts[None, :], 0), axis=1)
    mask = (segment[:, None] == segment[None, :]) & (index[None, :] <= index[:, None])
    return (position.astype(F32), mask)


def normalize(value):
    scale_inv = lax.rsqrt(jnp.mean(value * value, axis=-1, keepdims=True) + EPS)
    return (value * scale_inv, scale_inv)


def norm_back(grad_normed, normed, scale_inv, gain):
    scaled = grad_normed * gain
    return scale_inv * (scaled - normed * jnp.mean(scaled * normed, axis=-1, keepdims=True))


def mat_nn(left, right):
    return jnp.dot(left, right, preferred_element_type=F32)


def mat_nt(left, right):
    return lax.dot_general(left, right, (((1,), (1,)), ((), ())), preferred_element_type=F32)


def mat_tn(left, right):
    return lax.dot_general(left, right, (((0,), (0,)), ((), ())), preferred_element_type=F32)


def after(value, *others):
    return lax.optimization_barrier((value, *others))[0]


class Ways:
    def __init__(self):
        self.depth = lax.axis_size("line")
        self.n = self.depth * GROUP
        self.z = lax.axis_index("line")
        self.p = lax.axis_index("group")
        self.me = self.z * GROUP + self.p
        self.core = lax.axis_index("mp")

    def flip(self, value, k):
        return lax.ppermute(value, "group", [(i, i ^ k) for i in range(GROUP)])

    def swap(self, value):
        return lax.ppermute(value, "mp", [(0, 1), (1, 0)])

    def gather_line(self, value):
        return lax.all_gather(value, "line", axis=0, tiled=True)

    def scatter_line(self, whole):
        return lax.psum_scatter(
            whole.astype(BF), "line", scatter_dimension=0, tiled=True
        ).astype(F32)

    def gather_group(self, value):
        half = value.shape[0] // 2
        one, two = self.flip(value, 1), self.flip(value, 2)
        three = jnp.concatenate([self.flip(one[:half], 2), self.flip(two[half:], 1)])
        return [value, one, two, three]

    def scatter_group(self, parts):
        half = parts[0].shape[0] // 2
        first = self.flip(parts[3][:half].astype(BF), 2).astype(F32)
        second = self.flip(parts[3][half:].astype(BF), 1).astype(F32)
        one = jnp.concatenate([parts[1][:half] + first, parts[1][half:]]).astype(BF)
        two = jnp.concatenate([parts[2][:half], parts[2][half:] + second]).astype(BF)
        return parts[0] + self.flip(one, 1).astype(F32) + self.flip(two, 2).astype(F32)

    def spread_units(self, shards):
        rows, units = shards[0].shape[0], shards[0].shape[1] // GROUP
        send = jnp.stack(
            [
                jnp.concatenate([s[:, j * units : (j + 1) * units] for s in shards])
                for j in range(GROUP)
            ]
        )
        got = lax.all_to_all(send, "group", split_axis=0, concat_axis=0, tiled=True)
        return got.reshape(GROUP, len(shards), rows, units).swapaxes(0, 1).reshape(
            len(shards), GROUP * rows, units
        )

    def collect_units(self, whole):
        rows = whole.shape[0] // GROUP
        got = lax.all_to_all(
            whole.astype(BF), "group", split_axis=0, concat_axis=0, tiled=True
        ).astype(F32)
        return jnp.concatenate([got[j * rows : (j + 1) * rows] for j in range(GROUP)], axis=1)

    def exchange(self, value):
        return lax.all_to_all(value, ("line", "group"), split_axis=0, concat_axis=0, tiled=True)

    def own_half(self, value):
        half = value.shape[-1] // 2
        return jnp.where(self.core == 0, value[..., :half], value[..., half:])

    def other_half(self, value):
        half = value.shape[-1] // 2
        return jnp.where(self.core == 0, value[..., half:], value[..., :half])

    def join(self, mine, other):
        return jnp.where(
            self.core == 0,
            jnp.concatenate([mine, other], axis=-1),
            jnp.concatenate([other, mine], axis=-1),
        )


def deal_tables(token_order, me, rows):
    blocks = token_order.shape[0] // rows
    per = rows // blocks
    index = jnp.arange(rows, dtype=jnp.int32)
    wanted = lax.dynamic_slice_in_dim(token_order, me * rows, rows)
    source = wanted // rows
    same = (source[:, None] == source[None, :]) & (index[None, :] < index[:, None])
    slot = source * per + jnp.sum(same.astype(jnp.int32), axis=1)
    into = (slot[:, None] == index[None, :]).astype(BF)
    table = token_order.reshape(blocks, rows)
    taken = table // rows == me
    earlier = (index[:, None] < index[None, :]).astype(BF)
    rank = mat_nn(taken.astype(BF), earlier).astype(jnp.int32)
    hit = taken[:, None, :] & (rank[:, None, :] == jnp.arange(per, dtype=jnp.int32)[None, :, None])
    sent = jnp.sum(jnp.where(hit, (table - me * rows)[:, None, :], 0), axis=2).reshape(rows)
    out = (sent[:, None] == index[None, :]).astype(BF)
    return into, out


def on_device(
    tokens,
    cotangent,
    lengths,
    seq_deal,
    token_order,
    gain_attn,
    w_query,
    key_weight,
    value_weight,
    w_out,
    gain_ffn,
    w_gate,
    w_up,
    w_down,
    moment_gain_attn,
    moment_w_query,
    key_weight_momentum,
    value_weight_momentum,
    moment_w_out,
    moment_gain_ffn,
    moment_w_gate,
    moment_w_up,
    moment_w_down,
):
    ways = Ways()
    rows, width = tokens.shape
    me = ways.me
    shard_qkv = jnp.concatenate(
        [w_query.astype(BF), key_weight.astype(BF), value_weight.astype(BF)], axis=1
    )
    shard_out = w_out.astype(BF).T
    line_all = ways.gather_line(jnp.concatenate([shard_qkv, shard_out], axis=1))
    line_qkv = line_all[:, : shard_qkv.shape[1]]
    line_out = line_all[:, shard_qkv.shape[1] :]

    def natural(line):
        count, cols = ways.depth, line.shape[1]
        each = line.shape[0] // count
        whole = jnp.zeros((count, GROUP, each, cols), line.dtype)
        for k, part in enumerate(ways.gather_group(line)):
            whole = lax.dynamic_update_slice(
                whole, part.reshape(count, 1, each, cols), (0, ways.p ^ k, 0, 0)
            )
        return whole.reshape(count * GROUP * each, cols)

    into, out = deal_tables(token_order, me, rows)
    sent_tokens = mat_nn(out, ways.own_half(tokens)).astype(BF)
    sent_cot = mat_nn(out, ways.own_half(cotangent)).astype(BF)
    gains = jnp.stack([gain_attn, gain_ffn]).astype(BF)
    all_gains = ways.exchange(
        jnp.broadcast_to(gains[None], (ways.n, 2, gains.shape[1]))
    ).astype(F32)
    gain_a = all_gains[:, 0].reshape(width)
    gain_f = all_gains[:, 1].reshape(width)
    half_tokens = mat_nn(into, ways.exchange(sent_tokens)).astype(BF)
    dealt = ways.join(half_tokens, ways.swap(half_tokens))
    weight_qkv = natural(line_qkv)
    weight_out = natural(after(line_out, weight_qkv))
    half_cot = mat_nn(into, ways.exchange(after(sent_cot, weight_qkv))).astype(BF)
    wide_q = w_query.shape[1]
    wide_k = key_weight.shape[1]
    query_w = weight_qkv[:, :wide_q]
    key_w = weight_qkv[:, wide_q : wide_q + wide_k]
    value_w = weight_qkv[:, wide_q + wide_k :]

    units = ways.spread_units([w_down.astype(BF).T, w_gate.astype(BF), w_up.astype(BF)])
    line_units = lax.all_gather(units, "line", axis=1, tiled=False)
    down_t, gate_w, up_w = (line_units[i].reshape(width, -1) for i in range(3))

    cot_parts = jnp.concatenate(ways.gather_group(after(half_cot, weight_out)))
    group_cot = ways.join(cot_parts, ways.swap(cot_parts))
    dealt_cot = group_cot[:rows]

    seq_dev = seq_deal.shape[0] // ways.n
    mine = lax.dynamic_slice_in_dim(seq_deal, me * seq_dev, seq_dev)
    position, mask = layout(lengths[mine], rows)
    cosine, sine = angles(position, HEAD_SIZE)

    heads_q = query_w.shape[1] // HEAD_SIZE
    heads_kv = key_w.shape[1] // HEAD_SIZE
    head_group = heads_q // heads_kv
    root = HEAD_SIZE ** (-0.5)
    inputs = dealt.astype(F32)
    normed1, scale1 = normalize(inputs)
    hidden1 = (normed1 * gain_a).astype(BF)
    query = mat_nn(hidden1, query_w).reshape(rows, heads_q, HEAD_SIZE)
    key = mat_nn(hidden1, key_w).reshape(rows, heads_kv, HEAD_SIZE)
    value = mat_nn(hidden1, value_w).astype(BF).reshape(rows, heads_kv, HEAD_SIZE)
    query_rot = (
        apply_rotary(query, cosine, sine)
        .astype(BF)
        .reshape(rows, heads_kv, head_group, HEAD_SIZE)
    )
    key_rot = apply_rotary(key, cosine, sine).astype(BF)
    scores = jnp.einsum("rhgd,chd->hgrc", query_rot, key_rot, preferred_element_type=F32) * root
    scores = jnp.where(mask[None, None], scores, -1e30)
    top = jnp.max(scores, axis=-1, keepdims=True)
    expo = jnp.exp(scores - top)
    prob = expo / jnp.sum(expo, axis=-1, keepdims=True)
    prob_low = prob.astype(BF)
    mixed = (
        jnp.einsum("hgrc,chd->rhgd", prob_low, value, preferred_element_type=F32)
        .reshape(rows, heads_q * HEAD_SIZE)
        .astype(BF)
    )
    part = mat_nt(mixed, weight_out)
    middle = inputs + (part + ways.swap(part.astype(BF)).astype(F32))
    normed2, scale2 = normalize(middle)
    hidden2 = (normed2 * gain_f).astype(BF)

    parts = jnp.concatenate(ways.gather_group(ways.own_half(hidden2)))
    group_h2 = ways.join(parts, ways.swap(parts))
    grad_inner = mat_nn(group_cot, down_t)
    gate = mat_nn(group_h2, gate_w)
    upper = mat_nn(group_h2, up_w)
    sigma = jax.nn.sigmoid(gate)
    activ = gate * sigma
    inner = (activ * upper).astype(BF)
    grad_gate = (grad_inner * upper * (sigma * (1.0 + gate * (1.0 - sigma)))).astype(BF)
    grad_up = (grad_inner * activ).astype(BF)

    def token_sum(terms):
        other = ways.swap(ways.other_half(terms).astype(BF)).astype(F32)
        whole = ways.own_half(terms) + other
        return ways.scatter_group([whole[k * rows : (k + 1) * rows] for k in range(GROUP)])

    half_dh2 = token_sum(mat_nt(grad_gate, gate_w) + mat_nt(grad_up, up_w))
    sum_wd = ways.scatter_line(mat_tn(group_cot, inner))
    sum_wg = ways.scatter_line(mat_tn(group_h2, grad_gate))
    sum_wu = ways.scatter_line(mat_tn(group_h2, grad_up))
    half_result = ways.own_half(middle) + token_sum(mat_nt(inner, down_t))

    def give_back(half):
        slots = mat_tn(into, half.astype(BF)).astype(BF)
        back = mat_tn(out, ways.exchange(slots)).astype(BF)
        return ways.join(back, ways.swap(back))

    activations = give_back(half_result)

    grad_h2 = ways.join(half_dh2, ways.swap(half_dh2))
    grad_gf = jnp.sum(grad_h2 * normed2, axis=0)
    grad_mid = dealt_cot.astype(F32) + norm_back(grad_h2, normed2, scale2, gain_f)
    mid_low = grad_mid.astype(BF)

    grad_mixed = (
        mat_nn(mid_low, weight_out).astype(BF).reshape(rows, heads_kv, head_group, HEAD_SIZE)
    )
    grad_wo = mat_tn(mid_low, mixed)
    grad_prob = jnp.einsum("rhgd,chd->hgrc", grad_mixed, value, preferred_element_type=F32)
    delta = jnp.sum(prob * grad_prob, axis=-1, keepdims=True)
    grad_scores = (prob * (grad_prob - delta)).astype(BF)
    grad_qrot = (
        jnp.einsum("hgrc,chd->rhgd", grad_scores, key_rot, preferred_element_type=F32) * root
    )
    grad_krot = (
        jnp.einsum("hgrc,rhgd->chd", grad_scores, query_rot, preferred_element_type=F32) * root
    )
    grad_value = jnp.einsum("hgrc,rhgd->chd", prob_low, grad_mixed, preferred_element_type=F32)
    grad_q = (
        unrotate(grad_qrot.reshape(rows, heads_q, HEAD_SIZE), cosine, sine)
        .reshape(rows, heads_q * HEAD_SIZE)
        .astype(BF)
    )
    grad_k = unrotate(grad_krot, cosine, sine).reshape(rows, heads_kv * HEAD_SIZE).astype(BF)
    grad_v = grad_value.reshape(rows, heads_kv * HEAD_SIZE).astype(BF)

    def attention_sum(terms):
        count, cols = ways.depth, terms.shape[1]
        each = terms.shape[0] // (count * GROUP)
        view = terms.reshape(count, GROUP, each, cols)
        parts = [
            lax.dynamic_slice(
                view, (0, ways.p ^ k, 0, 0), (count, 1, each, cols)
            ).reshape(count * each, cols)
            for k in range(GROUP)
        ]
        return ways.scatter_line(ways.scatter_group(parts))

    sum_wo = attention_sum(grad_wo)
    grad_qkv = jnp.concatenate([grad_q, grad_k, grad_v], axis=1)
    sum_qkv = attention_sum(mat_tn(hidden1, grad_qkv))
    part = mat_nt(grad_qkv, weight_qkv)
    grad_h1 = part + ways.swap(part.astype(BF)).astype(F32)
    grad_ga = jnp.sum(grad_h1 * normed1, axis=0)
    grad_in = grad_mid + norm_back(grad_h1, normed1, scale1, gain_a)
    input_grad = give_back(ways.own_half(grad_in))

    gain_grads = jnp.sum(
        ways.exchange(jnp.stack([grad_ga, grad_gf]).reshape(2, ways.n, -1).swapaxes(0, 1)), axis=0
    )
    owned = (
        gain_grads[0],
        sum_qkv[:, :wide_q],
        sum_qkv[:, wide_q : wide_q + wide_k],
        sum_qkv[:, wide_q + wide_k :],
        sum_wo.T,
        gain_grads[1],
        ways.collect_units(sum_wg),
        ways.collect_units(sum_wu),
        ways.collect_units(sum_wd).T,
    )
    share = 0.5 * (jnp.sum(owned[0] * owned[0]) + jnp.sum(owned[5] * owned[5]))
    for k in (1, 2, 3, 4, 6, 7, 8):
        share = share + jnp.sum(owned[k] * owned[k])
    axes = ("line", "group", "mp")
    shares = jnp.broadcast_to(share, (2 * ways.n, 8, 128))
    shares = lax.all_to_all(shares, axes, split_axis=0, concat_axis=0, tiled=True)
    grad_norm = jnp.sqrt(jnp.sum(shares[:, 0, 0]))
    factor = jnp.minimum(1.0, math.sqrt(PARAMS) / grad_norm)
    weights = (gain_attn, w_query, key_weight, value_weight, w_out, gain_ffn, w_gate, w_up, w_down)
    moments = (
        moment_gain_attn,
        moment_w_query,
        key_weight_momentum,
        value_weight_momentum,
        moment_w_out,
        moment_gain_ffn,
        moment_w_gate,
        moment_w_up,
        moment_w_down,
    )
    new_moments = tuple(0.5 * m + 0.5 * factor * g for m, g in zip(moments, owned))
    new_weights = tuple(w - LEARN * (m + DECAY * w) for w, m in zip(weights, new_moments))
    return (activations, input_grad, grad_norm, *new_moments, *new_weights)


def solution(mesh):
    count, cores = mesh.devices.shape
    regrouped = Mesh(
        mesh.devices.reshape(count // GROUP, GROUP, cores), ("line", "group", "mp")
    )
    dp = ("line", "group")
    gain, tall, wide, row = P(dp), P(dp, "mp"), P("mp", dp), P(dp, None)
    leaves = (gain, tall, tall, tall, wide, gain, tall, tall, wide)
    return jax.shard_map(
        on_device,
        mesh=regrouped,
        in_specs=(row, row, P(), P(), P(), *leaves, *leaves),
        out_specs=(row, row, P(), *leaves, *leaves),
        check_vma=False,
    )
```

```python
import functools
import math

import jax
import jax.numpy as jnp
from jax import lax
from jax.experimental import pallas as pl
from jax.experimental.pallas import tpu as pltpu
from jax.sharding import Mesh
from jax.sharding import PartitionSpec as P

HEAD_SIZE = 256
PARAMS = 62918656
EPS = 1e-06
THETA = 1000042.0
LEARN = 0.5
DECAY = 0.1
GROUP = 4
BF = jnp.bfloat16
F32 = jnp.float32


def angles(position, head):
    half = head // 2
    freq = THETA ** (-(2.0 * jnp.arange(half, dtype=F32)) / head)
    turned = position[:, None] * freq[None, :]
    return (jnp.cos(turned)[:, None, :], jnp.sin(turned)[:, None, :])


def apply_rotary(value, cosine, sine):
    half = value.shape[-1] // 2
    first, second = value[..., :half], value[..., half:]
    return jnp.concatenate(
        [first * cosine - second * sine, second * cosine + first * sine], axis=-1
    )


def unrotate(grads, cosine, sine):
    half = grads.shape[-1] // 2
    first, second = grads[..., :half], grads[..., half:]
    return jnp.concatenate(
        [first * cosine + second * sine, second * cosine - first * sine], axis=-1
    )


def layout(block_len, rows):
    rank = jnp.arange(block_len.shape[0], dtype=jnp.int32)
    ends = jnp.sum(jnp.where(rank[None, :] <= rank[:, None], block_len[None, :], 0), axis=1)
    starts = ends - block_len
    index = jnp.arange(rows, dtype=jnp.int32)
    inside = (index[:, None] >= starts[None, :]) & (index[:, None] < ends[None, :])
    segment = jnp.sum(jnp.where(inside, rank[None, :], 0), axis=1)
    position = jnp.sum(jnp.where(inside, index[:, None] - starts[None, :], 0), axis=1)
    mask = (segment[:, None] == segment[None, :]) & (index[None, :] <= index[:, None])
    return (position.astype(F32), mask)


def normalize(value):
    scale_inv = lax.rsqrt(jnp.mean(value * value, axis=-1, keepdims=True) + EPS)
    return (value * scale_inv, scale_inv)


def norm_back(grad_normed, normed, scale_inv, gain):
    scaled = grad_normed * gain
    return scale_inv * (scaled - normed * jnp.mean(scaled * normed, axis=-1, keepdims=True))


def mat_nn(left, right):
    return jnp.dot(left, right, preferred_element_type=F32)


def mat_nt(left, right):
    return lax.dot_general(left, right, (((1,), (1,)), ((), ())), preferred_element_type=F32)


def mat_tn(left, right):
    return lax.dot_general(left, right, (((0,), (0,)), ((), ())), preferred_element_type=F32)


def after(value, *others):
    return lax.optimization_barrier((value, *others))[0]


MESH = pl.DeviceIdType.MESH
ANY = pl.BlockSpec(memory_space=pl.ANY)
WHOLE = pl.BlockSpec(memory_space=pltpu.VMEM)


def places():
    z, p, core = lax.axis_index("line"), lax.axis_index("group"), lax.axis_index("mp")
    one = p + 1 - 2 * lax.rem(p, 2)
    two = p + 2 - 4 * (p // 2)
    three = GROUP - 1 - p
    return z, p, core, one, two, three


def meet(partners):
    barrier = pltpu.get_barrier_semaphore()
    for partner in partners:
        pl.semaphore_signal(barrier, inc=1, device_id=partner, device_id_type=MESH)
    pl.semaphore_wait(barrier, len(partners))


def to(src, dst, send, recv, partner):
    return pltpu.make_async_remote_copy(
        src_ref=src, dst_ref=dst, send_sem=send, recv_sem=recv,
        device_id=partner, device_id_type=MESH,
    )


def share_rows_kernel(h, out, send, recv, local):
    z, p, core, one, two, _ = places()
    rows, width = h.shape
    half, wide = rows // 2, width // 2
    cols = pl.ds(pl.multiple_of(core * wide, wide), wide)
    x, y, twin = (z, one, core), (z, two, core), (z, p, 1 - core)
    meet([x, y, twin])
    own = pltpu.make_async_copy(h, out.at[pl.ds(0, rows)], local)
    own.start()
    first, second = pl.ds(0, half), pl.ds(half, half)

    def part(k, b):
        return out.at[pl.ds(k * rows + b * half, half), cols]

    copies = {}

    def go(name, i, src, dst, partner):
        copies[name] = to(src, dst, send.at[i], recv.at[i], partner)
        copies[name].start()

    go("1a", 0, h.at[first, cols], part(1, 0), x)
    go("2b", 3, h.at[second, cols], part(2, 1), y)
    go("1b", 1, h.at[second, cols], part(1, 1), x)
    go("2a", 2, h.at[first, cols], part(2, 0), y)
    copies["1a"].wait_recv()
    go("3a", 4, part(1, 0), part(3, 0), y)
    copies["2b"].wait_recv()
    go("3b", 5, part(2, 1), part(3, 1), x)
    go("t0", 6, part(1, 0), part(1, 0), twin)
    go("t3", 9, part(2, 1), part(2, 1), twin)
    copies["1b"].wait_recv()
    go("t1", 7, part(1, 1), part(1, 1), twin)
    copies["2a"].wait_recv()
    go("t2", 8, part(2, 0), part(2, 0), twin)
    copies["3a"].wait_recv()
    go("t4", 10, part(3, 0), part(3, 0), twin)
    copies["3b"].wait_recv()
    go("t5", 11, part(3, 1), part(3, 1), twin)
    for i in range(6):
        copies["t%d" % i].wait_recv()
    for c in copies.values():
        c.wait_send()
    own.wait()


def share_rows(h, ident):
    rows, width = h.shape
    return pl.pallas_call(
        share_rows_kernel,
        out_shape=jax.ShapeDtypeStruct((GROUP * rows, width), h.dtype),
        in_specs=[WHOLE],
        out_specs=ANY,
        scratch_shapes=[
            pltpu.SemaphoreType.DMA((12,)),
            pltpu.SemaphoreType.DMA((12,)),
            pltpu.SemaphoreType.DMA,
        ],
        compiler_params=pltpu.CompilerParams(collective_id=ident, has_side_effects=True),
        name="share_rows",
    )(h)


def share_weights_kernel(n, *refs):
    owns, outs, helds, (send, recv, local) = refs[:n], refs[n : 2 * n], refs[2 * n : 3 * n], refs[3 * n :]
    z, p, core, one, two, _ = places()
    x, y = (z, one, core), (z, two, core)
    half = owns[0].shape[0] // 2
    low, high = pl.ds(0, half), pl.ds(half, half)
    loads = [pltpu.make_async_copy(owns[i], helds[i], local.at[0, i]) for i in range(n)]
    stores = [pltpu.make_async_copy(helds[i], outs[i].at[:, p], local.at[1, i]) for i in range(n)]
    for load in loads:
        load.start()
    meet([x, y])
    copies = {}

    def go(i, c, src, dst, partner):
        copies[i, c] = to(src, dst, send.at[i, c], recv.at[i, c], partner)
        copies[i, c].start()

    for i in range(n):
        own, out = owns[i], outs[i]
        go(i, 0, own.at[low], out.at[low, p], x)
        go(i, 1, own.at[high], out.at[high, p], y)
        go(i, 2, own.at[high], out.at[high, p], x)
        go(i, 3, own.at[low], out.at[low, p], y)
    for i in range(n):
        loads[i].wait()
        stores[i].start()
    for i in range(n):
        copies[i, 0].wait_recv()
        go(i, 4, outs[i].at[low, one], outs[i].at[low, one], y)
        copies[i, 1].wait_recv()
        go(i, 5, outs[i].at[high, two], outs[i].at[high, two], x)
    for (_, c), copy in copies.items():
        if c > 1:
            copy.wait_recv()
    for copy in copies.values():
        copy.wait_send()
    for store in stores:
        store.wait()


def share_weights(lines, ident):
    depth = lax.axis_size("line")
    n = len(lines)
    each = lines[0].shape[0] // depth
    outs = pl.pallas_call(
        functools.partial(share_weights_kernel, n),
        out_shape=[
            jax.ShapeDtypeStruct((depth, GROUP, each, v.shape[1]), v.dtype) for v in lines
        ],
        in_specs=[ANY] * n,
        out_specs=[ANY] * n,
        scratch_shapes=[pltpu.VMEM((depth, each, v.shape[1]), v.dtype) for v in lines]
        + [
            pltpu.SemaphoreType.DMA((n, 6)),
            pltpu.SemaphoreType.DMA((n, 6)),
            pltpu.SemaphoreType.DMA((2, n)),
        ],
        compiler_params=pltpu.CompilerParams(collective_id=ident, has_side_effects=True),
        name="share_weights",
    )(*[v.reshape(depth, each, v.shape[1]) for v in lines])
    return [v.reshape(depth * GROUP * each, v.shape[3]) for v in outs]


TILE = 256


def sum_rows_kernel(sizes, *refs):
    pairs = sum(sizes)
    ins, outs = refs[: 2 * pairs], refs[2 * pairs : 2 * pairs + len(sizes)]
    refs = refs[2 * pairs + len(sizes) :]
    mines, others, refs = refs[:pairs], refs[pairs : 2 * pairs], refs[2 * pairs :]
    left, total, give, take, packed, from_x, from_y, diag_x, diag_y, send, recv, local = refs
    z, p, core, one, two, _ = places()
    rows, wide = outs[0].shape
    half = rows // 2
    x, y, twin = (z, one, core), (z, two, core), (z, p, 1 - core)
    firsts = [sum(sizes[:j]) for j in range(len(sizes))]
    steps = [(j, k) for j in range(len(sizes)) for k in (3, 1, 2, 0)]
    mine = pl.ds(pl.multiple_of(core * wide, wide), wide)
    other = pl.ds(pl.multiple_of((1 - core) * wide, wide), wide)
    loads, copies = {}, {}

    def load(name, i, src, dst):
        loads[name] = pltpu.make_async_copy(src, dst, local.at[i])
        loads[name].start()

    def load_left(t):
        j, k = steps[t]
        for i in range(sizes[j]):
            load(
                ("l", t, i),
                2 * pairs + t * max(sizes) + i,
                ins[2 * (firsts[j] + i)].at[pl.ds(k * rows, rows)],
                left.at[t % 2, i],
            )

    def load_right(kind, j, where, buffers):
        for i in range(firsts[j], firsts[j] + sizes[j]):
            load((kind, i), i + (pairs if kind == "m" else 0), ins[2 * i + 1].at[where], buffers[i])

    load_right("o", 0, other, others)
    load_left(0)
    load_right("m", 0, mine, mines)
    load_left(1)
    for j in range(1, len(sizes)):
        load_right("o", j, other, others)
        load_right("m", j, mine, mines)
    meet([x, y, twin])

    def go(name, j, i, src, dst, partner):
        copies[name, j] = to(src, dst, send.at[j, i], recv.at[j, i], partner)
        copies[name, j].start()

    def product(t, rights, store):
        j, _ = steps[t]

        def step(i, carry):
            at = pl.ds(pl.multiple_of(i * TILE, TILE), TILE)
            value = mat_nt(left[t % 2, 0], rights[firsts[j]][at, :])
            for n in range(1, sizes[j]):
                value = value + mat_nt(left[t % 2, n], rights[firsts[j] + n][at, :])
            store(at, value)
            return carry

        lax.fori_loop(0, wide // TILE, step, 0)

    def slot(t):
        j, k = steps[t]
        return t % 2 if k else 2 + j

    def away(t):
        j, k = steps[t]
        if t >= 2:
            copies[("t", steps[t - 2][1]), steps[t - 2][0]].wait_send()

        def store(at, value):
            give[t % 2, :, at] = value.astype(BF)

        product(t, others, store)
        go(("t", k), j, k, give.at[t % 2], take.at[j, k], twin)

    def here(t):
        def store(at, value):
            total[slot(t), :, at] = value

        product(t, mines, store)

    low, high = pl.ds(0, half), pl.ds(half, half)

    def term(t, at):
        j, k = steps[t]
        return total[slot(t), at, :] + take[j, k, at, :].astype(F32)

    def finish(t):
        j, k = steps[t]
        copies[("t", k), j].wait_recv()
        if k == 3:
            packed[j, 0] = term(t, pl.ds(0, rows)).astype(BF)
            go("3a", j, 4, packed.at[j, 0, low], diag_y.at[j], y)
            go("3b", j, 5, packed.at[j, 0, high], diag_x.at[j], x)
        elif k == 1:
            packed[j, 1, high, :] = term(t, high).astype(BF)
            go("1b", j, 6, packed.at[j, 1, high], from_x.at[j, high], x)
            value = term(t, low)
            packed[j, 1, low, :] = value.astype(BF)
        elif k == 2:
            packed[j, 2, low, :] = term(t, low).astype(BF)
            go("2a", j, 8, packed.at[j, 2, low], from_y.at[j, low], y)
            packed[j, 2, high, :] = term(t, high).astype(BF)

    def relay_x(j):
        copies["3a", j].wait_recv()
        packed[j, 1, low, :] = (packed[j, 1, low, :].astype(F32) + diag_y[j].astype(F32)).astype(BF)
        go("1a", j, 7, packed.at[j, 1, low], from_x.at[j, low], x)

    def relay_y(j):
        copies["3b", j].wait_recv()
        packed[j, 2, high, :] = (packed[j, 2, high, :].astype(F32) + diag_x[j].astype(F32)).astype(BF)
        go("2b", j, 9, packed.at[j, 2, high], from_y.at[j, high], y)

    def wait(kind, j):
        for i in range(firsts[j], firsts[j] + sizes[j]):
            loads[kind, i].wait()

    for t, (j, k) in enumerate(steps):
        for i in range(sizes[j]):
            loads["l", t, i].wait()
        if k == 3:
            wait("o", j)
        away(t)
        if k == 3:
            wait("m", j)
        if k in (1, 2, 0):
            finish(t - 1)
        if k == 0:
            relay_x(j)
        if k == 3 and j:
            relay_y(j - 1)
        here(t)
        if t + 2 < len(steps):
            load_left(t + 2)
    relay_y(len(sizes) - 1)
    for j in range(len(sizes)):
        copies[("t", 0), j].wait_recv()
        for name in ("1a", "1b", "2a", "2b"):
            copies[name, j].wait_recv()
        outs[j][...] = (
            term(4 * j + 3, pl.ds(0, rows)) + from_x[j].astype(F32) + from_y[j].astype(F32)
        )
    waited = {(("t", steps[t][1]), steps[t][0]) for t in range(len(steps) - 2)}
    for name, copy in copies.items():
        if name not in waited:
            copy.wait_send()


def sum_rows(sums, ident):
    sizes = tuple(len(pairs) for pairs in sums)
    flat = [v for pairs in sums for pair in pairs for v in pair]
    rows = flat[0].shape[0] // GROUP
    units = flat[0].shape[1]
    wide = flat[1].shape[0] // 2
    n, m = sum(sizes), len(sizes)
    return pl.pallas_call(
        functools.partial(sum_rows_kernel, sizes),
        out_shape=[jax.ShapeDtypeStruct((rows, wide), F32)] * m,
        in_specs=[ANY] * (2 * n),
        out_specs=[WHOLE] * m,
        scratch_shapes=[pltpu.VMEM((wide, units), BF)] * (2 * n)
        + [
            pltpu.VMEM((2, max(sizes), rows, units), BF),
            pltpu.VMEM((2 + m, rows, wide), F32),
            pltpu.VMEM((2, rows, wide), BF),
            pltpu.VMEM((m, GROUP, rows, wide), BF),
            pltpu.VMEM((m, 3, rows, wide), BF),
            pltpu.VMEM((m, rows, wide), BF),
            pltpu.VMEM((m, rows, wide), BF),
            pltpu.VMEM((m, rows // 2, wide), BF),
            pltpu.VMEM((m, rows // 2, wide), BF),
            pltpu.SemaphoreType.DMA((m, 10)),
            pltpu.SemaphoreType.DMA((m, 10)),
            pltpu.SemaphoreType.DMA((2 * n + 4 * m * max(sizes),)),
        ],
        compiler_params=pltpu.CompilerParams(
            collective_id=ident, has_side_effects=True, vmem_limit_bytes=58 << 20
        ),
        name="sum_rows",
    )(*flat)


WIDTH = 512


def finish_kernel(
    g_out, g_qkv, sum_0, sum_1, sum_d, slots, gain_terms,
    new_qkv, new_out, new_gate, new_up, new_down, new_gain, norm, back,
    own, to_x, to_y, diag_x, diag_y, from_x, from_y, add_x, add_y, sums, packed, line,
    ffn, gain_got, shares,
    send, recv, local, row_send, row_recv, ends, keeps, unit_send, unit_recv, unit_local, all_send, all_recv,
):
    z, p, core, one, two, three = places()
    depth, _, each, _ = g_out.shape
    count = slots.shape[0]
    wide = slots.shape[2] // 2
    units = sum_d.shape[1]
    span = units // 2
    me = z * GROUP + p
    half = depth // 2
    low, high = pl.ds(0, half), pl.ds(half, half)
    x, y, twin = (z, one, core), (z, two, core), (z, p, 1 - core)
    column = [(lax.rem(z + s, depth), p, core) for s in range(1, depth)]
    columns = pl.ds(pl.multiple_of(core * wide, wide), wide)
    places_of = [(g, c) for g in (g_out, g_qkv) for c in range(g.shape[3] // WIDTH)]
    chunks = len(places_of)

    def source(rows, q, c):
        g, at = places_of[c]
        return g.at[rows, q, :, pl.ds(at * WIDTH, WIDTH)]

    loads = []
    for c in range(chunks):
        loads.append(pltpu.make_async_copy(source(pl.ds(0, depth), p, c), own.at[c], local.at[0, c]))
        loads.append(pltpu.make_async_copy(source(low, one, c), to_x.at[c], local.at[1, c]))
        loads.append(pltpu.make_async_copy(source(high, two, c), to_y.at[c], local.at[2, c]))
    for load in loads:
        load.start()

    def partner(s):
        t = lax.rem(me + s, count)
        return t, (t // GROUP, lax.rem(t, GROUP), core)

    def anyone(s):
        t = lax.rem(me * 2 + core + s, 2 * count)
        return (t // (2 * GROUP), lax.rem(t // 2, GROUP), lax.rem(t, 2))

    barrier = pltpu.get_barrier_semaphore()

    def greet(s, carry):
        pl.semaphore_signal(barrier, inc=1, device_id=anyone(s), device_id_type=MESH)
        return carry

    lax.fori_loop(1, 2 * count, greet, 0)
    keep = [
        pltpu.make_async_copy(
            slots.at[me, :, pl.ds(i * wide, wide)], back.at[i, me, :, columns], keeps.at[i]
        )
        for i in range(2)
    ] + [pltpu.make_async_copy(gain_terms.at[me], gain_got.at[me], keeps.at[2])]
    for copy in keep:
        copy.start()

    def unit_parts(q, of):
        rows = pl.ds(pl.multiple_of(q * each, each), each)

        def place(i, shift, size):
            return ffn.at[i, :, pl.ds(pl.multiple_of(of * units + shift, span), size)]

        return [
            (sum_0.at[rows, pl.ds(0, span)], place(0, 0, span)),
            (sum_0.at[rows, pl.ds(span, span)], place(1, 0, span)),
            (sum_1.at[rows, pl.ds(0, span)], place(0, span, span)),
            (sum_1.at[rows, pl.ds(span, span)], place(1, span, span)),
            (sum_d.at[rows], place(2, 0, units)),
        ]

    stay = [
        pltpu.make_async_copy(src, dst, unit_local.at[i])
        for i, (src, dst) in enumerate(unit_parts(p, p))
    ]
    for copy in stay:
        copy.start()
    pl.semaphore_wait(barrier, 2 * count - 1)
    copies = {}

    def rows(s, kinds):
        t, who = partner(s)
        made = []
        for i in kinds:
            if i < 2:
                src, dst = slots.at[t, :, pl.ds(i * wide, wide)], back.at[i, me, :, columns]
            else:
                src, dst = gain_terms.at[t], gain_got.at[me]
            made.append(to(src, dst, row_send.at[i, s], row_recv.at[i, s], who))
        return made

    def each_row(act):
        def step(s, carry):
            for copy in rows(s, (0, 1, 2)):
                act(copy)
            return carry

        lax.fori_loop(1, count, step, 0)

    def go(name, c, i, src, dst, who):
        copies[name, c] = to(src, dst, send.at[c, i], recv.at[c, i], who)
        copies[name, c].start()

    def first(c):
        go("3a", c, 0, source(low, three, c), diag_y.at[c], y)
        go("3b", c, 1, source(high, three, c), diag_x.at[c], x)
        go("1b", c, 2, source(high, one, c), from_x.at[c, high], x)
        go("2a", c, 3, source(low, two, c), from_y.at[c, low], y)

    def relay(c):
        copies["3a", c].wait_recv()
        add_x[c] = (to_x[c].astype(F32) + diag_y[c].astype(F32)).astype(BF)
        go("1a", c, 4, add_x.at[c], from_x.at[c, low], x)
        copies["3b", c].wait_recv()
        add_y[c] = (to_y[c].astype(F32) + diag_x[c].astype(F32)).astype(BF)
        go("2b", c, 5, add_y.at[c], from_y.at[c, high], y)

    def along(c):
        for name in ("1a", "1b", "2a", "2b"):
            copies[name, c].wait_recv()
        sums[c] = own[c].astype(F32) + from_x[c].astype(F32) + from_y[c].astype(F32)
        packed[c] = sums[c].astype(BF)
        for s, who in enumerate(column, 1):
            go(s, c, 5 + s, packed.at[c, who[0]], line.at[c, s - 1], who)

    first(0)
    each_row(lambda copy: copy.start())
    first(1)
    shared = []
    for k, q in ((3, three), (1, one), (2, two)):
        for i, (src, dst) in enumerate(unit_parts(q, p)):
            copy = to(src, dst, unit_send.at[k, i], unit_recv.at[k, i], (z, q, core))
            copy.start()
            shared.append(copy)
    for load in loads:
        load.wait()
    for c in range(chunks):
        relay(c)
        if c + 2 < chunks:
            first(c + 2)
        if c:
            along(c - 1)
    for copy in keep:
        copy.wait()
    each_row(lambda copy: copy.wait_recv())
    pass_on = to(
        back.at[:, :, :, columns], back.at[:, :, :, columns], ends.at[0], ends.at[1], twin
    )
    pass_on.start()
    along(chunks - 1)

    def squares(value):
        return jnp.sum(jnp.sum(value * value, axis=0, keepdims=True), axis=1, keepdims=True)

    for copy in stay:
        copy.wait()
    for copy in shared:
        copy.wait_recv()
    total = jnp.zeros((1, 1), F32)
    for i, ref in ((0, new_gate), (1, new_up)):
        for at in range(0, ref.shape[1], WIDTH):
            value = ffn[i, :, at : at + WIDTH].astype(F32)
            total = total + squares(value)
            ref[:, at : at + WIDTH] = value
    for at in range(0, new_down.shape[0], 128):
        value = ffn[2, :, at : at + 128].astype(F32)
        total = total + squares(value)
        new_down[at : at + 128, :] = value.T
    gain = gain_got[0]
    for t in range(1, count):
        gain = gain + gain_got[t]
    new_gain[...] = gain
    total = total + 0.5 * squares(gain[:2])
    for c in range(chunks):
        value = sums[c, z]
        for s in range(1, depth):
            copies[s, c].wait_recv()
            value = value + line[c, s - 1].astype(F32)
        total = total + squares(value)
        g, at = places_of[c]
        if g is g_qkv:
            new_qkv[:, pl.ds(at * WIDTH, WIDTH)] = value
        else:
            for i in range(0, WIDTH, 128):
                new_out[pl.ds(at * WIDTH + i, 128), :] = value[:, i : i + 128].T
    shares[0] = jnp.broadcast_to(total, (8, 128))

    def tell(s):
        return to(shares.at[0], shares.at[s], all_send.at[s], all_recv.at[s], anyone(s))

    def tell_start(s, carry):
        tell(s).start()
        return carry

    def tell_end(s, carry):
        tell(s).wait_recv()
        return carry

    def tell_left(s, carry):
        tell(s).wait_send()
        return carry

    lax.fori_loop(1, 2 * count, tell_start, 0)
    lax.fori_loop(1, 2 * count, tell_end, 0)
    everyone = jnp.sum(shares[...], axis=0)
    norm[...] = jnp.sqrt(everyone)
    lax.fori_loop(1, 2 * count, tell_left, 0)
    pass_on.wait_recv()
    for copy in [*copies.values(), *shared]:
        copy.wait_send()
    each_row(lambda copy: copy.wait_send())
    pass_on.wait_send()


def finish(g_out, g_qkv, sum_0, sum_1, sum_d, slots, gain_terms, ident):
    depth = lax.axis_size("line")
    each = g_qkv.shape[0] // (depth * GROUP)
    units = sum_d.shape[1]
    chunks = (g_out.shape[1] + g_qkv.shape[1]) // WIDTH
    count, per, both = slots.shape

    def buffer(rows, dtype=BF):
        return pltpu.VMEM((chunks, rows, each, WIDTH), dtype)

    return pl.pallas_call(
        finish_kernel,
        out_shape=[
            jax.ShapeDtypeStruct((each, g_qkv.shape[1]), F32),
            jax.ShapeDtypeStruct((g_out.shape[1], each), F32),
            jax.ShapeDtypeStruct((each, GROUP * units), F32),
            jax.ShapeDtypeStruct((each, GROUP * units), F32),
            jax.ShapeDtypeStruct((GROUP * units, each), F32),
            jax.ShapeDtypeStruct(gain_terms.shape[1:], F32),
            jax.ShapeDtypeStruct((8, 128), F32),
            jax.ShapeDtypeStruct((2, count, per, both), BF),
        ],
        in_specs=[ANY] * 5 + [WHOLE] * 2,
        out_specs=[WHOLE] * 7 + [ANY],
        scratch_shapes=[
            buffer(depth),
            buffer(depth // 2),
            buffer(depth // 2),
            buffer(depth // 2),
            buffer(depth // 2),
            buffer(depth),
            buffer(depth),
            buffer(depth // 2),
            buffer(depth // 2),
            buffer(depth, F32),
            buffer(depth),
            buffer(depth - 1),
            pltpu.VMEM((3, each, GROUP * units), BF),
            pltpu.VMEM(gain_terms.shape, F32),
            pltpu.VMEM((2 * count, 8, 128), F32),
            pltpu.SemaphoreType.DMA((chunks, 5 + depth)),
            pltpu.SemaphoreType.DMA((chunks, 5 + depth)),
            pltpu.SemaphoreType.DMA((3, chunks)),
            pltpu.SemaphoreType.DMA((3, count)),
            pltpu.SemaphoreType.DMA((3, count)),
            pltpu.SemaphoreType.DMA((2,)),
            pltpu.SemaphoreType.DMA((3,)),
            pltpu.SemaphoreType.DMA((4, 5)),
            pltpu.SemaphoreType.DMA((4, 5)),
            pltpu.SemaphoreType.DMA((5,)),
            pltpu.SemaphoreType.DMA((2 * count,)),
            pltpu.SemaphoreType.DMA((2 * count,)),
        ],
        compiler_params=pltpu.CompilerParams(
            collective_id=ident, has_side_effects=True, vmem_limit_bytes=58 << 20
        ),
        name="finish",
    )(
        g_out.reshape(depth, GROUP, each, -1),
        g_qkv.reshape(depth, GROUP, each, -1),
        sum_0,
        sum_1,
        sum_d,
        slots,
        gain_terms,
    )


def deal_kernel(sent, pieces, gains, tokens, cots, units, all_gains, held, send, recv, ends, local):
    z, p, core, one, two, three = places()
    count, per, both = sent.shape
    wide = both // 2
    me = z * GROUP + p
    cols = pl.ds(pl.multiple_of(core * wide, wide), wide)
    twin = (z, p, 1 - core)

    def partner(s):
        t = lax.rem(me + s, count)
        return t, (t // GROUP, lax.rem(t, GROUP), core)

    barrier = pltpu.get_barrier_semaphore()

    def greet(s, carry):
        pl.semaphore_signal(barrier, inc=1, device_id=partner(s)[1], device_id_type=MESH)
        return carry

    lax.fori_loop(1, count, greet, 0)
    pl.semaphore_signal(barrier, inc=1, device_id=twin, device_id_type=MESH)
    mine = pltpu.make_async_copy(pieces.at[p], held, local.at[0])
    mine.start()
    keep = [
        pltpu.make_async_copy(sent.at[me, :, pl.ds(0, wide)], tokens.at[me, :, cols], local.at[1]),
        pltpu.make_async_copy(sent.at[me, :, pl.ds(wide, wide)], cots.at[me], local.at[2]),
        pltpu.make_async_copy(gains, all_gains.at[me], local.at[3]),
    ]
    for copy in keep:
        copy.start()
    pl.semaphore_wait(barrier, count)

    def rows(s):
        t, who = partner(s)
        return (
            to(sent.at[t, :, pl.ds(0, wide)], tokens.at[me, :, cols], send.at[0, s], recv.at[0, s], who),
            to(sent.at[t, :, pl.ds(wide, wide)], cots.at[me], send.at[1, s], recv.at[1, s], who),
            to(gains, all_gains.at[me], send.at[2, s], recv.at[2, s], who),
        )

    def start(i):
        def step(s, carry):
            rows(s)[i].start()
            return carry

        lax.fori_loop(1, count, step, 0)

    start(0)
    start(2)
    shares = [
        to(pieces.at[q], units.at[:, p], ends.at[0, k], ends.at[1, k], (z, q, core))
        for k, q in ((1, one), (2, two), (3, three))
    ]
    for copy in shares:
        copy.start()
    start(1)
    mine.wait()
    store = pltpu.make_async_copy(held, units.at[:, p], local.at[4])
    store.start()
    keep[0].wait()

    def arrived(i):
        def step(s, carry):
            rows(s)[i].wait_recv()
            return carry

        lax.fori_loop(1, count, step, 0)

    arrived(0)
    pass_on = to(tokens.at[:, :, cols], tokens.at[:, :, cols], ends.at[0, 0], ends.at[1, 0], twin)
    pass_on.start()
    arrived(2)
    for copy in shares:
        copy.wait_recv()
    arrived(1)
    pass_on.wait_recv()

    def leave(s, carry):
        for copy in rows(s):
            copy.wait_send()
        return carry

    lax.fori_loop(1, count, leave, 0)
    for copy in [*shares, pass_on]:
        copy.wait_send()
    keep[1].wait()
    keep[2].wait()
    store.wait()


def deal(sent, pieces, gains, ident):
    count, per, both = sent.shape
    _, three, rows, units = pieces.shape
    return pl.pallas_call(
        deal_kernel,
        out_shape=[
            jax.ShapeDtypeStruct((count, per, both), BF),
            jax.ShapeDtypeStruct((count, per, both // 2), BF),
            jax.ShapeDtypeStruct((three, GROUP, rows, units), BF),
            jax.ShapeDtypeStruct((count, *gains.shape), F32),
        ],
        in_specs=[WHOLE, ANY, WHOLE],
        out_specs=[ANY] * 4,
        scratch_shapes=[
            pltpu.VMEM((three, rows, units), BF),
            pltpu.SemaphoreType.DMA((3, count)),
            pltpu.SemaphoreType.DMA((3, count)),
            pltpu.SemaphoreType.DMA((2, 4)),
            pltpu.SemaphoreType.DMA((5,)),
        ],
        compiler_params=pltpu.CompilerParams(collective_id=ident, has_side_effects=True),
        name="deal",
    )(sent, pieces, gains)


class Ways:
    def __init__(self):
        self.depth = lax.axis_size("line")
        self.n = self.depth * GROUP
        self.z = lax.axis_index("line")
        self.p = lax.axis_index("group")
        self.me = self.z * GROUP + self.p
        self.core = lax.axis_index("mp")

    def flip(self, value, k):
        return lax.ppermute(value, "group", [(i, i ^ k) for i in range(GROUP)])

    def swap(self, value):
        return lax.ppermute(value, "mp", [(0, 1), (1, 0)])

    def gather_line(self, value):
        return lax.all_gather(value, "line", axis=0, tiled=True)

    def scatter_line(self, whole):
        return lax.psum_scatter(whole, "line", scatter_dimension=0, tiled=True)

    def gather_group(self, value):
        half = value.shape[0] // 2
        one, two = self.flip(value, 1), self.flip(value, 2)
        three = jnp.concatenate([self.flip(one[:half], 2), self.flip(two[half:], 1)])
        return [value, one, two, three]

    def scatter_group(self, parts):
        half = parts[0].shape[0] // 2
        first = self.flip(parts[3][:half].astype(BF), 2).astype(F32)
        second = self.flip(parts[3][half:].astype(BF), 1).astype(F32)
        one = jnp.concatenate([parts[1][:half] + first, parts[1][half:]]).astype(BF)
        two = jnp.concatenate([parts[2][:half], parts[2][half:] + second]).astype(BF)
        return parts[0] + self.flip(one, 1).astype(F32) + self.flip(two, 2).astype(F32)

    def exchange(self, value):
        return lax.all_to_all(value, ("line", "group"), split_axis=0, concat_axis=0, tiled=True)

    def own_half(self, value):
        half = value.shape[-1] // 2
        return jnp.where(self.core == 0, value[..., :half], value[..., half:])

    def other_half(self, value):
        half = value.shape[-1] // 2
        return jnp.where(self.core == 0, value[..., half:], value[..., :half])

    def join(self, mine, other):
        return jnp.where(
            self.core == 0,
            jnp.concatenate([mine, other], axis=-1),
            jnp.concatenate([other, mine], axis=-1),
        )


def unit_pieces(down, gate, upper):
    units = down.shape[1] // GROUP
    half = units // 2

    def cut(j, c):
        at = slice(j * units + c * half, j * units + (c + 1) * half)
        return jnp.concatenate([gate[:, at], upper[:, at]], axis=1)

    return jnp.stack(
        [
            jnp.stack([down[:, j * units : (j + 1) * units], cut(j, 0), cut(j, 1)])
            for j in range(GROUP)
        ]
    )


def deal_tables(token_order, me, rows):
    blocks = token_order.shape[0] // rows
    per = rows // blocks
    index = jnp.arange(rows, dtype=jnp.int32)
    wanted = lax.dynamic_slice_in_dim(token_order, me * rows, rows)
    source = wanted // rows
    same = (source[:, None] == source[None, :]) & (index[None, :] < index[:, None])
    slot = source * per + jnp.sum(same.astype(jnp.int32), axis=1)
    into = (slot[:, None] == index[None, :]).astype(BF)
    table = token_order.reshape(blocks, rows)
    taken = table // rows == me
    earlier = (index[:, None] < index[None, :]).astype(BF)
    rank = mat_nn(taken.astype(BF), earlier).astype(jnp.int32)
    hit = taken[:, None, :] & (rank[:, None, :] == jnp.arange(per, dtype=jnp.int32)[None, :, None])
    sent = jnp.sum(jnp.where(hit, (table - me * rows)[:, None, :], 0), axis=2).reshape(rows)
    out = (sent[:, None] == index[None, :]).astype(BF)
    return into, out


def on_device(
    tokens,
    cotangent,
    lengths,
    seq_deal,
    token_order,
    gain_attn,
    w_query,
    key_weight,
    value_weight,
    w_out,
    gain_ffn,
    w_gate,
    w_up,
    w_down,
    moment_gain_attn,
    moment_w_query,
    key_weight_momentum,
    value_weight_momentum,
    moment_w_out,
    moment_gain_ffn,
    moment_w_gate,
    moment_w_up,
    moment_w_down,
):
    ways = Ways()
    rows, width = tokens.shape
    me = ways.me
    shard_qkv = jnp.concatenate(
        [w_query.astype(BF), key_weight.astype(BF), value_weight.astype(BF)], axis=1
    )
    shard_out = w_out.astype(BF).T
    line_all = ways.gather_line(jnp.concatenate([shard_qkv, shard_out], axis=1))
    line_qkv = line_all[:, : shard_qkv.shape[1]]
    line_out = line_all[:, shard_qkv.shape[1] :]

    into, out = deal_tables(token_order, me, rows)
    sent = mat_nn(
        out, jnp.concatenate([ways.own_half(tokens), ways.own_half(cotangent)], axis=1)
    ).astype(BF)
    pieces = unit_pieces(w_down.astype(BF).T, w_gate.astype(BF), w_up.astype(BF))
    gains = jnp.pad(
        jnp.stack([gain_attn, gain_ffn]).astype(BF).astype(F32), ((0, 6), (0, 0))
    )
    got_tokens, got_cot, units, all_gains = deal(
        sent.reshape(ways.n, rows // ways.n, width), pieces, gains, 5
    )
    gain_a = all_gains[:, 0].reshape(width)
    gain_f = all_gains[:, 1].reshape(width)
    dealt = mat_nn(into, got_tokens.reshape(rows, width)).astype(BF)
    half_cot = mat_nn(into, got_cot.reshape(rows, width // 2)).astype(BF)

    weight_qkv, weight_out = share_weights([line_qkv, line_out], 4)
    wide_q = w_query.shape[1]
    wide_k = key_weight.shape[1]
    query_w = weight_qkv[:, :wide_q]
    key_w = weight_qkv[:, wide_q : wide_q + wide_k]
    value_w = weight_qkv[:, wide_q + wide_k :]

    line_units = lax.all_gather(
        units.reshape(3, -1, units.shape[-1]), "line", axis=1, tiled=False
    )
    down_t, first_w, second_w = (line_units[i].reshape(width, -1) for i in range(3))

    cot_parts = jnp.concatenate(ways.gather_group(after(half_cot, weight_out)))
    group_cot = ways.join(cot_parts, ways.swap(cot_parts))
    dealt_cot = group_cot[:rows]

    seq_dev = seq_deal.shape[0] // ways.n
    mine = lax.dynamic_slice_in_dim(seq_deal, me * seq_dev, seq_dev)
    position, mask = layout(lengths[mine], rows)
    cosine, sine = angles(position, HEAD_SIZE)

    heads_q = query_w.shape[1] // HEAD_SIZE
    heads_kv = key_w.shape[1] // HEAD_SIZE
    head_group = heads_q // heads_kv
    root = HEAD_SIZE ** (-0.5)
    inputs = dealt.astype(F32)
    normed1, scale1 = normalize(inputs)
    hidden1 = (normed1 * gain_a).astype(BF)
    query = mat_nn(hidden1, query_w).reshape(rows, heads_q, HEAD_SIZE)
    key = mat_nn(hidden1, key_w).reshape(rows, heads_kv, HEAD_SIZE)
    value = mat_nn(hidden1, value_w).astype(BF).reshape(rows, heads_kv, HEAD_SIZE)
    query_rot = (
        apply_rotary(query, cosine, sine)
        .astype(BF)
        .reshape(rows, heads_kv, head_group, HEAD_SIZE)
    )
    key_rot = apply_rotary(key, cosine, sine).astype(BF)
    scores = jnp.einsum("rhgd,chd->hgrc", query_rot, key_rot, preferred_element_type=F32) * root
    scores = jnp.where(mask[None, None], scores, -1e30)
    top = jnp.max(scores, axis=-1, keepdims=True)
    expo = jnp.exp(scores - top)
    prob = expo / jnp.sum(expo, axis=-1, keepdims=True)
    prob_low = prob.astype(BF)
    mixed = (
        jnp.einsum("hgrc,chd->rhgd", prob_low, value, preferred_element_type=F32)
        .reshape(rows, heads_q * HEAD_SIZE)
        .astype(BF)
    )
    part = mat_nt(mixed, weight_out)
    middle = inputs + (part + ways.swap(part.astype(BF)).astype(F32))
    normed2, scale2 = normalize(middle)
    hidden2 = (normed2 * gain_f).astype(BF)

    group_h2 = share_rows(hidden2, 1)
    grad_inner = mat_nn(group_cot, down_t)
    span = grad_inner.shape[1] // 2

    def units_half(group_rows, weight, grad_inner):
        both = mat_nn(group_rows, weight)
        gate, upper = both[:, :span], both[:, span:]
        sigma = jax.nn.sigmoid(gate)
        activ = gate * sigma
        inner = (activ * upper).astype(BF)
        slope = sigma * (1.0 + gate * (1.0 - sigma))
        grads = jnp.concatenate([grad_inner * upper * slope, grad_inner * activ], axis=1)
        return inner, grads.astype(BF)

    inner_0, grads_0 = units_half(group_h2, first_w, grad_inner[:, :span])
    terms_0 = mat_tn(group_h2, grads_0).astype(BF)
    sum_0 = ways.scatter_line(terms_0)
    inner_1, grads_1 = units_half(after(group_h2, terms_0), second_w, grad_inner[:, span:])
    inner = jnp.concatenate([inner_0, inner_1], axis=1)
    terms_d = mat_tn(group_cot, inner).astype(BF)
    sum_d = ways.scatter_line(terms_d)
    half_dh2, half_ffn = sum_rows(
        [[(grads_0, first_w), (after(grads_1, terms_d), second_w)], [(inner, down_t)]], 2
    )
    terms_1 = mat_tn(after(group_h2, half_dh2), grads_1).astype(BF)
    sum_1 = ways.scatter_line(terms_1)
    half_dh2 = after(half_dh2, terms_1)
    half_result = ways.own_half(middle) + half_ffn

    grad_h2 = ways.join(half_dh2, ways.swap(half_dh2)) + 0.0 * sum_0[0, 0].astype(F32)
    grad_gf = jnp.sum(grad_h2 * normed2, axis=0)
    grad_mid = dealt_cot.astype(F32) + norm_back(grad_h2, normed2, scale2, gain_f)
    mid_low = grad_mid.astype(BF)

    grad_mixed = (
        mat_nn(mid_low, weight_out).astype(BF).reshape(rows, heads_kv, head_group, HEAD_SIZE)
    )
    grad_wo = mat_tn(mid_low, mixed)
    grad_prob = jnp.einsum("rhgd,chd->hgrc", grad_mixed, value, preferred_element_type=F32)
    delta = jnp.sum(prob * grad_prob, axis=-1, keepdims=True)
    grad_scores = (prob * (grad_prob - delta)).astype(BF)
    grad_qrot = (
        jnp.einsum("hgrc,chd->rhgd", grad_scores, key_rot, preferred_element_type=F32) * root
    )
    grad_krot = (
        jnp.einsum("hgrc,rhgd->chd", grad_scores, query_rot, preferred_element_type=F32) * root
    )
    grad_value = jnp.einsum("hgrc,rhgd->chd", prob_low, grad_mixed, preferred_element_type=F32)
    grad_q = (
        unrotate(grad_qrot.reshape(rows, heads_q, HEAD_SIZE), cosine, sine)
        .reshape(rows, heads_q * HEAD_SIZE)
        .astype(BF)
    )
    grad_k = unrotate(grad_krot, cosine, sine).reshape(rows, heads_kv * HEAD_SIZE).astype(BF)
    grad_v = grad_value.reshape(rows, heads_kv * HEAD_SIZE).astype(BF)

    grad_qkv = jnp.concatenate([grad_q, grad_k, grad_v], axis=1)
    part = mat_nt(grad_qkv, weight_qkv)
    other = ways.swap(part.astype(BF)).astype(F32)
    terms_qkv = mat_tn(hidden1, grad_qkv).astype(BF)
    grad_h1 = part + other
    grad_ga = jnp.sum(grad_h1 * normed1, axis=0)
    grad_in = grad_mid + norm_back(grad_h1, normed1, scale1, gain_a)
    slots = mat_tn(
        into, jnp.concatenate([half_result, ways.own_half(grad_in)], axis=1).astype(BF)
    ).astype(BF)
    gain_terms = jnp.pad(
        jnp.stack([grad_ga, grad_gf]).reshape(2, ways.n, -1).swapaxes(0, 1), ((0, 0), (0, 6), (0, 0))
    )
    new_qkv, new_out, new_gate, new_up, new_down, new_gain, norm, back = finish(
        grad_wo.astype(BF), terms_qkv, sum_0, sum_1, sum_d,
        slots.reshape(ways.n, -1, width), gain_terms, 3,
    )
    activations = mat_tn(out, back[0].reshape(rows, width)).astype(BF)
    input_grad = mat_tn(out, back[1].reshape(rows, width)).astype(BF)
    owned = (
        new_gain[0],
        new_qkv[:, :wide_q],
        new_qkv[:, wide_q : wide_q + wide_k],
        new_qkv[:, wide_q + wide_k :],
        new_out,
        new_gain[1],
        new_gate,
        new_up,
        new_down,
    )
    grad_norm = norm[0, 0]
    factor = jnp.minimum(1.0, math.sqrt(PARAMS) / grad_norm)
    weights = (gain_attn, w_query, key_weight, value_weight, w_out, gain_ffn, w_gate, w_up, w_down)
    moments = (
        moment_gain_attn,
        moment_w_query,
        key_weight_momentum,
        value_weight_momentum,
        moment_w_out,
        moment_gain_ffn,
        moment_w_gate,
        moment_w_up,
        moment_w_down,
    )
    new_moments = tuple(0.5 * m + 0.5 * factor * g for m, g in zip(moments, owned))
    new_weights = tuple(w - LEARN * (m + DECAY * w) for w, m in zip(weights, new_moments))
    return (activations, input_grad, grad_norm, *new_moments, *new_weights)


def solution(mesh):
    count, cores = mesh.devices.shape
    regrouped = Mesh(
        mesh.devices.reshape(count // GROUP, GROUP, cores), ("line", "group", "mp")
    )
    dp = ("line", "group")
    gain, tall, wide, row = P(dp), P(dp, "mp"), P("mp", dp), P(dp, None)
    leaves = (gain, tall, tall, tall, wide, gain, tall, tall, wide)
    return jax.shard_map(
        on_device,
        mesh=regrouped,
        in_specs=(row, row, P(), P(), P(), *leaves, *leaves),
        out_specs=(row, row, P(), *leaves, *leaves),
        check_vma=False,
    )
```

```python
import functools
import math

import jax
import jax.numpy as jnp
from jax import lax
from jax.experimental import pallas as pl
from jax.experimental.pallas import tpu as pltpu
from jax.sharding import Mesh
from jax.sharding import PartitionSpec as P

HEAD_SIZE = 256
PARAMS = 62918656
EPS = 1e-06
THETA = 1000042.0
LEARN = 0.5
DECAY = 0.1
GROUP = 4
BF = jnp.bfloat16
F32 = jnp.float32


def angles(position, head):
    half = head // 2
    freq = THETA ** (-(2.0 * jnp.arange(half, dtype=F32)) / head)
    turned = position[:, None] * freq[None, :]
    return (jnp.cos(turned)[:, None, :], jnp.sin(turned)[:, None, :])


def apply_rotary(value, cosine, sine):
    half = value.shape[-1] // 2
    first, second = value[..., :half], value[..., half:]
    return jnp.concatenate(
        [first * cosine - second * sine, second * cosine + first * sine], axis=-1
    )


def layout(block_len, rows):
    rank = jnp.arange(block_len.shape[0], dtype=jnp.int32)
    ends = jnp.sum(jnp.where(rank[None, :] <= rank[:, None], block_len[None, :], 0), axis=1)
    starts = ends - block_len
    index = jnp.arange(rows, dtype=jnp.int32)
    inside = (index[:, None] >= starts[None, :]) & (index[:, None] < ends[None, :])
    segment = jnp.sum(jnp.where(inside, rank[None, :], 0), axis=1)
    position = jnp.sum(jnp.where(inside, index[:, None] - starts[None, :], 0), axis=1)
    mask = (segment[:, None] == segment[None, :]) & (index[None, :] <= index[:, None])
    return (position.astype(F32), mask)


def normalize(value):
    scale_inv = lax.rsqrt(jnp.mean(value * value, axis=-1, keepdims=True) + EPS)
    return (value * scale_inv, scale_inv)


def mat_nn(left, right):
    return jnp.dot(left, right, preferred_element_type=F32)


def mat_nt(left, right):
    return lax.dot_general(left, right, (((1,), (1,)), ((), ())), preferred_element_type=F32)


def mat_tn(left, right):
    return lax.dot_general(left, right, (((0,), (0,)), ((), ())), preferred_element_type=F32)


def after(value, *others):
    return lax.optimization_barrier((value, *others))[0]


MESH = pl.DeviceIdType.MESH
ANY = pl.BlockSpec(memory_space=pl.ANY)
WHOLE = pl.BlockSpec(memory_space=pltpu.VMEM)


def places():
    z, p, core = lax.axis_index("line"), lax.axis_index("group"), lax.axis_index("mp")
    one = p + 1 - 2 * lax.rem(p, 2)
    two = p + 2 - 4 * (p // 2)
    three = GROUP - 1 - p
    return z, p, core, one, two, three


def meet(partners):
    barrier = pltpu.get_barrier_semaphore()
    for partner in partners:
        pl.semaphore_signal(barrier, inc=1, device_id=partner, device_id_type=MESH)
    pl.semaphore_wait(barrier, len(partners))


def to(src, dst, send, recv, partner):
    return pltpu.make_async_remote_copy(
        src_ref=src, dst_ref=dst, send_sem=send, recv_sem=recv,
        device_id=partner, device_id_type=MESH,
    )


def share_rows_kernel(h, out, send, recv, local):
    z, p, core, one, two, _ = places()
    rows, width = h.shape
    half, wide = rows // 2, width // 2
    cols = pl.ds(pl.multiple_of(core * wide, wide), wide)
    x, y, twin = (z, one, core), (z, two, core), (z, p, 1 - core)
    meet([x, y, twin])
    own = pltpu.make_async_copy(h, out.at[pl.ds(0, rows)], local)
    own.start()
    first, second = pl.ds(0, half), pl.ds(half, half)

    def part(k, b):
        return out.at[pl.ds(k * rows + b * half, half), cols]

    copies = {}

    def go(name, i, src, dst, partner):
        copies[name] = to(src, dst, send.at[i], recv.at[i], partner)
        copies[name].start()

    go("1a", 0, h.at[first, cols], part(1, 0), x)
    go("2b", 3, h.at[second, cols], part(2, 1), y)
    go("1b", 1, h.at[second, cols], part(1, 1), x)
    go("2a", 2, h.at[first, cols], part(2, 0), y)
    copies["1a"].wait_recv()
    go("3a", 4, part(1, 0), part(3, 0), y)
    copies["2b"].wait_recv()
    go("3b", 5, part(2, 1), part(3, 1), x)
    go("t0", 6, part(1, 0), part(1, 0), twin)
    go("t3", 9, part(2, 1), part(2, 1), twin)
    copies["1b"].wait_recv()
    go("t1", 7, part(1, 1), part(1, 1), twin)
    copies["2a"].wait_recv()
    go("t2", 8, part(2, 0), part(2, 0), twin)
    copies["3a"].wait_recv()
    go("t4", 10, part(3, 0), part(3, 0), twin)
    copies["3b"].wait_recv()
    go("t5", 11, part(3, 1), part(3, 1), twin)
    for i in range(6):
        copies["t%d" % i].wait_recv()
    for c in copies.values():
        c.wait_send()
    own.wait()


def share_rows(h, ident):
    rows, width = h.shape
    return pl.pallas_call(
        share_rows_kernel,
        out_shape=jax.ShapeDtypeStruct((GROUP * rows, width), h.dtype),
        in_specs=[WHOLE],
        out_specs=ANY,
        scratch_shapes=[
            pltpu.SemaphoreType.DMA((12,)),
            pltpu.SemaphoreType.DMA((12,)),
            pltpu.SemaphoreType.DMA,
        ],
        compiler_params=pltpu.CompilerParams(collective_id=ident, has_side_effects=True),
        name="share_rows",
    )(h)


def share_weights_kernel(n, *refs):
    owns, outs, helds, (send, recv, local) = refs[:n], refs[n : 2 * n], refs[2 * n : 3 * n], refs[3 * n :]
    z, p, core, one, two, _ = places()
    x, y = (z, one, core), (z, two, core)
    half = owns[0].shape[0] // 2
    low, high = pl.ds(0, half), pl.ds(half, half)
    loads = [pltpu.make_async_copy(owns[i], helds[i], local.at[0, i]) for i in range(n)]
    stores = [pltpu.make_async_copy(helds[i], outs[i].at[:, p], local.at[1, i]) for i in range(n)]
    for load in loads:
        load.start()
    meet([x, y])
    copies = {}

    def go(i, c, src, dst, partner):
        copies[i, c] = to(src, dst, send.at[i, c], recv.at[i, c], partner)
        copies[i, c].start()

    for i in range(n):
        own, out = owns[i], outs[i]
        go(i, 0, own.at[low], out.at[low, p], x)
        go(i, 1, own.at[high], out.at[high, p], y)
        go(i, 2, own.at[high], out.at[high, p], x)
        go(i, 3, own.at[low], out.at[low, p], y)
    for i in range(n):
        loads[i].wait()
        stores[i].start()
    for i in range(n):
        copies[i, 0].wait_recv()
        go(i, 4, outs[i].at[low, one], outs[i].at[low, one], y)
        copies[i, 1].wait_recv()
        go(i, 5, outs[i].at[high, two], outs[i].at[high, two], x)
    for (_, c), copy in copies.items():
        if c > 1:
            copy.wait_recv()
    for copy in copies.values():
        copy.wait_send()
    for store in stores:
        store.wait()


def share_weights(lines, ident):
    depth = lax.axis_size("line")
    n = len(lines)
    each = lines[0].shape[0] // depth
    outs = pl.pallas_call(
        functools.partial(share_weights_kernel, n),
        out_shape=[
            jax.ShapeDtypeStruct((depth, GROUP, each, v.shape[1]), v.dtype) for v in lines
        ],
        in_specs=[ANY] * n,
        out_specs=[ANY] * n,
        scratch_shapes=[pltpu.VMEM((depth, each, v.shape[1]), v.dtype) for v in lines]
        + [
            pltpu.SemaphoreType.DMA((n, 6)),
            pltpu.SemaphoreType.DMA((n, 6)),
            pltpu.SemaphoreType.DMA((2, n)),
        ],
        compiler_params=pltpu.CompilerParams(collective_id=ident, has_side_effects=True),
        name="share_weights",
    )(*[v.reshape(depth, each, v.shape[1]) for v in lines])
    return [v.reshape(depth * GROUP * each, v.shape[3]) for v in outs]


TILE = 256


def sum_rows_kernel(sizes, *refs):
    pairs = sum(sizes)
    ins, outs = refs[: 2 * pairs], refs[2 * pairs : 2 * pairs + len(sizes)]
    refs = refs[2 * pairs + len(sizes) :]
    mines, others, refs = refs[:pairs], refs[pairs : 2 * pairs], refs[2 * pairs :]
    left, total, give, take, packed, from_x, from_y, diag_x, diag_y, send, recv, local = refs
    z, p, core, one, two, _ = places()
    rows, wide = outs[0].shape
    half = rows // 2
    x, y, twin = (z, one, core), (z, two, core), (z, p, 1 - core)
    firsts = [sum(sizes[:j]) for j in range(len(sizes))]
    steps = [(j, k) for j in range(len(sizes)) for k in (3, 1, 2, 0)]
    mine = pl.ds(pl.multiple_of(core * wide, wide), wide)
    other = pl.ds(pl.multiple_of((1 - core) * wide, wide), wide)
    loads, copies = {}, {}

    def load(name, i, src, dst):
        loads[name] = pltpu.make_async_copy(src, dst, local.at[i])
        loads[name].start()

    def load_left(t):
        j, k = steps[t]
        for i in range(sizes[j]):
            load(
                ("l", t, i),
                2 * pairs + t * max(sizes) + i,
                ins[2 * (firsts[j] + i)].at[pl.ds(k * rows, rows)],
                left.at[t % 2, i],
            )

    def load_right(kind, j, where, buffers):
        for i in range(firsts[j], firsts[j] + sizes[j]):
            load((kind, i), i + (pairs if kind == "m" else 0), ins[2 * i + 1].at[where], buffers[i])

    load_right("o", 0, other, others)
    load_left(0)
    load_right("m", 0, mine, mines)
    load_left(1)
    for j in range(1, len(sizes)):
        load_right("o", j, other, others)
        load_right("m", j, mine, mines)
    meet([x, y, twin])

    def go(name, j, i, src, dst, partner):
        copies[name, j] = to(src, dst, send.at[j, i], recv.at[j, i], partner)
        copies[name, j].start()

    def product(t, rights, store):
        j, _ = steps[t]

        def step(i, carry):
            at = pl.ds(pl.multiple_of(i * TILE, TILE), TILE)
            value = mat_nt(left[t % 2, 0], rights[firsts[j]][at, :])
            for n in range(1, sizes[j]):
                value = value + mat_nt(left[t % 2, n], rights[firsts[j] + n][at, :])
            store(at, value)
            return carry

        lax.fori_loop(0, wide // TILE, step, 0)

    def slot(t):
        j, k = steps[t]
        return t % 2 if k else 2 + j

    def away(t):
        j, k = steps[t]
        if t >= 2:
            copies[("t", steps[t - 2][1]), steps[t - 2][0]].wait_send()

        def store(at, value):
            give[t % 2, :, at] = value.astype(BF)

        product(t, others, store)
        go(("t", k), j, k, give.at[t % 2], take.at[j, k], twin)

    def here(t):
        def store(at, value):
            total[slot(t), :, at] = value

        product(t, mines, store)

    low, high = pl.ds(0, half), pl.ds(half, half)

    def term(t, at):
        j, k = steps[t]
        return total[slot(t), at, :] + take[j, k, at, :].astype(F32)

    def finish(t):
        j, k = steps[t]
        copies[("t", k), j].wait_recv()
        if k == 3:
            packed[j, 0] = term(t, pl.ds(0, rows)).astype(BF)
            go("3a", j, 4, packed.at[j, 0, low], diag_y.at[j], y)
            go("3b", j, 5, packed.at[j, 0, high], diag_x.at[j], x)
        elif k == 1:
            packed[j, 1, high, :] = term(t, high).astype(BF)
            go("1b", j, 6, packed.at[j, 1, high], from_x.at[j, high], x)
            value = term(t, low)
            packed[j, 1, low, :] = value.astype(BF)
        elif k == 2:
            packed[j, 2, low, :] = term(t, low).astype(BF)
            go("2a", j, 8, packed.at[j, 2, low], from_y.at[j, low], y)
            packed[j, 2, high, :] = term(t, high).astype(BF)

    def relay_x(j):
        copies["3a", j].wait_recv()
        packed[j, 1, low, :] = (packed[j, 1, low, :].astype(F32) + diag_y[j].astype(F32)).astype(BF)
        go("1a", j, 7, packed.at[j, 1, low], from_x.at[j, low], x)

    def relay_y(j):
        copies["3b", j].wait_recv()
        packed[j, 2, high, :] = (packed[j, 2, high, :].astype(F32) + diag_x[j].astype(F32)).astype(BF)
        go("2b", j, 9, packed.at[j, 2, high], from_y.at[j, high], y)

    def wait(kind, j):
        for i in range(firsts[j], firsts[j] + sizes[j]):
            loads[kind, i].wait()

    for t, (j, k) in enumerate(steps):
        for i in range(sizes[j]):
            loads["l", t, i].wait()
        if k == 3:
            wait("o", j)
        away(t)
        if k == 3:
            wait("m", j)
        if k in (1, 2, 0):
            finish(t - 1)
        if k == 0:
            relay_x(j)
        if k == 3 and j:
            relay_y(j - 1)
        here(t)
        if t + 2 < len(steps):
            load_left(t + 2)
    relay_y(len(sizes) - 1)
    for j in range(len(sizes)):
        copies[("t", 0), j].wait_recv()
        for name in ("1a", "1b", "2a", "2b"):
            copies[name, j].wait_recv()
        outs[j][...] = (
            term(4 * j + 3, pl.ds(0, rows)) + from_x[j].astype(F32) + from_y[j].astype(F32)
        )
    waited = {(("t", steps[t][1]), steps[t][0]) for t in range(len(steps) - 2)}
    for name, copy in copies.items():
        if name not in waited:
            copy.wait_send()


def sum_rows(sums, ident):
    sizes = tuple(len(pairs) for pairs in sums)
    flat = [v for pairs in sums for pair in pairs for v in pair]
    rows = flat[0].shape[0] // GROUP
    units = flat[0].shape[1]
    wide = flat[1].shape[0] // 2
    n, m = sum(sizes), len(sizes)
    return pl.pallas_call(
        functools.partial(sum_rows_kernel, sizes),
        out_shape=[jax.ShapeDtypeStruct((rows, wide), F32)] * m,
        in_specs=[ANY] * (2 * n),
        out_specs=[WHOLE] * m,
        scratch_shapes=[pltpu.VMEM((wide, units), BF)] * (2 * n)
        + [
            pltpu.VMEM((2, max(sizes), rows, units), BF),
            pltpu.VMEM((2 + m, rows, wide), F32),
            pltpu.VMEM((2, rows, wide), BF),
            pltpu.VMEM((m, GROUP, rows, wide), BF),
            pltpu.VMEM((m, 3, rows, wide), BF),
            pltpu.VMEM((m, rows, wide), BF),
            pltpu.VMEM((m, rows, wide), BF),
            pltpu.VMEM((m, rows // 2, wide), BF),
            pltpu.VMEM((m, rows // 2, wide), BF),
            pltpu.SemaphoreType.DMA((m, 10)),
            pltpu.SemaphoreType.DMA((m, 10)),
            pltpu.SemaphoreType.DMA((2 * n + 4 * m * max(sizes),)),
        ],
        compiler_params=pltpu.CompilerParams(
            collective_id=ident, has_side_effects=True, vmem_limit_bytes=58 << 20
        ),
        name="sum_rows",
    )(*flat)


WIDTH = 512


def deal_kernel(sent, pieces, gains, tokens, cots, units, all_gains, held, send, recv, ends, local):
    z, p, core, one, two, three = places()
    count, per, both = sent.shape
    wide = both // 2
    me = z * GROUP + p
    cols = pl.ds(pl.multiple_of(core * wide, wide), wide)
    twin = (z, p, 1 - core)

    def partner(s):
        t = lax.rem(me + s, count)
        return t, (t // GROUP, lax.rem(t, GROUP), core)

    barrier = pltpu.get_barrier_semaphore()

    def greet(s, carry):
        pl.semaphore_signal(barrier, inc=1, device_id=partner(s)[1], device_id_type=MESH)
        return carry

    lax.fori_loop(1, count, greet, 0)
    pl.semaphore_signal(barrier, inc=1, device_id=twin, device_id_type=MESH)
    mine = pltpu.make_async_copy(pieces.at[p], held, local.at[0])
    mine.start()
    keep = [
        pltpu.make_async_copy(sent.at[me, :, pl.ds(0, wide)], tokens.at[me, :, cols], local.at[1]),
        pltpu.make_async_copy(sent.at[me, :, pl.ds(wide, wide)], cots.at[me], local.at[2]),
        pltpu.make_async_copy(gains, all_gains.at[me], local.at[3]),
    ]
    for copy in keep:
        copy.start()
    pl.semaphore_wait(barrier, count)

    def rows(s):
        t, who = partner(s)
        return (
            to(sent.at[t, :, pl.ds(0, wide)], tokens.at[me, :, cols], send.at[0, s], recv.at[0, s], who),
            to(sent.at[t, :, pl.ds(wide, wide)], cots.at[me], send.at[1, s], recv.at[1, s], who),
            to(gains, all_gains.at[me], send.at[2, s], recv.at[2, s], who),
        )

    def start(i):
        def step(s, carry):
            rows(s)[i].start()
            return carry

        lax.fori_loop(1, count, step, 0)

    start(0)
    start(2)
    shares = [
        to(pieces.at[q], units.at[:, p], ends.at[0, k], ends.at[1, k], (z, q, core))
        for k, q in ((1, one), (2, two), (3, three))
    ]
    for copy in shares:
        copy.start()
    start(1)
    mine.wait()
    store = pltpu.make_async_copy(held, units.at[:, p], local.at[4])
    store.start()
    keep[0].wait()

    def arrived(i):
        def step(s, carry):
            rows(s)[i].wait_recv()
            return carry

        lax.fori_loop(1, count, step, 0)

    arrived(0)
    pass_on = to(tokens.at[:, :, cols], tokens.at[:, :, cols], ends.at[0, 0], ends.at[1, 0], twin)
    pass_on.start()
    arrived(2)
    for copy in shares:
        copy.wait_recv()
    arrived(1)
    pass_on.wait_recv()

    def leave(s, carry):
        for copy in rows(s):
            copy.wait_send()
        return carry

    lax.fori_loop(1, count, leave, 0)
    for copy in [*shares, pass_on]:
        copy.wait_send()
    keep[1].wait()
    keep[2].wait()
    store.wait()


def deal(sent, pieces, gains, ident):
    count, per, both = sent.shape
    _, three, rows, units = pieces.shape
    return pl.pallas_call(
        deal_kernel,
        out_shape=[
            jax.ShapeDtypeStruct((count, per, both), BF),
            jax.ShapeDtypeStruct((count, per, both // 2), BF),
            jax.ShapeDtypeStruct((three, GROUP, rows, units), BF),
            jax.ShapeDtypeStruct((count, *gains.shape), F32),
        ],
        in_specs=[WHOLE, ANY, WHOLE],
        out_specs=[ANY] * 4,
        scratch_shapes=[
            pltpu.VMEM((three, rows, units), BF),
            pltpu.SemaphoreType.DMA((3, count)),
            pltpu.SemaphoreType.DMA((3, count)),
            pltpu.SemaphoreType.DMA((2, 4)),
            pltpu.SemaphoreType.DMA((5,)),
        ],
        compiler_params=pltpu.CompilerParams(collective_id=ident, has_side_effects=True),
        name="deal",
    )(sent, pieces, gains)


STRIP = 16


def attend_back_kernel(
    dh2_half, middle, cot, w_out, w_qkv, mixed, q_rot, k_rot, value, prob, tokens, half_result,
    scale1, scale2, gain_a, gain_f, cosine, sine, into,
    new_qkv, new_out, new_gain, back,
    dh2, mid, low_mid, xs, hidden, w_part, g, mix, d_mix, qs, ks, vs, pb, gq, got_part,
    from_x, from_y, diag_x, diag_y, own, line, slots, half_rows, gain_terms, gain_got,
    send, recv, loads, row_send, row_recv, ends, keeps,
):
    z, p, core, one, two, three = places()
    chunks, depth, _, each, _ = g.shape
    rows, width = mid.shape
    wide = width // 2
    query_cols, key_cols = qs.shape[1], ks.shape[1]
    outs = query_cols // WIDTH
    count, per, _ = slots.shape[1:]
    me = z * GROUP + p
    half = depth // 2
    low, high = pl.ds(0, half), pl.ds(half, half)
    x, y, twin = (z, one, core), (z, two, core), (z, p, 1 - core)
    column = [(lax.rem(z + s, depth), p, core) for s in range(1, depth)]
    columns = pl.ds(pl.multiple_of(core * wide, wide), wide)
    root = HEAD_SIZE ** (-0.5)
    pending = {}

    def load(name, i, src, dst):
        pending[name] = pltpu.make_async_copy(src, dst, loads.at[i])
        pending[name].start()

    load("half", 0, half_result, half_rows)
    load("dh2", 1, dh2_half, dh2.at[:, columns])
    load("mid", 2, middle, mid)
    load("cot", 3, cot, low_mid)
    load("x", 4, tokens, xs)
    load("mix", 5, mixed, mix)
    for i in range(outs):
        load(("out", i), 6 + i, w_out.at[:, :, :, pl.ds(i * WIDTH, WIDTH)], g.at[chunks - outs + i])
    at = 6 + outs
    load("q", at, q_rot, qs)
    load("k", at + 1, k_rot, ks)
    load("v", at + 2, value, vs)
    load(("p", 0), at + 3, prob.at[0], pb.at[0])
    load(("p", 1), at + 4, prob.at[1], pb.at[1])
    block = w_part.shape[1]

    def load_part(i):
        load(("w", i), at + 5 + i % 2, w_qkv.at[pl.ds(i * block, block)], w_part.at[i % 2])

    load_part(0)
    load_part(1)

    def partner(s):
        t = lax.rem(me + s, count)
        return t, (t // GROUP, lax.rem(t, GROUP), core)

    barrier = pltpu.get_barrier_semaphore()

    def greet(s, carry):
        pl.semaphore_signal(barrier, inc=1, device_id=partner(s)[1], device_id_type=MESH)
        return carry

    lax.fori_loop(1, count, greet, 0)
    pl.semaphore_signal(barrier, inc=1, device_id=twin, device_id_type=MESH)
    pl.semaphore_wait(barrier, count)
    copies = {}

    def go(name, c, i, src, dst, who):
        copies[name, c] = to(src, dst, send.at[c, i], recv.at[c, i], who)
        copies[name, c].start()

    def row(i, s):
        t, who = partner(s)
        if i < 2:
            return to(slots.at[i, t], back.at[i, me, :, columns], row_send.at[i, s], row_recv.at[i, s], who)
        return to(gain_terms.at[t], gain_got.at[me], row_send.at[2, s], row_recv.at[2, s], who)

    def each_row(kinds, act):
        def step(s, carry):
            for i in kinds:
                act(row(i, s))
            return carry

        lax.fori_loop(1, count, step, 0)

    kept = []

    def give_rows(i):
        slots[i] = mat_tn(into[...], half_rows[...]).reshape(count, per, wide).astype(BF)
        kept.append(pltpu.make_async_copy(slots.at[i, me], back.at[i, me, :, columns], keeps.at[i]))
        kept[-1].start()
        each_row((i,), lambda copy: copy.start())

    def first(c):
        go("3a", c, 0, g.at[c, low, three], diag_y.at[c], y)
        go("3b", c, 1, g.at[c, high, three], diag_x.at[c], x)
        go("1b", c, 2, g.at[c, high, one], from_x.at[c, high], x)
        go("2a", c, 3, g.at[c, low, two], from_y.at[c, low], y)

    def relay(c):
        copies["3a", c].wait_recv()
        for j in range(half):
            diag_y[c, j] = (g[c, j, one].astype(F32) + diag_y[c, j].astype(F32)).astype(BF)
        go("1a", c, 4, diag_y.at[c], from_x.at[c, low], x)
        copies["3b", c].wait_recv()
        for j in range(half):
            diag_x[c, j] = (g[c, half + j, two].astype(F32) + diag_x[c, j].astype(F32)).astype(BF)
        go("2b", c, 5, diag_x.at[c], from_y.at[c, high], y)

    def along(c):
        for name in ("1a", "1b", "2a", "2b"):
            copies[name, c].wait_recv()
        own[c] = g[c, z, p].astype(F32) + from_x[c, z].astype(F32) + from_y[c, z].astype(F32)
        for j in range(depth):
            from_x[c, j] = (
                g[c, j, p].astype(F32) + from_x[c, j].astype(F32) + from_y[c, j].astype(F32)
            ).astype(BF)
        for s, who in enumerate(column, 1):
            go(s, c, 5 + s, from_x.at[c, who[0]], line.at[c, s - 1], who)

    def terms(c, left, right):
        span = GROUP * each
        for j in range(depth):
            part = mat_tn(left[:, j * span : (j + 1) * span], right)
            g[c, j] = part.reshape(GROUP, each, WIDTH).astype(BF)
        first(c)

    pending["dh2"].wait()
    swap = to(dh2.at[:, columns], dh2.at[:, columns], ends.at[0, 0], ends.at[1, 0], twin)
    swap.start()
    pending["half"].wait()
    give_rows(0)
    for name in ("mid", "cot", "x"):
        pending[name].wait()
    swap.wait_recv()

    def norm_2(i, total):
        strip = pl.ds(pl.multiple_of(i * STRIP, STRIP), STRIP)
        r2 = scale2[strip, :]
        n2 = mid[strip, :] * r2
        d = dh2[strip, :]
        s = d * gain_f[...]
        mean = jnp.sum(s * n2, axis=1, keepdims=True) * (1.0 / width)
        dm = low_mid[strip, :].astype(F32) + r2 * (s - n2 * mean)
        mid[strip, :] = dm
        low_mid[strip, :] = dm.astype(BF)
        hidden[strip, :] = (xs[strip, :].astype(F32) * scale1[strip, :] * gain_a[...]).astype(BF)
        return total + jnp.sum(d * n2, axis=0, keepdims=True)

    grad_gf = lax.fori_loop(0, rows // STRIP, norm_2, jnp.zeros((1, width), F32))
    pending["mix"].wait()
    for i in range(outs):
        pending["out", i].wait()
        d_mix[:, i * WIDTH : (i + 1) * WIDTH] = mat_nn(
            low_mid[...], g[chunks - outs + i].reshape(width, WIDTH)
        ).astype(BF)
    for i in range(outs):
        terms(i, low_mid, mix[:, i * WIDTH : (i + 1) * WIDTH])
    swap.wait_send()

    def turned_back(grad):
        a, b = grad[:, : HEAD_SIZE // 2], grad[:, HEAD_SIZE // 2 :]
        c, s = cosine[...], sine[...]
        return jnp.concatenate([a * c + b * s, b * c - a * s], axis=1).astype(BF)

    for name in ("q", "k", "v"):
        pending[name].wait()
    heads, kv_heads = query_cols // HEAD_SIZE, key_cols // HEAD_SIZE
    each_kv = heads // kv_heads
    for h in range(kv_heads):
        kk, vv = ks[:, h * HEAD_SIZE : (h + 1) * HEAD_SIZE], vs[:, h * HEAD_SIZE : (h + 1) * HEAD_SIZE]
        dk = dv = None
        for j in range(h * each_kv, (h + 1) * each_kv):
            cols = slice(j * HEAD_SIZE, (j + 1) * HEAD_SIZE)
            pending["p", j].wait()
            pr = pb[j % 2]
            do = d_mix[:, cols]
            dp = mat_nt(do, vv)
            delta = jnp.sum(pr * dp, axis=1, keepdims=True)
            ds = (pr * (dp - delta)).astype(BF)
            gq[:, cols] = turned_back(mat_nn(ds, kk) * root)
            more_k, more_v = mat_tn(ds, qs[:, cols]), mat_tn(pr.astype(BF), do)
            dk, dv = (more_k, more_v) if dk is None else (dk + more_k, dv + more_v)
            if j + 2 < heads:
                load(("p", j + 2), at + 3 + j % 2, prob.at[j + 2], pb.at[j % 2])
        base = query_cols + h * HEAD_SIZE
        gq[:, base : base + HEAD_SIZE] = turned_back(dk * root)
        base += key_cols
        gq[:, base : base + HEAD_SIZE] = dv.astype(BF)
        done = (h + 1) * each_kv * HEAD_SIZE // WIDTH
        for i in range(h * each_kv * HEAD_SIZE // WIDTH, done):
            terms(outs + i, hidden, gq[:, i * WIDTH : (i + 1) * WIDTH])
        if h < outs:
            relay(h)
    for i in range(kv_heads, outs):
        relay(i)
    for i in range(done, gq.shape[1] // WIDTH):
        terms(outs + i, hidden, gq[:, i * WIDTH : (i + 1) * WIDTH])
    for i in range(width // block):
        pending["w", i].wait()
        part = mat_nt(gq[...], w_part[i % 2])
        dh2[:, i * block : (i + 1) * block] = part
        low_mid[:, i * block : (i + 1) * block] = part.astype(BF)
        if i + 2 < width // block:
            load_part(i + 2)
    pass_part = to(low_mid, got_part, ends.at[0, 1], ends.at[1, 1], twin)
    pass_part.start()
    for c in range(outs):
        along(c)
    relay(outs)
    each_row((0,), lambda copy: copy.wait_send())
    pass_part.wait_recv()

    def norm_1(i, total):
        strip = pl.ds(pl.multiple_of(i * STRIP, STRIP), STRIP)
        r1 = scale1[strip, :]
        n1 = xs[strip, :].astype(F32) * r1
        d = dh2[strip, :] + got_part[strip, :].astype(F32)
        s = d * gain_a[...]
        mean = jnp.sum(s * n1, axis=1, keepdims=True) * (1.0 / width)
        dx = mid[strip, :] + r1 * (s - n1 * mean)
        half_rows[strip, :] = jnp.where(core == 0, dx[:, :wide], dx[:, wide:]).astype(BF)
        return total + jnp.sum(d * n1, axis=0, keepdims=True)

    grad_ga = lax.fori_loop(0, rows // STRIP, norm_1, jnp.zeros((1, width), F32))
    give_rows(1)
    for t in range(count):
        gain_terms[t, 0:1, :] = grad_ga[:, t * each : (t + 1) * each]
        gain_terms[t, 1:2, :] = grad_gf[:, t * each : (t + 1) * each]
        gain_terms[t, 2:8, :] = jnp.zeros((6, each), F32)
    kept.append(pltpu.make_async_copy(gain_terms.at[me], gain_got.at[me], keeps.at[2]))
    kept[-1].start()
    each_row((2,), lambda copy: copy.start())
    for c in range(outs + 1, chunks):
        relay(c)
        along(c - 1)
    for copy in kept:
        copy.wait()
    each_row((0, 1, 2), lambda copy: copy.wait_recv())
    pass_on = to(
        back.at[:, :, :, columns], back.at[:, :, :, columns], ends.at[0, 2], ends.at[1, 2], twin
    )
    pass_on.start()
    along(chunks - 1)
    gain = gain_got[0]
    for t in range(1, count):
        gain = gain + gain_got[t]
    new_gain[...] = gain
    for c in range(chunks):
        total = own[c]
        for s in range(1, depth):
            copies[s, c].wait_recv()
            total = total + line[c, s - 1].astype(F32)
        if c < outs:
            new_out[:, c * WIDTH : (c + 1) * WIDTH] = total
        else:
            new_qkv[:, (c - outs) * WIDTH : (c - outs + 1) * WIDTH] = total
    pass_on.wait_recv()
    for copy in copies.values():
        copy.wait_send()
    each_row((1, 2), lambda copy: copy.wait_send())
    pass_part.wait_send()
    pass_on.wait_send()


def attend_back(
    dh2_half, middle, cot, w_out, w_qkv, mixed, q_rot, k_rot, value, prob, tokens, half_result,
    scale1, scale2, gain_a, gain_f, cosine, sine, into, ident,
):
    depth = lax.axis_size("line")
    count = depth * GROUP
    rows, width = middle.shape
    wide = width // 2
    each = width // count
    query_cols, key_cols = q_rot.shape[1], k_rot.shape[1]
    cols = query_cols + 2 * key_cols
    chunks = (query_cols + cols) // WIDTH
    block = min(512, width)

    def vmem(*shape, dtype=BF):
        return pltpu.VMEM(shape, dtype)

    return pl.pallas_call(
        attend_back_kernel,
        out_shape=[
            jax.ShapeDtypeStruct((each, cols), F32),
            jax.ShapeDtypeStruct((each, query_cols), F32),
            jax.ShapeDtypeStruct((8, each), F32),
            jax.ShapeDtypeStruct((2, count, rows // count, width), BF),
        ],
        in_specs=[ANY] * 12 + [WHOLE] * 7,
        out_specs=[WHOLE] * 3 + [ANY],
        scratch_shapes=[
            vmem(rows, width, dtype=F32),
            vmem(rows, width, dtype=F32),
            vmem(rows, width),
            vmem(rows, width),
            vmem(rows, width),
            vmem(2, block, cols),
            vmem(chunks, depth, GROUP, each, WIDTH),
            vmem(rows, query_cols),
            vmem(rows, query_cols),
            vmem(rows, query_cols),
            vmem(rows, key_cols),
            vmem(rows, key_cols),
            vmem(2, rows, rows, dtype=F32),
            vmem(rows, cols),
            vmem(rows, width),
            vmem(chunks, depth, each, WIDTH),
            vmem(chunks, depth, each, WIDTH),
            vmem(chunks, depth // 2, each, WIDTH),
            vmem(chunks, depth // 2, each, WIDTH),
            vmem(chunks, each, WIDTH, dtype=F32),
            vmem(chunks, depth - 1, each, WIDTH),
            vmem(2, count, rows // count, wide),
            vmem(rows, wide),
            vmem(count, 8, each, dtype=F32),
            vmem(count, 8, each, dtype=F32),
            pltpu.SemaphoreType.DMA((chunks, 5 + depth)),
            pltpu.SemaphoreType.DMA((chunks, 5 + depth)),
            pltpu.SemaphoreType.DMA((16,)),
            pltpu.SemaphoreType.DMA((3, count)),
            pltpu.SemaphoreType.DMA((3, count)),
            pltpu.SemaphoreType.DMA((2, 3)),
            pltpu.SemaphoreType.DMA((3,)),
        ],
        compiler_params=pltpu.CompilerParams(
            collective_id=ident, has_side_effects=True, vmem_limit_bytes=62 << 20
        ),
        name="attend_back",
    )(
        dh2_half, middle, cot, w_out.reshape(depth, GROUP, each, query_cols), w_qkv, mixed, q_rot, k_rot, value,
        prob, tokens, half_result, scale1, scale2, gain_a, gain_f, cosine, sine, into,
    )


def settle_kernel(
    sum_0, sum_1, sum_d, grad_qkv, grad_out, grad_gain, norm, new_ffn, new_down, new_out,
    ffn, shares, store, unit_send, unit_recv, unit_local, all_send, all_recv,
):
    z, p, core, one, two, three = places()
    count = shares.shape[0] // 2
    me = z * GROUP + p
    each, units = ffn.shape[1], sum_d.shape[1]
    span = units // 2

    def anyone(s):
        t = lax.rem(me * 2 + core + s, 2 * count)
        return (t // (2 * GROUP), lax.rem(t // 2, GROUP), lax.rem(t, 2))

    barrier = pltpu.get_barrier_semaphore()

    def greet(s, carry):
        pl.semaphore_signal(barrier, inc=1, device_id=anyone(s), device_id_type=MESH)
        return carry

    lax.fori_loop(1, 2 * count, greet, 0)

    def unit_parts(q, of):
        rows = pl.ds(pl.multiple_of(q * each, each), each)

        def place(i, shift, size):
            return ffn.at[i, :, pl.ds(pl.multiple_of(of * units + shift, span), size)]

        return [
            (sum_d.at[rows], place(2, 0, units)),
            (sum_0.at[rows, pl.ds(0, span)], place(0, 0, span)),
            (sum_0.at[rows, pl.ds(span, span)], place(1, 0, span)),
            (sum_1.at[rows, pl.ds(0, span)], place(0, span, span)),
            (sum_1.at[rows, pl.ds(span, span)], place(1, span, span)),
        ]

    stay = [
        pltpu.make_async_copy(src, dst, unit_local.at[i])
        for i, (src, dst) in enumerate(unit_parts(p, p))
    ]
    for copy in stay:
        copy.start()
    pl.semaphore_wait(barrier, 2 * count - 1)
    shared = []
    for i in range(5):
        for k, q in ((3, three), (1, one), (2, two)):
            src, dst = unit_parts(q, p)[i]
            copy = to(src, dst, unit_send.at[k, i], unit_recv.at[k, i], (z, q, core))
            copy.start()
            shared.append(copy)

    def squares(value):
        return jnp.sum(jnp.sum(value * value, axis=0, keepdims=True), axis=1, keepdims=True)

    gain = grad_gain[...]
    total = 0.5 * squares(gain[:2])
    for at in range(0, grad_qkv.shape[1], WIDTH):
        total = total + squares(grad_qkv[:, at : at + WIDTH])
    for at in range(0, grad_out.shape[1], 128):
        value = grad_out[:, at : at + 128]
        total = total + squares(value)
        new_out[at : at + 128, :] = value.T
    for copy in stay:
        copy.wait()
    for copy in shared[:3]:
        copy.wait_recv()
    for at in range(0, new_down.shape[0], 128):
        value = ffn[2, :, at : at + 128].astype(F32)
        total = total + squares(value)
        new_down[at : at + 128, :] = value.T
    for copy in shared[3:]:
        copy.wait_recv()
    keep = pltpu.make_async_copy(ffn.at[pl.ds(0, 2)], new_ffn, store)
    keep.start()
    for i in range(2):
        for at in range(0, GROUP * units, WIDTH):
            total = total + squares(ffn[i, :, at : at + WIDTH].astype(F32))
    shares[0] = jnp.broadcast_to(total, (8, 128))

    def tell(s):
        return to(shares.at[0], shares.at[s], all_send.at[s], all_recv.at[s], anyone(s))

    def tell_start(s, carry):
        tell(s).start()
        return carry

    def tell_end(s, carry):
        tell(s).wait_recv()
        return carry

    def tell_left(s, carry):
        tell(s).wait_send()
        return carry

    lax.fori_loop(1, 2 * count, tell_start, 0)
    lax.fori_loop(1, 2 * count, tell_end, 0)
    norm[...] = jnp.sqrt(jnp.sum(shares[...], axis=0))
    lax.fori_loop(1, 2 * count, tell_left, 0)
    for copy in shared:
        copy.wait_send()
    keep.wait()


def settle(sum_0, sum_1, sum_d, grad_qkv, grad_out, grad_gain, ident):
    count = lax.axis_size("line") * GROUP
    each, units = grad_qkv.shape[0], sum_d.shape[1]
    return pl.pallas_call(
        settle_kernel,
        out_shape=[
            jax.ShapeDtypeStruct((8, 128), F32),
            jax.ShapeDtypeStruct((2, each, GROUP * units), BF),
            jax.ShapeDtypeStruct((GROUP * units, each), F32),
            jax.ShapeDtypeStruct(grad_out.shape[::-1], F32),
        ],
        in_specs=[ANY] * 3 + [WHOLE] * 3,
        out_specs=[WHOLE, ANY, WHOLE, WHOLE],
        scratch_shapes=[
            pltpu.VMEM((3, each, GROUP * units), BF),
            pltpu.VMEM((2 * count, 8, 128), F32),
            pltpu.SemaphoreType.DMA,
            pltpu.SemaphoreType.DMA((4, 5)),
            pltpu.SemaphoreType.DMA((4, 5)),
            pltpu.SemaphoreType.DMA((5,)),
            pltpu.SemaphoreType.DMA((2 * count,)),
            pltpu.SemaphoreType.DMA((2 * count,)),
        ],
        compiler_params=pltpu.CompilerParams(
            collective_id=ident, has_side_effects=True, vmem_limit_bytes=24 << 20
        ),
        name="settle",
    )(sum_0, sum_1, sum_d, grad_qkv, grad_out, grad_gain)


def update_kernel(limit, norm, gain, qkv, ffn, down, out, *refs):
    weights, moments, new_moments, new_weights = refs[:9], refs[9:18], refs[18:27], refs[27:36]
    w_buf, m_buf = refs[36:45], refs[45:54]
    qkv_buf, ffn_buf, down_buf, out_buf, loads, stores, grads = refs[54:]
    sources = {
        6: pltpu.make_async_copy(ffn, ffn_buf, grads.at[0]),
        8: pltpu.make_async_copy(down, down_buf, grads.at[1]),
        1: pltpu.make_async_copy(qkv, qkv_buf, grads.at[2]),
        4: pltpu.make_async_copy(out, out_buf, grads.at[3]),
    }
    order = (0, 5, 2, 3, 1, 4, 8, 6, 7)
    pending = {}
    for i in order:
        if i in sources and i != 1:
            sources[i].start()
        if i == 2:
            sources[1].start()
        pending[i] = [
            pltpu.make_async_copy(weights[i], w_buf[i], loads.at[0, i]),
            pltpu.make_async_copy(moments[i], m_buf[i], loads.at[1, i]),
        ]
        for copy in pending[i]:
            copy.start()
    factor = 0.5 * jnp.minimum(1.0, limit / norm[:1, :1])
    writes = []
    everything = slice(None)
    base = qkv_buf.shape[1] // 2

    def update(i, at, grad):
        m = 0.5 * m_buf[i][at] + factor * grad
        w = w_buf[i][at]
        m_buf[i][at] = m
        w_buf[i][at] = w - LEARN * (m + DECAY * w)

    for i in order:
        if i in sources and i != 1:
            sources[i].wait()
        if i == 2:
            sources[1].wait()
        for copy in pending[i]:
            copy.wait()
        if i in (0, 5):
            update(i, (everything, everything), gain[i // 5 : i // 5 + 1, :])
        elif i in (1, 2, 3):
            shift = 0 if i == 1 else base + (i - 2) * w_buf[2].shape[1]
            for at in range(0, w_buf[i].shape[1], WIDTH):
                update(i, (everything, slice(at, at + WIDTH)), qkv_buf[:, shift + at : shift + at + WIDTH])
        elif i in (6, 7):
            for at in range(0, w_buf[i].shape[1], WIDTH):
                cols = (everything, slice(at, at + WIDTH))
                update(i, cols, ffn_buf[(i - 6, *cols)].astype(F32))
        else:
            source = down_buf if i == 8 else out_buf
            for at in range(0, w_buf[i].shape[0], WIDTH):
                rows = (slice(at, at + WIDTH), everything)
                update(i, rows, source[rows])
        for buf, new, j in ((m_buf, new_moments, 0), (w_buf, new_weights, 1)):
            writes.append(pltpu.make_async_copy(buf[i], new[i], stores.at[j, i]))
            writes[-1].start()
    for copy in writes:
        copy.wait()


def update(norm, gain, qkv, ffn, down, out, weights, moments, limit):
    like = [jax.ShapeDtypeStruct(v.shape, F32) for v in weights]
    size = sum(v.size for v in weights)
    return pl.pallas_call(
        functools.partial(update_kernel, limit),
        out_shape=[*like, *like],
        in_specs=[WHOLE] * 2 + [ANY] * 22,
        out_specs=[ANY] * 18,
        scratch_shapes=[pltpu.VMEM(v.shape, F32) for v in (*weights, *moments)]
        + [pltpu.VMEM(v.shape, v.dtype) for v in (qkv, ffn, down, out)]
        + [
            pltpu.SemaphoreType.DMA((2, 9)),
            pltpu.SemaphoreType.DMA((2, 9)),
            pltpu.SemaphoreType.DMA((4,)),
        ],
        compiler_params=pltpu.CompilerParams(vmem_limit_bytes=40 << 20),
        cost_estimate=pl.CostEstimate(flops=7 * size, bytes_accessed=20 * size, transcendentals=0),
        name="update",
    )(norm, gain, qkv, ffn, down, out, *weights, *moments)


class Ways:
    def __init__(self):
        self.depth = lax.axis_size("line")
        self.n = self.depth * GROUP
        self.z = lax.axis_index("line")
        self.p = lax.axis_index("group")
        self.me = self.z * GROUP + self.p
        self.core = lax.axis_index("mp")

    def flip(self, value, k):
        return lax.ppermute(value, "group", [(i, i ^ k) for i in range(GROUP)])

    def swap(self, value):
        return lax.ppermute(value, "mp", [(0, 1), (1, 0)])

    def gather_line(self, value):
        return lax.all_gather(value, "line", axis=0, tiled=True)

    def scatter_line(self, whole):
        return lax.psum_scatter(whole, "line", scatter_dimension=0, tiled=True)

    def gather_group(self, value):
        half = value.shape[0] // 2
        one, two = self.flip(value, 1), self.flip(value, 2)
        three = jnp.concatenate([self.flip(one[:half], 2), self.flip(two[half:], 1)])
        return [value, one, two, three]

    def own_half(self, value):
        half = value.shape[-1] // 2
        return jnp.where(self.core == 0, value[..., :half], value[..., half:])

    def other_half(self, value):
        half = value.shape[-1] // 2
        return jnp.where(self.core == 0, value[..., half:], value[..., :half])

    def join(self, mine, other):
        return jnp.where(
            self.core == 0,
            jnp.concatenate([mine, other], axis=-1),
            jnp.concatenate([other, mine], axis=-1),
        )


def unit_pieces(down, gate, upper):
    units = down.shape[1] // GROUP
    half = units // 2

    def cut(j, c):
        at = slice(j * units + c * half, j * units + (c + 1) * half)
        return jnp.concatenate([gate[:, at], upper[:, at]], axis=1)

    return jnp.stack(
        [
            jnp.stack([down[:, j * units : (j + 1) * units], cut(j, 0), cut(j, 1)])
            for j in range(GROUP)
        ]
    )


def deal_tables(token_order, me, rows):
    blocks = token_order.shape[0] // rows
    per = rows // blocks
    index = jnp.arange(rows, dtype=jnp.int32)
    wanted = lax.dynamic_slice_in_dim(token_order, me * rows, rows)
    source = wanted // rows
    same = (source[:, None] == source[None, :]) & (index[None, :] < index[:, None])
    slot = source * per + jnp.sum(same.astype(jnp.int32), axis=1)
    into = (slot[:, None] == index[None, :]).astype(BF)
    table = token_order.reshape(blocks, rows)
    taken = table // rows == me
    earlier = (index[:, None] < index[None, :]).astype(BF)
    rank = mat_nn(taken.astype(BF), earlier).astype(jnp.int32)
    hit = taken[:, None, :] & (rank[:, None, :] == jnp.arange(per, dtype=jnp.int32)[None, :, None])
    sent = jnp.sum(jnp.where(hit, (table - me * rows)[:, None, :], 0), axis=2).reshape(rows)
    out = (sent[:, None] == index[None, :]).astype(BF)
    return into, out


def on_device(
    tokens,
    cotangent,
    lengths,
    seq_deal,
    token_order,
    gain_attn,
    w_query,
    key_weight,
    value_weight,
    w_out,
    gain_ffn,
    w_gate,
    w_up,
    w_down,
    moment_gain_attn,
    moment_w_query,
    key_weight_momentum,
    value_weight_momentum,
    moment_w_out,
    moment_gain_ffn,
    moment_w_gate,
    moment_w_up,
    moment_w_down,
):
    ways = Ways()
    rows, width = tokens.shape
    me = ways.me
    shard_qkv = jnp.concatenate(
        [w_query.astype(BF), key_weight.astype(BF), value_weight.astype(BF)], axis=1
    )
    shard_out = w_out.astype(BF).T
    line_all = ways.gather_line(jnp.concatenate([shard_qkv, shard_out], axis=1))
    line_qkv = line_all[:, : shard_qkv.shape[1]]
    line_out = line_all[:, shard_qkv.shape[1] :]

    into, out = deal_tables(token_order, me, rows)
    sent = mat_nn(
        out, jnp.concatenate([ways.own_half(tokens), ways.own_half(cotangent)], axis=1)
    ).astype(BF)
    pieces = unit_pieces(w_down.astype(BF).T, w_gate.astype(BF), w_up.astype(BF))
    gains = jnp.pad(
        jnp.stack([gain_attn, gain_ffn]).astype(BF).astype(F32), ((0, 6), (0, 0))
    )
    got_tokens, got_cot, units, all_gains = deal(
        sent.reshape(ways.n, rows // ways.n, width), pieces, gains, 5
    )
    gain_a = all_gains[:, 0].reshape(width)
    gain_f = all_gains[:, 1].reshape(width)
    dealt = mat_nn(into, got_tokens.reshape(rows, width)).astype(BF)
    half_cot = mat_nn(into, got_cot.reshape(rows, width // 2)).astype(BF)

    weight_qkv, weight_out = share_weights([line_qkv, line_out], 4)
    wide_q = w_query.shape[1]
    wide_k = key_weight.shape[1]
    query_w = weight_qkv[:, :wide_q]
    key_w = weight_qkv[:, wide_q : wide_q + wide_k]
    value_w = weight_qkv[:, wide_q + wide_k :]

    line_units = lax.all_gather(
        units.reshape(3, -1, units.shape[-1]), "line", axis=1, tiled=False
    )
    down_t, first_w, second_w = (line_units[i].reshape(width, -1) for i in range(3))

    cot_parts = jnp.concatenate(ways.gather_group(after(half_cot, weight_out)))
    group_cot = ways.join(cot_parts, ways.swap(cot_parts))
    dealt_cot = group_cot[:rows]

    seq_dev = seq_deal.shape[0] // ways.n
    mine = lax.dynamic_slice_in_dim(seq_deal, me * seq_dev, seq_dev)
    position, mask = layout(lengths[mine], rows)
    cosine, sine = angles(position, HEAD_SIZE)

    heads_q = query_w.shape[1] // HEAD_SIZE
    heads_kv = key_w.shape[1] // HEAD_SIZE
    head_group = heads_q // heads_kv
    root = HEAD_SIZE ** (-0.5)
    inputs = dealt.astype(F32)
    normed1, scale1 = normalize(inputs)
    hidden1 = (normed1 * gain_a).astype(BF)
    query = mat_nn(hidden1, query_w).reshape(rows, heads_q, HEAD_SIZE)
    key = mat_nn(hidden1, key_w).reshape(rows, heads_kv, HEAD_SIZE)
    value = mat_nn(hidden1, value_w).astype(BF).reshape(rows, heads_kv, HEAD_SIZE)
    query_rot = (
        apply_rotary(query, cosine, sine)
        .astype(BF)
        .reshape(rows, heads_kv, head_group, HEAD_SIZE)
    )
    key_rot = apply_rotary(key, cosine, sine).astype(BF)
    scores = jnp.einsum("rhgd,chd->hgrc", query_rot, key_rot, preferred_element_type=F32) * root
    scores = jnp.where(mask[None, None], scores, -1e30)
    top = jnp.max(scores, axis=-1, keepdims=True)
    expo = jnp.exp(scores - top)
    prob = expo / jnp.sum(expo, axis=-1, keepdims=True)
    prob_low = prob.astype(BF)
    mixed = (
        jnp.einsum("hgrc,chd->rhgd", prob_low, value, preferred_element_type=F32)
        .reshape(rows, heads_q * HEAD_SIZE)
        .astype(BF)
    )
    part = mat_nt(mixed, weight_out)
    middle = inputs + (part + ways.swap(part.astype(BF)).astype(F32))
    normed2, scale2 = normalize(middle)
    hidden2 = (normed2 * gain_f).astype(BF)

    group_h2 = share_rows(hidden2, 1)
    grad_inner = mat_nn(group_cot, down_t)
    span = grad_inner.shape[1] // 2

    def units_half(group_rows, weight, grad_inner):
        both = mat_nn(group_rows, weight)
        gate, upper = both[:, :span], both[:, span:]
        sigma = jax.nn.sigmoid(gate)
        activ = gate * sigma
        inner = (activ * upper).astype(BF)
        slope = sigma * (1.0 + gate * (1.0 - sigma))
        grads = jnp.concatenate([grad_inner * upper * slope, grad_inner * activ], axis=1)
        return inner, grads.astype(BF)

    inner_0, grads_0 = units_half(group_h2, first_w, grad_inner[:, :span])
    terms_0 = mat_tn(group_h2, grads_0).astype(BF)
    sum_0 = ways.scatter_line(terms_0)
    inner_1, grads_1 = units_half(after(group_h2, terms_0), second_w, grad_inner[:, span:])
    inner = jnp.concatenate([inner_0, inner_1], axis=1)
    terms_d = mat_tn(group_cot, inner).astype(BF)
    sum_d = ways.scatter_line(terms_d)
    half_dh2, half_ffn = sum_rows(
        [[(grads_0, first_w), (after(grads_1, terms_d), second_w)], [(inner, down_t)]], 2
    )
    terms_1 = mat_tn(after(group_h2, half_dh2), grads_1).astype(BF)
    sum_1 = ways.scatter_line(terms_1)
    half_dh2 = after(half_dh2, terms_1)
    half_result = (ways.own_half(middle) + half_ffn).astype(BF)
    dh2_first = half_dh2 + 0.0 * sum_0[0, 0].astype(F32)
    new_qkv, new_out, new_gain, back = attend_back(
        dh2_first,
        middle,
        dealt_cot,
        weight_out,
        weight_qkv,
        mixed,
        query_rot.reshape(rows, -1),
        key_rot.reshape(rows, -1),
        value.reshape(rows, -1),
        prob.reshape(heads_q, rows, rows),
        dealt,
        half_result,
        scale1,
        scale2,
        gain_a.reshape(1, width),
        gain_f.reshape(1, width),
        cosine[:, 0],
        sine[:, 0],
        into,
        6,
    )
    norm, new_ffn, new_down, new_out_t = settle(sum_0, sum_1, sum_d, new_qkv, new_out, new_gain, 7)
    activations = mat_tn(out, back[0].reshape(rows, width)).astype(BF)
    input_grad = mat_tn(out, back[1].reshape(rows, width)).astype(BF)
    weights = (gain_attn, w_query, key_weight, value_weight, w_out, gain_ffn, w_gate, w_up, w_down)
    moments = (
        moment_gain_attn,
        moment_w_query,
        key_weight_momentum,
        value_weight_momentum,
        moment_w_out,
        moment_gain_ffn,
        moment_w_gate,
        moment_w_up,
        moment_w_down,
    )
    flat = [v if v.ndim == 2 else v.reshape(1, -1) for v in (*weights, *moments)]
    new = update(
        norm, new_gain, new_qkv, new_ffn, new_down, new_out_t, flat[:9], flat[9:], math.sqrt(PARAMS)
    )
    new = [v.reshape(old.shape) for v, old in zip(new, (*weights, *weights))]
    return (activations, input_grad, norm[0, 0], *new)


def solution(mesh):
    count, cores = mesh.devices.shape
    regrouped = Mesh(
        mesh.devices.reshape(count // GROUP, GROUP, cores), ("line", "group", "mp")
    )
    dp = ("line", "group")
    gain, tall, wide, row = P(dp), P(dp, "mp"), P("mp", dp), P(dp, None)
    leaves = (gain, tall, tall, tall, wide, gain, tall, tall, wide)
    return jax.shard_map(
        on_device,
        mesh=regrouped,
        in_specs=(row, row, P(), P(), P(), *leaves, *leaves),
        out_specs=(row, row, P(), *leaves, *leaves),
        check_vma=False,
    )
```

```python
import functools
import math

import jax
import jax.numpy as jnp
from jax import lax
from jax.experimental import pallas as pl
from jax.experimental.pallas import tpu as pltpu
from jax.sharding import Mesh
from jax.sharding import PartitionSpec as P

HEAD_SIZE = 256
PARAMS = 62918656
EPS = 1e-06
THETA = 1000042.0
LEARN = 0.5
DECAY = 0.1
GROUP = 4
BF = jnp.bfloat16
F32 = jnp.float32


def angles(position, head):
    half = head // 2
    freq = THETA ** (-(2.0 * jnp.arange(half, dtype=F32)) / head)
    turned = position[:, None] * freq[None, :]
    return (jnp.cos(turned), jnp.sin(turned))


def layout(block_len, rows):
    rank = jnp.arange(block_len.shape[0], dtype=jnp.int32)
    ends = jnp.sum(jnp.where(rank[None, :] <= rank[:, None], block_len[None, :], 0), axis=1)
    starts = ends - block_len
    index = jnp.arange(rows, dtype=jnp.int32)
    inside = (index[:, None] >= starts[None, :]) & (index[:, None] < ends[None, :])
    segment = jnp.sum(jnp.where(inside, rank[None, :], 0), axis=1)
    position = jnp.sum(jnp.where(inside, index[:, None] - starts[None, :], 0), axis=1)
    return (position.astype(F32), segment.astype(jnp.int32))


def mat_nn(left, right):
    return jnp.dot(left, right, preferred_element_type=F32)


def mat_nt(left, right):
    return lax.dot_general(left, right, (((1,), (1,)), ((), ())), preferred_element_type=F32)


def mat_tn(left, right):
    return lax.dot_general(left, right, (((0,), (0,)), ((), ())), preferred_element_type=F32)


def after(value, *others):
    return lax.optimization_barrier((value, *others))[0]


MESH = pl.DeviceIdType.MESH
ANY = pl.BlockSpec(memory_space=pl.ANY)
WHOLE = pl.BlockSpec(memory_space=pltpu.VMEM)


def places():
    z, p, core = lax.axis_index("line"), lax.axis_index("group"), lax.axis_index("mp")
    one = p + 1 - 2 * lax.rem(p, 2)
    two = p + 2 - 4 * (p // 2)
    three = GROUP - 1 - p
    return z, p, core, one, two, three


def meet(partners):
    barrier = pltpu.get_barrier_semaphore()
    for partner in partners:
        pl.semaphore_signal(barrier, inc=1, device_id=partner, device_id_type=MESH)
    pl.semaphore_wait(barrier, len(partners))


def to(src, dst, send, recv, partner):
    return pltpu.make_async_remote_copy(
        src_ref=src, dst_ref=dst, send_sem=send, recv_sem=recv,
        device_id=partner, device_id_type=MESH,
    )


def share_weights_kernel(line, out, held, send, recv, local):
    z, p, core, one, two, _ = places()
    x, y = (z, one, core), (z, two, core)
    half = line.shape[0] // 2
    cols = pl.ds(0, out.shape[3])
    low, high = pl.ds(0, half), pl.ds(half, half)
    load = pltpu.make_async_copy(line.at[:, :, cols], held, local.at[0])
    load.start()
    meet([x, y])
    copies = []

    def go(src, dst, partner):
        i = len(copies)
        copies.append(to(src, dst, send.at[i], recv.at[i], partner))
        copies[i].start()

    go(line.at[low, :, cols], out.at[low, p], x)
    go(line.at[high, :, cols], out.at[high, p], y)
    go(line.at[high, :, cols], out.at[high, p], x)
    go(line.at[low, :, cols], out.at[low, p], y)
    load.wait()
    store = pltpu.make_async_copy(held, out.at[:, p], local.at[1])
    store.start()
    copies[0].wait_recv()
    go(out.at[low, one], out.at[low, one], y)
    copies[1].wait_recv()
    go(out.at[high, two], out.at[high, two], x)
    for i in range(2, 6):
        copies[i].wait_recv()
    for copy in copies:
        copy.wait_send()
    store.wait()


def share_weights(line, cols, ident):
    depth = lax.axis_size("line")
    each = line.shape[0] // depth
    out = pl.pallas_call(
        share_weights_kernel,
        out_shape=jax.ShapeDtypeStruct((depth, GROUP, each, cols), line.dtype),
        in_specs=[ANY],
        out_specs=ANY,
        scratch_shapes=[
            pltpu.VMEM((depth, each, cols), line.dtype),
            pltpu.SemaphoreType.DMA((6,)),
            pltpu.SemaphoreType.DMA((6,)),
            pltpu.SemaphoreType.DMA((2,)),
        ],
        compiler_params=pltpu.CompilerParams(collective_id=ident, has_side_effects=True),
        name="share_weights",
    )(line.reshape(depth, each, line.shape[1]))
    return out.reshape(depth * GROUP * each, cols)


TILE = 256


def sum_rows_kernel(sizes, *refs):
    pairs = sum(sizes)
    ins, outs = refs[: 2 * pairs], refs[2 * pairs : 2 * pairs + len(sizes)]
    refs = refs[2 * pairs + len(sizes) :]
    mines, others, refs = refs[:pairs], refs[pairs : 2 * pairs], refs[2 * pairs :]
    left, total, give, take, packed, from_x, from_y, diag_x, diag_y, send, recv, local = refs
    z, p, core, one, two, _ = places()
    rows, wide = outs[0].shape
    half = rows // 2
    x, y, twin = (z, one, core), (z, two, core), (z, p, 1 - core)
    firsts = [sum(sizes[:j]) for j in range(len(sizes))]
    steps = [(j, k) for j in range(len(sizes)) for k in (3, 1, 2, 0)]
    mine = pl.ds(pl.multiple_of(core * wide, wide), wide)
    other = pl.ds(pl.multiple_of((1 - core) * wide, wide), wide)
    loads, copies = {}, {}

    def load(name, i, src, dst):
        loads[name] = pltpu.make_async_copy(src, dst, local.at[i])
        loads[name].start()

    def load_left(t):
        j, k = steps[t]
        for i in range(sizes[j]):
            load(
                ("l", t, i),
                2 * pairs + t * max(sizes) + i,
                ins[2 * (firsts[j] + i)].at[pl.ds(k * rows, rows)],
                left.at[t % 2, i],
            )

    def load_right(kind, j, where, buffers):
        for i in range(firsts[j], firsts[j] + sizes[j]):
            load((kind, i), i + (pairs if kind == "m" else 0), ins[2 * i + 1].at[where], buffers[i])

    load_right("o", 0, other, others)
    load_left(0)
    load_right("m", 0, mine, mines)
    load_left(1)
    for j in range(1, len(sizes)):
        load_right("o", j, other, others)
        load_right("m", j, mine, mines)
    meet([x, y, twin])

    def go(name, j, i, src, dst, partner):
        copies[name, j] = to(src, dst, send.at[j, i], recv.at[j, i], partner)
        copies[name, j].start()

    def product(t, rights, store):
        j, _ = steps[t]

        def step(i, carry):
            at = pl.ds(pl.multiple_of(i * TILE, TILE), TILE)
            value = mat_nt(left[t % 2, 0], rights[firsts[j]][at, :])
            for n in range(1, sizes[j]):
                value = value + mat_nt(left[t % 2, n], rights[firsts[j] + n][at, :])
            store(at, value)
            return carry

        lax.fori_loop(0, wide // TILE, step, 0)

    def slot(t):
        j, k = steps[t]
        return t % 2 if k else 2 + j

    def away(t):
        j, k = steps[t]
        if t >= 2:
            copies[("t", steps[t - 2][1]), steps[t - 2][0]].wait_send()

        def store(at, value):
            give[t % 2, :, at] = value.astype(BF)

        product(t, others, store)
        go(("t", k), j, k, give.at[t % 2], take.at[j, k], twin)

    def here(t):
        def store(at, value):
            total[slot(t), :, at] = value

        product(t, mines, store)

    low, high = pl.ds(0, half), pl.ds(half, half)

    def term(t, at):
        j, k = steps[t]
        return total[slot(t), at, :] + take[j, k, at, :].astype(F32)

    def finish(t):
        j, k = steps[t]
        copies[("t", k), j].wait_recv()
        if k == 3:
            packed[j, 0] = term(t, pl.ds(0, rows)).astype(BF)
            go("3a", j, 4, packed.at[j, 0, low], diag_y.at[j], y)
            go("3b", j, 5, packed.at[j, 0, high], diag_x.at[j], x)
        elif k == 1:
            packed[j, 1, high, :] = term(t, high).astype(BF)
            go("1b", j, 6, packed.at[j, 1, high], from_x.at[j, high], x)
            value = term(t, low)
            packed[j, 1, low, :] = value.astype(BF)
        elif k == 2:
            packed[j, 2, low, :] = term(t, low).astype(BF)
            go("2a", j, 8, packed.at[j, 2, low], from_y.at[j, low], y)
            packed[j, 2, high, :] = term(t, high).astype(BF)

    def relay_x(j):
        copies["3a", j].wait_recv()
        packed[j, 1, low, :] = (packed[j, 1, low, :].astype(F32) + diag_y[j].astype(F32)).astype(BF)
        go("1a", j, 7, packed.at[j, 1, low], from_x.at[j, low], x)

    def relay_y(j):
        copies["3b", j].wait_recv()
        packed[j, 2, high, :] = (packed[j, 2, high, :].astype(F32) + diag_x[j].astype(F32)).astype(BF)
        go("2b", j, 9, packed.at[j, 2, high], from_y.at[j, high], y)

    def wait(kind, j):
        for i in range(firsts[j], firsts[j] + sizes[j]):
            loads[kind, i].wait()

    for t, (j, k) in enumerate(steps):
        for i in range(sizes[j]):
            loads["l", t, i].wait()
        if k == 3:
            wait("o", j)
        away(t)
        if k == 3:
            wait("m", j)
        if k in (1, 2, 0):
            finish(t - 1)
        if k == 0:
            relay_x(j)
        if k == 3 and j:
            relay_y(j - 1)
        here(t)
        if t + 2 < len(steps):
            load_left(t + 2)
    relay_y(len(sizes) - 1)
    for j in range(len(sizes)):
        copies[("t", 0), j].wait_recv()
        for name in ("1a", "1b", "2a", "2b"):
            copies[name, j].wait_recv()
        outs[j][...] = (
            term(4 * j + 3, pl.ds(0, rows)) + from_x[j].astype(F32) + from_y[j].astype(F32)
        )
    waited = {(("t", steps[t][1]), steps[t][0]) for t in range(len(steps) - 2)}
    for name, copy in copies.items():
        if name not in waited:
            copy.wait_send()


def sum_rows(sums, ident):
    sizes = tuple(len(pairs) for pairs in sums)
    flat = [v for pairs in sums for pair in pairs for v in pair]
    rows = flat[0].shape[0] // GROUP
    units = flat[0].shape[1]
    wide = flat[1].shape[0] // 2
    n, m = sum(sizes), len(sizes)
    return pl.pallas_call(
        functools.partial(sum_rows_kernel, sizes),
        out_shape=[jax.ShapeDtypeStruct((rows, wide), F32)] * m,
        in_specs=[ANY] * (2 * n),
        out_specs=[WHOLE] * m,
        scratch_shapes=[pltpu.VMEM((wide, units), BF)] * (2 * n)
        + [
            pltpu.VMEM((2, max(sizes), rows, units), BF),
            pltpu.VMEM((2 + m, rows, wide), F32),
            pltpu.VMEM((2, rows, wide), BF),
            pltpu.VMEM((m, GROUP, rows, wide), BF),
            pltpu.VMEM((m, 3, rows, wide), BF),
            pltpu.VMEM((m, rows, wide), BF),
            pltpu.VMEM((m, rows, wide), BF),
            pltpu.VMEM((m, rows // 2, wide), BF),
            pltpu.VMEM((m, rows // 2, wide), BF),
            pltpu.SemaphoreType.DMA((m, 10)),
            pltpu.SemaphoreType.DMA((m, 10)),
            pltpu.SemaphoreType.DMA((2 * n + 4 * m * max(sizes),)),
        ],
        compiler_params=pltpu.CompilerParams(
            collective_id=ident, has_side_effects=True, vmem_limit_bytes=58 << 20
        ),
        name="sum_rows",
    )(*flat)


WIDTH = 512


def deal_kernel(sent, pieces, gains, tokens, cots, units_0, units_1, all_gains, held, send, recv, ends, local):
    z, p, core, one, two, three = places()
    count, per, both = sent.shape
    wide = both // 2
    me = z * GROUP + p
    cols = pl.ds(pl.multiple_of(core * wide, wide), wide)
    twin = (z, p, 1 - core)

    def partner(s):
        t = lax.rem(me + s, count)
        return t, (t // GROUP, lax.rem(t, GROUP), core)

    barrier = pltpu.get_barrier_semaphore()

    def greet(s, carry):
        pl.semaphore_signal(barrier, inc=1, device_id=partner(s)[1], device_id_type=MESH)
        return carry

    lax.fori_loop(1, count, greet, 0)
    pl.semaphore_signal(barrier, inc=1, device_id=twin, device_id_type=MESH)
    mine = pltpu.make_async_copy(pieces.at[p], held, local.at[0])
    mine.start()
    keep = [
        pltpu.make_async_copy(sent.at[me, :, pl.ds(0, wide)], tokens.at[me, :, cols], local.at[1]),
        pltpu.make_async_copy(sent.at[me, :, pl.ds(wide, wide)], cots.at[me], local.at[2]),
        pltpu.make_async_copy(gains, all_gains.at[me], local.at[3]),
    ]
    for copy in keep:
        copy.start()
    pl.semaphore_wait(barrier, count)

    def row(i, s):
        t, who = partner(s)
        src = (sent.at[t, :, pl.ds(0, wide)], sent.at[t, :, pl.ds(wide, wide)], gains)[i]
        dst = (tokens.at[me, :, cols], cots.at[me], all_gains.at[me])[i]
        return to(src, dst, send.at[i, s], recv.at[i, s], who)

    def start(i):
        def step(s, carry):
            row(i, s).start()
            return carry

        lax.fori_loop(1, count, step, 0)

    start(0)
    start(2)
    units = (units_0.at[0], units_0.at[1], units_1)
    shares = [
        to(pieces.at[q, i], units[i].at[p], ends.at[0, k, i], ends.at[1, k, i], (z, q, core))
        for i in range(3)
        for k, q in ((3, three), (1, one), (2, two))
    ]
    for copy in shares:
        copy.start()
    start(1)
    mine.wait()
    stores = [
        pltpu.make_async_copy(held.at[i], units[i].at[p], local.at[4 + i]) for i in range(3)
    ]
    for store in stores:
        store.start()
    keep[0].wait()

    def arrived(i):
        def step(s, carry):
            row(i, s).wait_recv()
            return carry

        lax.fori_loop(1, count, step, 0)

    arrived(0)
    pass_on = to(tokens.at[:, :, cols], tokens.at[:, :, cols], ends.at[0, 0, 0], ends.at[1, 0, 0], twin)
    pass_on.start()
    arrived(2)
    for copy in shares:
        copy.wait_recv()
    arrived(1)
    pass_on.wait_recv()

    def leave(s, carry):
        for i in range(3):
            row(i, s).wait_send()
        return carry

    lax.fori_loop(1, count, leave, 0)
    for copy in [*shares, pass_on]:
        copy.wait_send()
    for copy in [*keep[1:], *stores]:
        copy.wait()


def deal(sent, pieces, gains, ident):
    count, per, both = sent.shape
    _, three, rows, units = pieces.shape
    return pl.pallas_call(
        deal_kernel,
        out_shape=[
            jax.ShapeDtypeStruct((count, per, both), BF),
            jax.ShapeDtypeStruct((count, per, both // 2), BF),
            jax.ShapeDtypeStruct((2, GROUP, rows, units), BF),
            jax.ShapeDtypeStruct((GROUP, rows, units), BF),
            jax.ShapeDtypeStruct((count, *gains.shape), F32),
        ],
        in_specs=[WHOLE, ANY, WHOLE],
        out_specs=[ANY] * 5,
        scratch_shapes=[
            pltpu.VMEM((three, rows, units), BF),
            pltpu.SemaphoreType.DMA((3, count)),
            pltpu.SemaphoreType.DMA((3, count)),
            pltpu.SemaphoreType.DMA((2, 4, 3)),
            pltpu.SemaphoreType.DMA((7,)),
        ],
        compiler_params=pltpu.CompilerParams(collective_id=ident, has_side_effects=True),
        name="deal",
    )(sent, pieces, gains)


STRIP = 16


def attend_back_kernel(
    dh2_half, middle, cot, w_out, w_qkv, mixed, q_rot, k_rot, value, prob, tokens, half_result, sum_0, sum_d,
    scale1, scale2, gain_a, gain_f, cosine, sine, into,
    new_qkv, new_out, new_gain, back, ffn, down,
    dh2, mid, low_mid, xs, hidden, w_part, g, mix, d_mix, qs, ks, vs, pb, gq, got_part,
    from_x, from_y, diag_x, diag_y, own, line, slots, half_rows, gain_terms, gain_got,
    send, recv, loads, row_send, row_recv, ends, keeps, unit_send, unit_recv,
):
    z, p, core, one, two, three = places()
    chunks, depth, _, each, _ = g.shape
    rows, width = mid.shape
    wide = width // 2
    query_cols, key_cols = qs.shape[1], ks.shape[1]
    outs = query_cols // WIDTH
    count, per, _ = slots.shape
    me = z * GROUP + p
    half = depth // 2
    low, high = pl.ds(0, half), pl.ds(half, half)
    x, y, twin = (z, one, core), (z, two, core), (z, p, 1 - core)
    column = [(lax.rem(z + s, depth), p, core) for s in range(1, depth)]
    columns = pl.ds(pl.multiple_of(core * wide, wide), wide)
    root = HEAD_SIZE ** (-0.5)
    pending = {}

    def load(name, i, src, dst):
        pending[name] = pltpu.make_async_copy(src, dst, loads.at[i])
        pending[name].start()

    load("half", 0, half_result, half_rows)
    load("dh2", 1, dh2_half, dh2.at[:, columns])
    load("mid", 2, middle, mid)
    load("cot", 3, cot.at[pl.ds(0, rows)], low_mid)
    load("x", 4, tokens, xs)
    load("mix", 5, mixed, mix)
    for i in range(outs):
        load(("out", i), 6 + i, w_out.at[:, :, :, pl.ds(i * WIDTH, WIDTH)], g.at[chunks - outs + i])
    at = 6 + outs
    load("q", at, q_rot, qs)
    load("k", at + 1, k_rot, ks)
    load("v", at + 2, value, vs)
    load(("p", 0), at + 3, prob.at[0], pb.at[0])
    load(("p", 1), at + 4, prob.at[1], pb.at[1])
    block = w_part.shape[1]

    def load_part(i):
        load(("w", i), at + 5 + i % 2, w_qkv.at[pl.ds(i * block, block)], w_part.at[i % 2])

    load_part(0)
    load_part(1)

    def partner(s):
        t = lax.rem(me + s, count)
        return t, (t // GROUP, lax.rem(t, GROUP), core)

    barrier = pltpu.get_barrier_semaphore()

    def greet(s, carry):
        pl.semaphore_signal(barrier, inc=1, device_id=partner(s)[1], device_id_type=MESH)
        return carry

    lax.fori_loop(1, count, greet, 0)
    pl.semaphore_signal(barrier, inc=1, device_id=twin, device_id_type=MESH)
    pl.semaphore_wait(barrier, count)
    copies = {}

    def go(name, c, i, src, dst, who):
        copies[name, c] = to(src, dst, send.at[c, i], recv.at[c, i], who)
        copies[name, c].start()

    def row(i, s):
        t, who = partner(s)
        if i < 2:
            return to(slots.at[t], back.at[i, me, :, columns], row_send.at[i, s], row_recv.at[i, s], who)
        return to(gain_terms.at[t], gain_got.at[me], row_send.at[2, s], row_recv.at[2, s], who)

    def each_row(kinds, act):
        def step(s, carry):
            for i in kinds:
                act(row(i, s))
            return carry

        lax.fori_loop(1, count, step, 0)

    kept = []

    def give_rows(i):
        slots[...] = mat_tn(into[...], half_rows[...]).reshape(count, per, wide).astype(BF)
        kept.append(pltpu.make_async_copy(slots.at[me], back.at[i, me, :, columns], keeps.at[i]))
        kept[-1].start()
        each_row((i,), lambda copy: copy.start())

    def first(c):
        go("3a", c, 0, g.at[c, low, three], diag_y.at[c], y)
        go("3b", c, 1, g.at[c, high, three], diag_x.at[c], x)
        go("1b", c, 2, g.at[c, high, one], from_x.at[c, high], x)
        go("2a", c, 3, g.at[c, low, two], from_y.at[c, low], y)

    def relay(c):
        copies["3a", c].wait_recv()
        for j in range(half):
            diag_y[c, j] = (g[c, j, one].astype(F32) + diag_y[c, j].astype(F32)).astype(BF)
        go("1a", c, 4, diag_y.at[c], from_x.at[c, low], x)
        copies["3b", c].wait_recv()
        for j in range(half):
            diag_x[c, j] = (g[c, half + j, two].astype(F32) + diag_x[c, j].astype(F32)).astype(BF)
        go("2b", c, 5, diag_x.at[c], from_y.at[c, high], y)

    def along(c):
        for name in ("1a", "1b", "2a", "2b"):
            copies[name, c].wait_recv()
        own[c] = g[c, z, p].astype(F32) + from_x[c, z].astype(F32) + from_y[c, z].astype(F32)
        for j in range(depth):
            from_x[c, j] = (
                g[c, j, p].astype(F32) + from_x[c, j].astype(F32) + from_y[c, j].astype(F32)
            ).astype(BF)
        for s, who in enumerate(column, 1):
            go(s, c, 5 + s, from_x.at[c, who[0]], line.at[c, s - 1], who)

    def terms(c, left, right):
        span = GROUP * each
        for j in range(depth):
            part = mat_tn(left[:, j * span : (j + 1) * span], right)
            g[c, j] = part.reshape(GROUP, each, WIDTH).astype(BF)
        first(c)

    units = sum_d.shape[1]
    span = units // 2

    def unit_parts(q, of):
        at = pl.multiple_of(of * units, units)
        rows_0 = unit_rows(sum_0, q, each)
        return [
            (unit_rows(sum_d, q, each), down.at[:, pl.ds(at, units)]),
            (rows_0.at[:, pl.ds(0, span)], ffn.at[0, :, pl.ds(at, span)]),
            (rows_0.at[:, pl.ds(span, span)], ffn.at[1, :, pl.ds(at, span)]),
        ]

    shared = []

    def collect():
        for i in range(3):
            for k, q in ((3, three), (1, one), (2, two)):
                src, dst = unit_parts(q, p)[i]
                copy = to(src, dst, unit_send.at[k, i], unit_recv.at[k, i], (z, q, core))
                copy.start()
                shared.append(copy)

    stay = []
    for i, (src, dst) in enumerate(unit_parts(p, p)):
        held = gq.at[pl.ds(0, each), pl.ds(i * span + (span if i else 0), units if i == 0 else span)]
        copy = pltpu.make_async_copy(src, held, keeps.at[3 + i])
        copy.start()
        stay.append((copy, pltpu.make_async_copy(held, dst, keeps.at[6 + i])))
    pending["dh2"].wait()
    swap = to(dh2.at[:, columns], dh2.at[:, columns], ends.at[0, 0], ends.at[1, 0], twin)
    swap.start()
    pending["half"].wait()
    give_rows(0)
    collect()
    for first_copy, second_copy in stay:
        first_copy.wait()
        second_copy.start()
    for name in ("mid", "cot", "x"):
        pending[name].wait()
    swap.wait_recv()

    def norm_2(i, total):
        strip = pl.ds(pl.multiple_of(i * STRIP, STRIP), STRIP)
        r2 = scale2[strip, :]
        n2 = mid[strip, :] * r2
        d = dh2[strip, :]
        s = d * gain_f[...]
        mean = jnp.sum(s * n2, axis=1, keepdims=True) * (1.0 / width)
        dm = low_mid[strip, :].astype(F32) + r2 * (s - n2 * mean)
        mid[strip, :] = dm
        low_mid[strip, :] = dm.astype(BF)
        hidden[strip, :] = (xs[strip, :].astype(F32) * scale1[strip, :] * gain_a[...]).astype(BF)
        return total + jnp.sum(d * n2, axis=0, keepdims=True)

    grad_gf = lax.fori_loop(0, rows // STRIP, norm_2, jnp.zeros((1, width), F32))
    pending["mix"].wait()
    for i in range(outs):
        pending["out", i].wait()
        d_mix[:, i * WIDTH : (i + 1) * WIDTH] = mat_nn(
            low_mid[...], g[chunks - outs + i].reshape(width, WIDTH)
        ).astype(BF)
    for i in range(outs):
        terms(i, low_mid, mix[:, i * WIDTH : (i + 1) * WIDTH])
    swap.wait_send()

    def turned_back(grad):
        a, b = grad[:, : HEAD_SIZE // 2], grad[:, HEAD_SIZE // 2 :]
        c, s = cosine[...], sine[...]
        return jnp.concatenate([a * c + b * s, b * c - a * s], axis=1).astype(BF)

    for name in ("q", "k", "v"):
        pending[name].wait()
    for _, copy in stay:
        copy.wait()
    heads, kv_heads = query_cols // HEAD_SIZE, key_cols // HEAD_SIZE
    each_kv = heads // kv_heads
    for h in range(kv_heads):
        kk, vv = ks[:, h * HEAD_SIZE : (h + 1) * HEAD_SIZE], vs[:, h * HEAD_SIZE : (h + 1) * HEAD_SIZE]
        dk = dv = None
        for j in range(h * each_kv, (h + 1) * each_kv):
            cols = slice(j * HEAD_SIZE, (j + 1) * HEAD_SIZE)
            pending["p", j].wait()
            pr = pb[j % 2]
            do = d_mix[:, cols]
            dp = mat_nt(do, vv)
            delta = jnp.sum(pr * dp, axis=1, keepdims=True)
            ds = (pr * (dp - delta)).astype(BF)
            gq[:, cols] = turned_back(mat_nn(ds, kk) * root)
            more_k, more_v = mat_tn(ds, qs[:, cols]), mat_tn(pr.astype(BF), do)
            dk, dv = (more_k, more_v) if dk is None else (dk + more_k, dv + more_v)
            if j + 2 < heads:
                load(("p", j + 2), at + 3 + j % 2, prob.at[j + 2], pb.at[j % 2])
        base = query_cols + h * HEAD_SIZE
        gq[:, base : base + HEAD_SIZE] = turned_back(dk * root)
        base += key_cols
        gq[:, base : base + HEAD_SIZE] = dv.astype(BF)
        done = (h + 1) * each_kv * HEAD_SIZE // WIDTH
        for i in range(h * each_kv * HEAD_SIZE // WIDTH, done):
            terms(outs + i, hidden, gq[:, i * WIDTH : (i + 1) * WIDTH])
        if h < outs:
            relay(h)
    for i in range(kv_heads, outs):
        relay(i)
    for i in range(done, gq.shape[1] // WIDTH):
        terms(outs + i, hidden, gq[:, i * WIDTH : (i + 1) * WIDTH])
    for i in range(width // block):
        pending["w", i].wait()
        part = mat_nt(gq[...], w_part[i % 2])
        dh2[:, i * block : (i + 1) * block] = part
        low_mid[:, i * block : (i + 1) * block] = part.astype(BF)
        if i + 2 < width // block:
            load_part(i + 2)
    pass_part = to(low_mid, got_part, ends.at[0, 1], ends.at[1, 1], twin)
    pass_part.start()
    for c in range(outs):
        along(c)
    relay(outs)
    each_row((0,), lambda copy: copy.wait_send())
    kept[0].wait()
    pass_part.wait_recv()

    def norm_1(i, total):
        strip = pl.ds(pl.multiple_of(i * STRIP, STRIP), STRIP)
        r1 = scale1[strip, :]
        n1 = xs[strip, :].astype(F32) * r1
        d = dh2[strip, :] + got_part[strip, :].astype(F32)
        s = d * gain_a[...]
        mean = jnp.sum(s * n1, axis=1, keepdims=True) * (1.0 / width)
        dx = mid[strip, :] + r1 * (s - n1 * mean)
        half_rows[strip, :] = jnp.where(core == 0, dx[:, :wide], dx[:, wide:]).astype(BF)
        return total + jnp.sum(d * n1, axis=0, keepdims=True)

    grad_ga = lax.fori_loop(0, rows // STRIP, norm_1, jnp.zeros((1, width), F32))
    give_rows(1)
    for t in range(count):
        gain_terms[t, 0:1, :] = grad_ga[:, t * each : (t + 1) * each]
        gain_terms[t, 1:2, :] = grad_gf[:, t * each : (t + 1) * each]
        gain_terms[t, 2:8, :] = jnp.zeros((6, each), F32)
    kept.append(pltpu.make_async_copy(gain_terms.at[me], gain_got.at[me], keeps.at[2]))
    kept[-1].start()
    each_row((2,), lambda copy: copy.start())
    for c in range(outs + 1, chunks):
        relay(c)
        along(c - 1)
    for copy in kept[1:]:
        copy.wait()
    each_row((0, 1, 2), lambda copy: copy.wait_recv())
    pass_on = to(
        back.at[:, :, :, columns], back.at[:, :, :, columns], ends.at[0, 2], ends.at[1, 2], twin
    )
    pass_on.start()
    along(chunks - 1)
    gain = gain_got[0]
    for t in range(1, count):
        gain = gain + gain_got[t]
    new_gain[...] = gain
    for c in range(chunks):
        total = own[c]
        for s in range(1, depth):
            copies[s, c].wait_recv()
            total = total + line[c, s - 1].astype(F32)
        if c < outs:
            new_out[:, c * WIDTH : (c + 1) * WIDTH] = total
        else:
            new_qkv[:, (c - outs) * WIDTH : (c - outs + 1) * WIDTH] = total
    pass_on.wait_recv()
    for copy in shared:
        copy.wait_recv()
    for copy in [*copies.values(), *shared]:
        copy.wait_send()
    each_row((1, 2), lambda copy: copy.wait_send())
    pass_part.wait_send()
    pass_on.wait_send()


def attend_back(
    dh2_half, middle, cot, w_out, w_qkv, mixed, q_rot, k_rot, value, prob, tokens, half_result, sum_0, sum_d,
    scale1, scale2, gain_a, gain_f, cosine, sine, into, ident,
):
    depth = lax.axis_size("line")
    count = depth * GROUP
    rows, width = middle.shape
    wide = width // 2
    each = width // count
    query_cols, key_cols = q_rot.shape[1], k_rot.shape[1]
    cols = query_cols + 2 * key_cols
    chunks = (query_cols + cols) // WIDTH
    block = min(512, width)
    units = sum_d.shape[1]

    def vmem(*shape, dtype=BF):
        return pltpu.VMEM(shape, dtype)

    return pl.pallas_call(
        attend_back_kernel,
        out_shape=[
            jax.ShapeDtypeStruct((each, cols), F32),
            jax.ShapeDtypeStruct((each, query_cols), F32),
            jax.ShapeDtypeStruct((8, each), F32),
            jax.ShapeDtypeStruct((2, count, rows // count, width), BF),
            jax.ShapeDtypeStruct((2, each, GROUP * units), BF),
            jax.ShapeDtypeStruct((each, GROUP * units), BF),
        ],
        in_specs=[ANY] * 14 + [WHOLE] * 7,
        out_specs=[WHOLE] * 3 + [ANY] * 3,
        scratch_shapes=[
            vmem(rows, width, dtype=F32),
            vmem(rows, width, dtype=F32),
            vmem(rows, width),
            vmem(rows, width),
            vmem(rows, width),
            vmem(2, block, cols),
            vmem(chunks, depth, GROUP, each, WIDTH),
            vmem(rows, query_cols),
            vmem(rows, query_cols),
            vmem(rows, query_cols),
            vmem(rows, key_cols),
            vmem(rows, key_cols),
            vmem(2, rows, rows, dtype=F32),
            vmem(rows, cols),
            vmem(rows, width),
            vmem(chunks, depth, each, WIDTH),
            vmem(chunks, depth, each, WIDTH),
            vmem(chunks, depth // 2, each, WIDTH),
            vmem(chunks, depth // 2, each, WIDTH),
            vmem(chunks, each, WIDTH, dtype=F32),
            vmem(chunks, depth - 1, each, WIDTH),
            vmem(count, rows // count, wide),
            vmem(rows, wide),
            vmem(count, 8, each, dtype=F32),
            vmem(count, 8, each, dtype=F32),
            pltpu.SemaphoreType.DMA((chunks, 5 + depth)),
            pltpu.SemaphoreType.DMA((chunks, 5 + depth)),
            pltpu.SemaphoreType.DMA((16,)),
            pltpu.SemaphoreType.DMA((3, count)),
            pltpu.SemaphoreType.DMA((3, count)),
            pltpu.SemaphoreType.DMA((2, 3)),
            pltpu.SemaphoreType.DMA((9,)),
            pltpu.SemaphoreType.DMA((4, 3)),
            pltpu.SemaphoreType.DMA((4, 3)),
        ],
        compiler_params=pltpu.CompilerParams(
            collective_id=ident, has_side_effects=True, vmem_limit_bytes=62 << 20
        ),
        name="attend_back",
    )(
        dh2_half, middle, cot, w_out, w_qkv, mixed, q_rot, k_rot, value,
        prob, tokens, half_result, sum_0, sum_d, scale1, scale2, gain_a, gain_f, cosine, sine, into,
    )


def unit_rows(ref, q, each):
    return ref.at[pl.ds(pl.multiple_of(q * each, each), each)]


def settle_kernel(
    sum_1, ffn, down, grad_qkv, grad_out, grad_gain, norm, new_ffn, new_down, new_out,
    rest, held, shares, local, unit_send, unit_recv, all_send, all_recv,
):
    z, p, core, one, two, three = places()
    count = shares.shape[0] // 2
    me = z * GROUP + p
    each, units = rest.shape[2], sum_1.shape[1]
    span = units // 2

    def anyone(s):
        t = lax.rem(me * 2 + core + s, 2 * count)
        return (t // (2 * GROUP), lax.rem(t // 2, GROUP), lax.rem(t, 2))

    barrier = pltpu.get_barrier_semaphore()

    def greet(s, carry):
        pl.semaphore_signal(barrier, inc=1, device_id=anyone(s), device_id_type=MESH)
        return carry

    lax.fori_loop(1, 2 * count, greet, 0)

    def unit_parts(q, of):
        rows = unit_rows(sum_1, q, each)
        return [(rows.at[:, pl.ds(i * span, span)], rest.at[i, of]) for i in range(2)]

    stay = [
        pltpu.make_async_copy(src, dst, local.at[i])
        for i, (src, dst) in enumerate(unit_parts(p, p))
    ] + [
        pltpu.make_async_copy(ffn, held.at[pl.ds(0, 2)], local.at[2]),
        pltpu.make_async_copy(down, held.at[2], local.at[3]),
    ]
    for copy in stay:
        copy.start()
    pl.semaphore_wait(barrier, 2 * count - 1)
    shared = []
    for i in range(2):
        for k, q in ((3, three), (1, one), (2, two)):
            src, dst = unit_parts(q, p)[i]
            copy = to(src, dst, unit_send.at[k, i], unit_recv.at[k, i], (z, q, core))
            copy.start()
            shared.append(copy)

    def squares(value):
        return jnp.sum(jnp.sum(value * value, axis=0, keepdims=True), axis=1, keepdims=True)

    gain = grad_gain[...]
    total = 0.5 * squares(gain[:2])
    for at in range(0, grad_qkv.shape[1], WIDTH):
        total = total + squares(grad_qkv[:, at : at + WIDTH])
    for at in range(0, grad_out.shape[1], 128):
        value = grad_out[:, at : at + 128]
        total = total + squares(value)
        new_out[at : at + 128, :] = value.T
    for copy in stay:
        copy.wait()
    for at in range(0, new_down.shape[0], 128):
        value = held[2, :, at : at + 128].astype(F32)
        total = total + squares(value)
        new_down[at : at + 128, :] = value.T
    for i in range(2):
        for q in range(GROUP):
            total = total + squares(held[i, :, q * units : q * units + span].astype(F32))
    for copy in shared:
        copy.wait_recv()
    for i in range(2):
        for q in range(GROUP):
            value = rest[i, q]
            total = total + squares(value.astype(F32))
            held[i, :, q * units + span : (q + 1) * units] = value
    shares[0] = jnp.broadcast_to(total, (8, 128))

    def tell(s):
        return to(shares.at[0], shares.at[s], all_send.at[s], all_recv.at[s], anyone(s))

    def tell_start(s, carry):
        tell(s).start()
        return carry

    def tell_end(s, carry):
        tell(s).wait_recv()
        return carry

    def tell_left(s, carry):
        tell(s).wait_send()
        return carry

    lax.fori_loop(1, 2 * count, tell_start, 0)
    keep = pltpu.make_async_copy(held.at[pl.ds(0, 2)], new_ffn, local.at[4])
    keep.start()
    lax.fori_loop(1, 2 * count, tell_end, 0)
    norm[...] = jnp.sqrt(jnp.sum(shares[...], axis=0))
    lax.fori_loop(1, 2 * count, tell_left, 0)
    for copy in shared:
        copy.wait_send()
    keep.wait()


def settle(sum_1, ffn, down, grad_qkv, grad_out, grad_gain, ident):
    count = lax.axis_size("line") * GROUP
    each, units = grad_qkv.shape[0], sum_1.shape[1]
    return pl.pallas_call(
        settle_kernel,
        out_shape=[
            jax.ShapeDtypeStruct((8, 128), F32),
            jax.ShapeDtypeStruct((2, each, GROUP * units), BF),
            jax.ShapeDtypeStruct((GROUP * units, each), F32),
            jax.ShapeDtypeStruct(grad_out.shape[::-1], F32),
        ],
        in_specs=[ANY] * 3 + [WHOLE] * 3,
        out_specs=[WHOLE, ANY, WHOLE, WHOLE],
        scratch_shapes=[
            pltpu.VMEM((2, GROUP, each, units // 2), BF),
            pltpu.VMEM((3, each, GROUP * units), BF),
            pltpu.VMEM((2 * count, 8, 128), F32),
            pltpu.SemaphoreType.DMA((5,)),
            pltpu.SemaphoreType.DMA((4, 2)),
            pltpu.SemaphoreType.DMA((4, 2)),
            pltpu.SemaphoreType.DMA((2 * count,)),
            pltpu.SemaphoreType.DMA((2 * count,)),
        ],
        compiler_params=pltpu.CompilerParams(
            collective_id=ident, has_side_effects=True, vmem_limit_bytes=24 << 20
        ),
        name="settle",
    )(sum_1, ffn, down, grad_qkv, grad_out, grad_gain)


def update_kernel(limit, norm, gain, moves, qkv, ffn, down, out, back, *refs):
    weights, moments, placed = refs[:9], refs[9:18], refs[18:20]
    new_moments, new_weights = refs[20:29], refs[29:38]
    w_buf, m_buf = refs[38:47], refs[47:56]
    qkv_buf, ffn_buf, down_buf, out_buf, rows_buf, loads, stores, grads = refs[56:]
    sources = {
        6: pltpu.make_async_copy(ffn, ffn_buf, grads.at[0]),
        8: pltpu.make_async_copy(down, down_buf, grads.at[1]),
        1: pltpu.make_async_copy(qkv, qkv_buf, grads.at[2]),
        4: pltpu.make_async_copy(out, out_buf, grads.at[3]),
    }
    order = (0, 5, 2, 3, 1, 4, 8, 6, 7)
    pending = {}
    returned = [
        pltpu.make_async_copy(back.at[i], rows_buf.at[i], grads.at[4 + i]) for i in range(2)
    ]
    for copy in returned:
        copy.start()
    for i in order:
        if i in sources and i != 1:
            sources[i].start()
        if i == 2:
            sources[1].start()
        pending[i] = [
            pltpu.make_async_copy(weights[i], w_buf[i], loads.at[0, i]),
            pltpu.make_async_copy(moments[i], m_buf[i], loads.at[1, i]),
        ]
        for copy in pending[i]:
            copy.start()
    factor = 0.5 * jnp.minimum(1.0, limit / norm[:1, :1])
    writes = []
    everything = slice(None)
    base = qkv_buf.shape[1] // 2

    def update(i, at, grad):
        m = 0.5 * m_buf[i][at] + factor * grad
        w = w_buf[i][at]
        m_buf[i][at] = m
        w_buf[i][at] = w - LEARN * (m + DECAY * w)

    placing = []
    for i in range(2):
        returned[i].wait()
        rows_buf[i] = mat_tn(moves[...], rows_buf[i]).astype(BF)
        placing.append(pltpu.make_async_copy(rows_buf.at[i], placed[i], grads.at[6 + i]))
        placing[i].start()
    for i in order:
        if i in sources and i != 1:
            sources[i].wait()
        if i == 2:
            sources[1].wait()
        for copy in pending[i]:
            copy.wait()
        if i in (0, 5):
            update(i, (everything, everything), gain[i // 5 : i // 5 + 1, :])
        elif i in (1, 2, 3):
            shift = 0 if i == 1 else base + (i - 2) * w_buf[2].shape[1]
            for at in range(0, w_buf[i].shape[1], WIDTH):
                update(i, (everything, slice(at, at + WIDTH)), qkv_buf[:, shift + at : shift + at + WIDTH])
        elif i in (6, 7):
            for at in range(0, w_buf[i].shape[1], WIDTH):
                cols = (everything, slice(at, at + WIDTH))
                update(i, cols, ffn_buf[(i - 6, *cols)].astype(F32))
        else:
            source = down_buf if i == 8 else out_buf
            for at in range(0, w_buf[i].shape[0], WIDTH):
                rows = (slice(at, at + WIDTH), everything)
                update(i, rows, source[rows])
        for buf, new, j in ((m_buf, new_moments, 0), (w_buf, new_weights, 1)):
            writes.append(pltpu.make_async_copy(buf[i], new[i], stores.at[j, i]))
            writes[-1].start()
    for copy in [*placing, *writes]:
        copy.wait()


def update(norm, gain, moves, qkv, ffn, down, out, back, weights, moments, limit):
    like = [jax.ShapeDtypeStruct(v.shape, F32) for v in weights]
    size = sum(v.size for v in weights)
    return pl.pallas_call(
        functools.partial(update_kernel, limit),
        out_shape=[*[jax.ShapeDtypeStruct(back.shape[1:], BF)] * 2, *like, *like],
        in_specs=[WHOLE] * 3 + [ANY] * 23,
        out_specs=[ANY] * 20,
        scratch_shapes=[pltpu.VMEM(v.shape, F32) for v in (*weights, *moments)]
        + [pltpu.VMEM(v.shape, v.dtype) for v in (qkv, ffn, down, out, back)]
        + [
            pltpu.SemaphoreType.DMA((2, 9)),
            pltpu.SemaphoreType.DMA((2, 9)),
            pltpu.SemaphoreType.DMA((8,)),
        ],
        compiler_params=pltpu.CompilerParams(vmem_limit_bytes=44 << 20),
        cost_estimate=pl.CostEstimate(flops=7 * size, bytes_accessed=20 * size, transcendentals=0),
        name="update",
    )(norm, gain, moves, qkv, ffn, down, out, back, *weights, *moments)


class Sharing:
    def __init__(self, out, rows, send, recv):
        self.z, self.p, self.core, self.one, self.two, _ = places()
        self.out, self.rows, self.half = out, rows, rows // 2
        wide = out.shape[1] // 2
        self.cols = pl.ds(pl.multiple_of(self.core * wide, wide), wide)
        self.send, self.recv, self.copies = send, recv, {}
        self.x, self.y = (self.z, self.one, self.core), (self.z, self.two, self.core)
        self.twin = (self.z, self.p, 1 - self.core)

    def part(self, k, b):
        return self.out.at[pl.ds(k * self.rows + b * self.half, self.half), self.cols]

    def go(self, name, i, src, dst, partner):
        self.copies[name] = to(src, dst, self.send.at[i], self.recv.at[i], partner)
        self.copies[name].start()

    def start(self, source):
        self.go("1a", 0, source(0), self.part(1, 0), self.x)
        self.go("2b", 3, source(1), self.part(2, 1), self.y)
        self.go("1b", 1, source(1), self.part(1, 1), self.x)
        self.go("2a", 2, source(0), self.part(2, 0), self.y)

    def own(self, source):
        for b in range(2):
            self.go("o%d" % b, 12 + b, source(b), self.part(0, b), self.twin)

    def pass_on(self, name, i, k, b):
        self.copies[name].wait_recv()
        self.go("t" + name, i, self.part(k, b), self.part(k, b), self.twin)

    def relay(self):
        self.copies["1a"].wait_recv()
        self.go("3a", 4, self.part(1, 0), self.part(3, 0), self.y)
        self.go("t1a", 6, self.part(1, 0), self.part(1, 0), self.twin)
        self.copies["2b"].wait_recv()
        self.go("3b", 5, self.part(2, 1), self.part(3, 1), self.x)
        self.go("t2b", 9, self.part(2, 1), self.part(2, 1), self.twin)

    def end(self):
        self.pass_on("1b", 7, 1, 1)
        self.pass_on("2a", 8, 2, 0)
        self.pass_on("3a", 10, 3, 0)
        self.pass_on("3b", 11, 3, 1)
        for name, copy in self.copies.items():
            if name[0] in "to":
                copy.wait_recv()
        for copy in self.copies.values():
            copy.wait_send()


def attend_kernel(
    line, w_qkv, tokens, cot, gain_a, gain_f, cosine, sine, segment, segment_row,
    w_out, group_h2, group_cot, middle, q_rot, k_rot, value, mixed, prob, scale1, scale2,
    xs, hidden, w_part, held, wo, mid, packed, got, pb, qs, ks, vs, mix,
    sends, recvs, out_send, out_recv, ends, loads, stores,
):
    z, p, core, one, two, _ = places()
    rows, width = xs.shape
    wide = width // 2
    depth, each, _ = line.shape
    query_cols, key_cols = qs.shape[1], ks.shape[1]
    half = depth // 2
    low, high = pl.ds(0, half), pl.ds(half, half)
    x, y, twin = (z, one, core), (z, two, core), (z, p, 1 - core)
    root = HEAD_SIZE ** (-0.5)
    pending = {}
    out_cols = pl.ds(query_cols + 2 * key_cols, query_cols)

    def load(name, i, src, dst):
        pending[name] = pltpu.make_async_copy(src, dst, loads.at[i])
        pending[name].start()

    load("x", 0, tokens, xs)
    order = [query_cols // WIDTH + i for i in range(2 * key_cols // WIDTH)]
    order += list(range(query_cols // WIDTH))

    def load_part(i):
        load(("w", i), 1 + i % 2, w_qkv.at[:, pl.ds(order[i] * WIDTH, WIDTH)], w_part.at[i % 2])

    load_part(0)
    load_part(1)
    load("held", 3, line.at[:, :, out_cols], held)
    meet([x, y, twin])
    outs = []

    def go(src, dst, partner):
        i = len(outs)
        outs.append(to(src, dst, out_send.at[i], out_recv.at[i], partner))
        outs[i].start()

    go(line.at[low, :, out_cols], w_out.at[low, p], x)
    go(line.at[high, :, out_cols], w_out.at[high, p], y)
    go(line.at[high, :, out_cols], w_out.at[high, p], x)
    go(line.at[low, :, out_cols], w_out.at[low, p], y)
    cots = Sharing(group_cot, rows, sends.at[0], recvs.at[0])
    shares = Sharing(group_h2, rows, sends.at[1], recvs.at[1])
    halves = [pl.ds(0, rows // 2), pl.ds(rows // 2, rows // 2)]
    cots.own(lambda b: cot.at[halves[b]])
    kept = []

    def keep(src, dst):
        kept.append(pltpu.make_async_copy(src, dst, stores.at[len(kept)]))
        kept[-1].start()

    keep(cot, group_cot.at[pl.ds(0, rows), cots.cols])
    pending["x"].wait()

    def norm_1(i, carry):
        strip = pl.ds(pl.multiple_of(i * STRIP, STRIP), STRIP)
        v = xs[strip, :].astype(F32)
        r = lax.rsqrt(jnp.sum(v * v, axis=1, keepdims=True) * (1.0 / width) + EPS)
        scale1[strip, :] = r
        hidden[strip, :] = (v * r * gain_a[...]).astype(BF)
        return carry

    lax.fori_loop(0, rows // STRIP, norm_1, 0)

    def turned(v):
        a, b = v[:, : HEAD_SIZE // 2], v[:, HEAD_SIZE // 2 :]
        c, s = cosine[...], sine[...]
        return jnp.concatenate([a * c - b * s, b * c + a * s], axis=1).astype(BF)

    def project(i):
        pending["w", i].wait()
        v = mat_nn(hidden[...], w_part[i % 2])
        at = order[i] * WIDTH
        if at >= query_cols + key_cols:
            at -= query_cols + key_cols
            vs[:, at : at + WIDTH] = v.astype(BF)
        else:
            ref, at = (qs, at) if at < query_cols else (ks, at - query_cols)
            for j in range(0, WIDTH, HEAD_SIZE):
                ref[:, at + j : at + j + HEAD_SIZE] = turned(v[:, j : j + HEAD_SIZE])
        if i + 2 < len(order):
            load_part(i + 2)

    for i in range(2 * key_cols // WIDTH):
        project(i)
    pending["held"].wait()
    keep(held, w_out.at[:, p])
    index = lax.broadcasted_iota(jnp.int32, (rows, rows), 0)
    seen = (segment[...] == segment_row[...]) & (
        lax.broadcasted_iota(jnp.int32, (rows, rows), 1) <= index
    )
    heads, kv_heads = query_cols // HEAD_SIZE, key_cols // HEAD_SIZE
    puts = []

    def attend_head(j):
        h = j // (heads // kv_heads)
        kv = slice(h * HEAD_SIZE, (h + 1) * HEAD_SIZE)
        cols = slice(j * HEAD_SIZE, (j + 1) * HEAD_SIZE)
        s = mat_nt(qs[:, cols], ks[:, kv]) * root
        s = jnp.where(seen, s, -1e30)
        e = jnp.exp(s - jnp.max(s, axis=1, keepdims=True))
        pr = e / jnp.sum(e, axis=1, keepdims=True)
        if j >= 2:
            puts[j - 2].wait()
        pb[j % 2] = pr
        puts.append(pltpu.make_async_copy(pb.at[j % 2], prob.at[j], stores.at[8 + j]))
        puts[j].start()
        mix[:, cols] = mat_nn(pr.astype(BF), vs[:, kv]).astype(BF)

    relayed = False
    for i in range(2 * key_cols // WIDTH, len(order)):
        project(i)
        if not relayed:
            relayed = True
            outs[0].wait_recv()
            go(w_out.at[low, one], w_out.at[low, one], y)
            outs[1].wait_recv()
            go(w_out.at[high, two], w_out.at[high, two], x)
        for j in range(order[i] * WIDTH // HEAD_SIZE, (order[i] + 1) * WIDTH // HEAD_SIZE):
            attend_head(j)
    keep(ks, k_rot)
    keep(vs, value)
    keep(qs, q_rot)
    keep(mix, mixed)
    for i in range(2, 6):
        outs[i].wait_recv()
    cots.start(lambda b: cot.at[halves[b]])
    kept[1].wait()
    load("wo", 4, w_out, wo)
    pending["wo"].wait()
    span = GROUP * each
    for j in range(depth):
        v = mat_nt(mix[...], wo[j].reshape(span, query_cols))
        mid[:, j * span : (j + 1) * span] = v
        packed[:, j * span : (j + 1) * span] = v.astype(BF)
    swap = to(packed, got, ends.at[0], ends.at[1], twin)
    swap.start()
    swap.wait_recv()
    swap.wait_send()

    def norm_2(i, carry):
        strip = pl.ds(pl.multiple_of(i * STRIP, STRIP), STRIP)
        v = xs[strip, :].astype(F32) + (mid[strip, :] + got[strip, :].astype(F32))
        mid[strip, :] = v
        r = lax.rsqrt(jnp.sum(v * v, axis=1, keepdims=True) * (1.0 / width) + EPS)
        scale2[strip, :] = r
        packed[strip, :] = (v * r * gain_f[...]).astype(BF)
        return carry

    lax.fori_loop(0, rows // STRIP, norm_2, 0)
    shares.start(lambda b: packed.at[halves[b], shares.cols])
    keep(packed, group_h2.at[pl.ds(0, rows)])
    keep(mid, middle)
    shares.relay()
    cots.relay()
    shares.end()
    cots.end()
    for copy in outs:
        copy.wait_send()
    for i, copy in enumerate(kept):
        if i != 1:
            copy.wait()
    for copy in puts[-2:]:
        copy.wait()


def attend(line, w_qkv, tokens, cot, gain_a, gain_f, cosine, sine, segment, key_cols, ident):
    depth = lax.axis_size("line")
    rows, width = tokens.shape
    each = line.shape[0] // depth
    cols = w_qkv.shape[1]
    query_cols = cols - 2 * key_cols
    heads = query_cols // HEAD_SIZE

    def vmem(*shape, dtype=BF):
        return pltpu.VMEM(shape, dtype)

    def like(*shape, dtype=BF):
        return jax.ShapeDtypeStruct(shape, dtype)

    return pl.pallas_call(
        attend_kernel,
        out_shape=[
            like(depth, GROUP, each, query_cols),
            like(GROUP * rows, width),
            like(GROUP * rows, width),
            like(rows, width, dtype=F32),
            like(rows, query_cols),
            like(rows, key_cols),
            like(rows, key_cols),
            like(rows, query_cols),
            like(heads, rows, rows, dtype=F32),
            like(rows, 1, dtype=F32),
            like(rows, 1, dtype=F32),
        ],
        in_specs=[ANY] * 3 + [WHOLE] * 7,
        out_specs=[ANY] * 9 + [WHOLE] * 2,
        scratch_shapes=[
            vmem(rows, width),
            vmem(rows, width),
            vmem(2, width, WIDTH),
            vmem(depth, each, query_cols),
            vmem(depth, GROUP, each, query_cols),
            vmem(rows, width, dtype=F32),
            vmem(rows, width),
            vmem(rows, width),
            vmem(2, rows, rows, dtype=F32),
            vmem(rows, query_cols),
            vmem(rows, key_cols),
            vmem(rows, key_cols),
            vmem(rows, query_cols),
            pltpu.SemaphoreType.DMA((2, 14)),
            pltpu.SemaphoreType.DMA((2, 14)),
            pltpu.SemaphoreType.DMA((6,)),
            pltpu.SemaphoreType.DMA((6,)),
            pltpu.SemaphoreType.DMA((2,)),
            pltpu.SemaphoreType.DMA((5,)),
            pltpu.SemaphoreType.DMA((8 + heads,)),
        ],
        compiler_params=pltpu.CompilerParams(
            collective_id=ident, has_side_effects=True, vmem_limit_bytes=56 << 20
        ),
        name="attend",
    )(
        line.reshape(depth, each, line.shape[1]), w_qkv, tokens, cot, gain_a, gain_f, cosine, sine,
        segment[:, None], segment[None, :],
    )


class Ways:
    def __init__(self):
        self.depth = lax.axis_size("line")
        self.n = self.depth * GROUP
        self.z = lax.axis_index("line")
        self.p = lax.axis_index("group")
        self.me = self.z * GROUP + self.p
        self.core = lax.axis_index("mp")

    def gather_line(self, value):
        return lax.all_gather(value, "line", axis=0, tiled=True)

    def scatter_line(self, whole):
        return lax.psum_scatter(whole, "line", scatter_dimension=0, tiled=True)

    def own_half(self, value):
        half = value.shape[-1] // 2
        return jnp.where(self.core == 0, value[..., :half], value[..., half:])


def unit_pieces(down, gate, upper):
    units = down.shape[1] // GROUP
    half = units // 2

    def cut(j, c):
        at = slice(j * units + c * half, j * units + (c + 1) * half)
        return jnp.concatenate([gate[:, at], upper[:, at]], axis=1)

    return jnp.stack(
        [
            jnp.stack([down[:, j * units : (j + 1) * units], cut(j, 0), cut(j, 1)])
            for j in range(GROUP)
        ]
    )


def deal_tables(token_order, me, rows):
    blocks = token_order.shape[0] // rows
    per = rows // blocks
    index = jnp.arange(rows, dtype=jnp.int32)
    wanted = lax.dynamic_slice_in_dim(token_order, me * rows, rows)
    source = wanted // rows
    same = (source[:, None] == source[None, :]) & (index[None, :] < index[:, None])
    slot = source * per + jnp.sum(same.astype(jnp.int32), axis=1)
    into = (slot[:, None] == index[None, :]).astype(BF)
    table = token_order.reshape(blocks, rows)
    taken = table // rows == me
    earlier = (index[:, None] < index[None, :]).astype(BF)
    rank = mat_nn(taken.astype(BF), earlier).astype(jnp.int32)
    hit = taken[:, None, :] & (rank[:, None, :] == jnp.arange(per, dtype=jnp.int32)[None, :, None])
    sent = jnp.sum(jnp.where(hit, (table - me * rows)[:, None, :], 0), axis=2).reshape(rows)
    out = (sent[:, None] == index[None, :]).astype(BF)
    return into, out


def on_device(
    tokens,
    cotangent,
    lengths,
    seq_deal,
    token_order,
    gain_attn,
    w_query,
    key_weight,
    value_weight,
    w_out,
    gain_ffn,
    w_gate,
    w_up,
    w_down,
    moment_gain_attn,
    moment_w_query,
    key_weight_momentum,
    value_weight_momentum,
    moment_w_out,
    moment_gain_ffn,
    moment_w_gate,
    moment_w_up,
    moment_w_down,
):
    ways = Ways()
    rows, width = tokens.shape
    me = ways.me
    shard_qkv = jnp.concatenate(
        [w_query.astype(BF), key_weight.astype(BF), value_weight.astype(BF)], axis=1
    )
    shard_out = w_out.astype(BF).T
    line = ways.gather_line(jnp.concatenate([shard_qkv, shard_out], axis=1))

    into, out = deal_tables(token_order, me, rows)
    sent = mat_nn(
        out, jnp.concatenate([ways.own_half(tokens), ways.own_half(cotangent)], axis=1)
    ).astype(BF)
    pieces = unit_pieces(w_down.astype(BF).T, w_gate.astype(BF), w_up.astype(BF))
    gains = jnp.pad(
        jnp.stack([gain_attn, gain_ffn]).astype(BF).astype(F32), ((0, 6), (0, 0))
    )
    got_tokens, got_cot, units_0, units_1, all_gains = deal(
        sent.reshape(ways.n, rows // ways.n, width), pieces, gains, 5
    )
    gain_a = all_gains[:, 0].reshape(width)
    gain_f = all_gains[:, 1].reshape(width)
    dealt = mat_nn(into, got_tokens.reshape(rows, width)).astype(BF)
    half_cot = mat_nn(into, got_cot.reshape(rows, width // 2)).astype(BF)

    wide_k = key_weight.shape[1]
    weight_qkv = share_weights(line, shard_qkv.shape[1], 4)

    units = units_1.shape[-1]
    first_units = lax.all_gather(
        units_0.reshape(2, -1, units), "line", axis=1, tiled=False
    ).reshape(2, width, units)
    down_t, first_w = first_units[0], first_units[1]
    second_w = ways.gather_line(units_1.reshape(-1, units))

    seq_dev = seq_deal.shape[0] // ways.n
    mine = lax.dynamic_slice_in_dim(seq_deal, me * seq_dev, seq_dev)
    position, segment = layout(lengths[mine], rows)
    cosine, sine = angles(position, HEAD_SIZE)
    gain_a, gain_f = gain_a.reshape(1, width), gain_f.reshape(1, width)
    (
        weight_out,
        group_h2,
        group_cot,
        middle,
        query_rot,
        key_rot,
        value,
        mixed,
        prob,
        scale1,
        scale2,
    ) = attend(line, weight_qkv, dealt, half_cot, gain_a, gain_f, cosine, sine, segment, wide_k, 8)

    grad_inner = mat_nn(group_cot, down_t)
    span = grad_inner.shape[1] // 2

    def units_half(group_rows, weight, grad_inner):
        both = mat_nn(group_rows, weight)
        gate, upper = both[:, :span], both[:, span:]
        sigma = jax.nn.sigmoid(gate)
        activ = gate * sigma
        inner = (activ * upper).astype(BF)
        slope = sigma * (1.0 + gate * (1.0 - sigma))
        grads = jnp.concatenate([grad_inner * upper * slope, grad_inner * activ], axis=1)
        return inner, grads.astype(BF)

    inner_0, grads_0 = units_half(group_h2, first_w, grad_inner[:, :span])
    terms_0 = mat_tn(group_h2, grads_0).astype(BF)
    sum_0 = ways.scatter_line(terms_0)
    inner_1, grads_1 = units_half(after(group_h2, terms_0), second_w, grad_inner[:, span:])
    inner = jnp.concatenate([inner_0, inner_1], axis=1)
    terms_d = mat_tn(group_cot, inner).astype(BF)
    sum_d = ways.scatter_line(terms_d)
    half_dh2, half_ffn = sum_rows(
        [[(grads_0, first_w), (after(grads_1, terms_d), second_w)], [(inner, down_t)]], 2
    )
    terms_1 = mat_tn(after(group_h2, half_dh2), grads_1).astype(BF)
    sum_1 = ways.scatter_line(terms_1)
    half_dh2 = after(half_dh2, terms_1)
    half_result = (ways.own_half(middle) + half_ffn).astype(BF)
    new_qkv, new_out, new_gain, back, ffn, down = attend_back(
        half_dh2,
        middle,
        group_cot,
        weight_out,
        weight_qkv,
        mixed,
        query_rot,
        key_rot,
        value,
        prob,
        dealt,
        half_result,
        sum_0,
        sum_d,
        scale1,
        scale2,
        gain_a,
        gain_f,
        cosine,
        sine,
        into,
        6,
    )
    norm, new_ffn, new_down, new_out_t = settle(sum_1, ffn, down, new_qkv, new_out, new_gain, 7)
    weights = (gain_attn, w_query, key_weight, value_weight, w_out, gain_ffn, w_gate, w_up, w_down)
    moments = (
        moment_gain_attn,
        moment_w_query,
        key_weight_momentum,
        value_weight_momentum,
        moment_w_out,
        moment_gain_ffn,
        moment_w_gate,
        moment_w_up,
        moment_w_down,
    )
    flat = [v if v.ndim == 2 else v.reshape(1, -1) for v in (*weights, *moments)]
    activations, input_grad, *new = update(
        norm,
        new_gain,
        out,
        new_qkv,
        new_ffn,
        new_down,
        new_out_t,
        back.reshape(2, rows, width),
        flat[:9],
        flat[9:],
        math.sqrt(PARAMS),
    )
    new = [v.reshape(old.shape) for v, old in zip(new, (*weights, *weights))]
    return (activations, input_grad, norm[0, 0], *new)


def solution(mesh):
    count, cores = mesh.devices.shape
    regrouped = Mesh(
        mesh.devices.reshape(count // GROUP, GROUP, cores), ("line", "group", "mp")
    )
    dp = ("line", "group")
    gain, tall, wide, row = P(dp), P(dp, "mp"), P("mp", dp), P(dp, None)
    leaves = (gain, tall, tall, tall, wide, gain, tall, tall, wide)
    return jax.shard_map(
        on_device,
        mesh=regrouped,
        in_specs=(row, row, P(), P(), P(), *leaves, *leaves),
        out_specs=(row, row, P(), *leaves, *leaves),
        check_vma=False,
    )
```
